32 devices in a mesh: img: 16 (over z, y, x), ref: 2 (over core).
Axes of the slice: x: 2, y: 2, z: 4, core: 2. Of those that a mesh axis runs over, the one named last changes fastest.
Arguments:
- images: bfloat16 [16384, 2048], P('img'), may hold values from -8 to 8
- references: bfloat16 [1024, 2048], P('ref'), may hold values from -1 to 1
- initial_contrast: float32 [16384], P('img'), may hold values from 0.25 to 1.75
Outputs:
- new_references: bfloat16 [1024, 2048], P('ref')
- contrast: float32 [16384], P('img')
- loglik: float32 [16384], P('img')
The draws below stay inside these ranges and needn't reach their ends.
All inputs are finite; a program needn't handle non-finite values.
Results may differ from the reference program's by a relative error of at most 0.0041.
Values may be sent and summed in bfloat16 or wider, within the bound.
A program may use at most 64 MiB of HBM per device.

```python
import math
import jax
import jax.numpy as jnp
from jax import lax

F = 2048
IMG_DEV = 1024
ITERS = 3
NIMG = 16384
NREF = 1024


def ref_table(key):
    subkey = jax.random.fold_in(key, 11)
    gaussian = jnp.clip(jax.random.normal(subkey, (NREF, F), jnp.float32), -4.0, 4.0)
    row_scale = 0.6 + 1.2 * jnp.arange(NREF, dtype=jnp.float32) / NREF
    return gaussian * row_scale[:, None] * F ** (-0.5)


def draw_references(key, part):
    return ref_table(key).astype(jnp.bfloat16)


def draw_images(key, part):
    subkey = jax.random.fold_in(key, 23)
    gaussian = jax.random.normal(subkey, (NIMG, F), jnp.float32)
    return jnp.clip(gaussian, -8.0, 8.0).astype(jnp.bfloat16)


def setup_inputs(seed: int = 0) -> dict:
    key_of = jax.random.split(jax.random.key(seed), 4)
    images = draw_images(jax.random.fold_in(key_of[3], 71), 0)
    references = draw_references(jax.random.fold_in(key_of[3], 71), 0)
    initial_contrast = jnp.clip(1.0 + 0.15 * jax.random.normal(key_of[2], (NIMG,), jnp.float32), 0.25, 1.75)
    return {"images": images, "references": references, "initial_contrast": initial_contrast}


sharpness = 2.0
prior_weight = 1.0
epsilon = 1e-06

def scores_of(cross_terms, ref_norms, contrast):
    contrast_col = contrast[:, None]
    return sharpness * (contrast_col * cross_terms - 0.5 * (contrast_col * contrast_col) * ref_norms[None, :])

def statistics(cross_terms, ref_norms, contrast):
    scored = scores_of(cross_terms, ref_norms, contrast)
    highest = lax.optimization_barrier(jnp.max(scored, axis=1))
    exponent = jnp.exp(scored - highest[:, None])
    summed = lax.optimization_barrier(jnp.sum(exponent, axis=1))
    weighted_cross = lax.optimization_barrier(jnp.sum(exponent * cross_terms, axis=1))
    weighted_norm = lax.optimization_barrier(jnp.sum(exponent * ref_norms[None, :], axis=1))
    return (highest, summed, weighted_cross, weighted_norm, exponent)

def normalize(sums):
    meansq = lax.optimization_barrier(jnp.mean(sums * sums, axis=1))
    return (sums * lax.rsqrt(meansq + epsilon)[:, None]).astype(jnp.bfloat16)

def reference(images, references, initial_contrast):
    ref_norms = lax.optimization_barrier(jnp.sum(jnp.square(references.astype(jnp.float32)), axis=1))
    image_blocks = images.reshape(NIMG // IMG_DEV, IMG_DEV, F)
    prior_blocks = initial_contrast.reshape(NIMG // IMG_DEV, IMG_DEV)

    def one_block(running, carried):
        image_block, prior = carried
        cross_terms = lax.dot_general(image_block, references, (((1,), (1,)), ((), ())), preferred_element_type=jnp.float32)
        contrast = prior
        for iteration in range(ITERS + 1):
            highest, summed, weighted_cross, weighted_norm, exponent = statistics(cross_terms, ref_norms, contrast)
            if iteration < ITERS:
                contrast = (weighted_cross / summed + prior_weight * prior) / (weighted_norm / summed + prior_weight)
        posterior = exponent / summed[:, None]
        weights = (posterior * contrast[:, None]).astype(jnp.bfloat16)
        running = running + lax.dot_general(weights, image_block, (((0,), (0,)), ((), ())), preferred_element_type=jnp.float32)
        return (running, contrast)
    sums, contrasts = lax.scan(one_block, jnp.zeros((NREF, F), jnp.float32), (image_blocks, prior_blocks))
    new_references = normalize(sums)
    new_norms = lax.optimization_barrier(jnp.sum(jnp.square(new_references.astype(jnp.float32)), axis=1)) / F

    def rescore(carried):
        image_block, contrast = carried
        new_cross = lax.dot_general(image_block, new_references, (((1,), (1,)), ((), ())), preferred_element_type=jnp.float32) * F ** (-0.5)
        highest, summed, weighted_cross, weighted_norm, exponent = statistics(new_cross, new_norms, contrast)
        return highest + jnp.log(summed) - math.log(NREF)
    loglik = lax.map(rescore, (image_blocks, contrasts))
    return (new_references, contrasts.reshape(NIMG), loglik.reshape(NIMG))
```

```python
import functools
import math

import jax
import jax.numpy as jnp
from jax import lax
from jax.experimental import pallas as pl
from jax.experimental.pallas import tpu as pltpu
from jax.sharding import PartitionSpec as P

ITERS = 3

sharpness = 2.0
prior_weight = 1.0
epsilon = 1e-06

MESH = pl.DeviceIdType.MESH
LANES = 256
BLOCK = 512
ROWS = 64
LOG2E = math.log2(math.e)
QUADS = ((1, 0), (1, 1), (0, 1), (0, 0))
F32 = jnp.float32
BF16 = jnp.bfloat16


def kernel(
    nz, n_ref, im_hbm, ref_hbm, prior_ref, newref_hbm, contrast_ref, loglik_ref,
    im, refs, norms, cross, w, snd1, rcv1, acc, snd2, rcv2, snd3, rcv3, gath,
    stat_snd, stat_rcv, vecs, keep, *rest,
):
    n, width = im.shape
    *split, im_sem, ref_sem, out_sem, ssem, rsem = rest
    paired = bool(split)
    mine = n // n_ref
    rows = refs.shape[0]
    rb = rows // (4 * nz)
    qr = nz * rb
    half = width // 2
    me = lax.axis_index("img")
    rme = lax.axis_index("ref")
    x, y, z = lax.rem(me, 2), lax.rem(me // 2, 2), me // 4
    counter = [0]

    def chip(dx, dy, dz):
        zz, bit = z, 1
        while bit < nz:
            if dz & bit:
                zz = zz + bit - 2 * bit * lax.rem(z // bit, 2)
            bit *= 2
        return zz * 4 + lax.rem(y + dy, 2) * 2 + lax.rem(x + dx, 2)

    def send(src, dst, dev):
        i = counter[0]
        counter[0] += 1
        copy = pltpu.make_async_remote_copy(
            src_ref=src, dst_ref=dst, send_sem=ssem.at[i], recv_sem=rsem.at[i],
            device_id=dev, device_id_type=MESH,
        )
        copy.start()
        sent.append(copy)
        return copy

    sent = []
    x_dev = {"img": chip(1, 0, 0)}
    y_dev = {"img": chip(0, 1, 0)}
    z_dev = [{"img": chip(0, 0, k)} for k in range(nz)]
    r_dev = [{"ref": lax.rem(rme + k, n_ref)} for k in range(n_ref)]

    ref_copies = []
    for q, (dx, dy) in enumerate(QUADS):
        for dz in range(nz):
            s = q * nz + dz
            copy = pltpu.make_async_copy(
                ref_hbm.at[pl.ds(chip(dx, dy, dz) * rb, rb)],
                refs.at[pl.ds(s * rb, rb)], ref_sem.at[s],
            )
            copy.start()
            ref_copies.append(copy)
    im_copies = []
    for b in range(n // LANES):
        at = b * LANES
        if paired:
            at = lax.rem(rme * mine + at, n)
        part = pl.ds(b * LANES, LANES)
        copy = pltpu.make_async_copy(im_hbm.at[pl.ds(at, LANES)], im.at[part], im_sem.at[b])
        im_copies.append(copy)
    first_theirs = mine // LANES if paired else 0
    for b in range(n // LANES):
        im_copies[(b + first_theirs) % (n // LANES)].start()

    barrier = pltpu.get_barrier_semaphore()
    peers = [x_dev, y_dev] + [z_dev[k] for k in range(1, nz) if k & (k - 1) == 0] + r_dev[1:]
    for dev in peers:
        pl.semaphore_signal(barrier, inc=1, device_id=dev, device_id_type=MESH)

    stat_snd[...] = jnp.zeros_like(stat_snd)

    def lanes_of(k):
        return pl.ds(pl.multiple_of(lax.rem(rme + k, n_ref) * mine, 128), mine)

    if paired:
        for k in range(n_ref):
            vecs[0:1, k * mine : (k + 1) * mine] = prior_ref[:, lanes_of(k)]
    else:
        vecs[0:1, :] = prior_ref[...]
    vecs[3:4, :] = vecs[0:1, :]

    def square_sums(source, r0, count, scale):
        block = source[r0 : r0 + count, :].astype(F32)
        total = jnp.sum(block * block, axis=1, keepdims=True) * scale
        norms[r0 : r0 + count, :] = jnp.broadcast_to(total, (count, 128))

    for s, copy in enumerate(ref_copies):
        copy.wait()
        square_sums(refs, s * rb, rb, 1.0)

    nt = (((1,), (1,)), ((), ()))
    nn = (((1,), (0,)), ((), ()))

    def score_block(source, r0, count, scale):
        def body(b, carry):
            part = pl.ds(pl.multiple_of(b * LANES, LANES), LANES)
            out = lax.dot_general(
                source[r0 : r0 + count, :], im[part, :], nt, preferred_element_type=F32
            )
            cross[r0 : r0 + count, part] = out if scale is None else out * scale
            return carry

        lax.fori_loop(0, n // LANES, body, 0)

    def fold(x):
        return x.reshape(x.shape[0] // 8, 8, 128)

    def spread8(x):
        return jnp.broadcast_to(x, (8, 128))

    def coefficients(c0, width_):
        a = vecs[0:1, c0 : c0 + width_]
        slope = (sharpness * LOG2E) * a
        bend = (0.5 * sharpness * LOG2E) * (a * a)
        tiles = range(0, width_, 128)
        return (
            [spread8(slope[:, t : t + 128]) for t in tiles],
            [spread8(bend[:, t : t + 128]) for t in tiles],
        )

    def over_rows(count, body, init):
        return lax.fori_loop(
            0, count // ROWS, lambda i, c: body(pl.multiple_of(i * ROWS, ROWS), c), init
        )

    def scores(parts, c0, width_, keep):
        slope, bend = coefficients(c0, width_)
        tiles = width_ // 128
        high = tuple(jnp.full((8, 128), -jnp.inf, F32) for _ in range(tiles))
        k0 = 0
        for values, norm, v0 in parts:

            def body(r, high, values=values, norm=norm, v0=v0, k0=k0):
                rows_ = pl.ds(r, ROWS)
                nrm = fold(norm[rows_, :])
                out = []
                for t in range(tiles):
                    c = fold(values[rows_, v0 + t * 128 : v0 + (t + 1) * 128])
                    sc = slope[t][None] * c - bend[t][None] * nrm
                    keep[pl.ds(k0 + r, ROWS), t * 128 : (t + 1) * 128] = sc.reshape(ROWS, 128)
                    out.append(jnp.maximum(high[t], jnp.max(sc, axis=0)))
                return tuple(out)

            high = over_rows(values.shape[0], body, high)
            k0 += values.shape[0]
        return [jnp.max(h, axis=0, keepdims=True) for h in high]

    def sums_of(parts, high, keep, full):
        tiles = len(high)
        top = [spread8(h) for h in high]
        zero = jnp.zeros((8, 128), F32)
        carry = tuple(zero for _ in range(tiles * (3 if full else 1)))
        k0 = 0
        for values, norm, v0 in parts:

            def body(r, carry, values=values, norm=norm, v0=v0, k0=k0):
                rows_ = pl.ds(r, ROWS)
                nrm = fold(norm[rows_, :]) if full else None
                out = list(carry)
                for t in range(tiles):
                    sc = fold(keep[pl.ds(k0 + r, ROWS), t * 128 : (t + 1) * 128])
                    e = jnp.exp2(sc - top[t][None])
                    out[t] = out[t] + jnp.sum(e, axis=0)
                    if full:
                        c = fold(values[rows_, v0 + t * 128 : v0 + (t + 1) * 128])
                        out[tiles + t] = out[tiles + t] + jnp.sum(e * c, axis=0)
                        out[2 * tiles + t] = out[2 * tiles + t] + jnp.sum(e * nrm, axis=0)
                return tuple(out)

            carry = over_rows(values.shape[0], body, carry)
            k0 += values.shape[0]
        return [jnp.sum(x, axis=0, keepdims=True) for x in carry]

    def statistics(it, full):
        for c0 in range(0, n, BLOCK):
            parts = [(cross, norms, c0)]
            high = scores(parts, c0, BLOCK, keep)
            sums = sums_of(parts, high, keep, full)
            for t in range(BLOCK // 128):
                at = slice(c0 + t * 128, c0 + (t + 1) * 128)
                stat_snd[it, 0:1, at] = high[t]
                for j in range(len(sums) // len(high)):
                    stat_snd[it, j + 1 : j + 2, at] = sums[j * len(high) + t]
        copies = [
            send(stat_snd.at[it], stat_rcv.at[it * (n_ref - 1) + k - 1], r_dev[k])
            for k in range(1, n_ref)
        ]
        for copy in copies:
            copy.wait_recv()
        blocks = [stat_snd[it]]
        for k in range(1, n_ref):
            theirs = stat_rcv[it * (n_ref - 1) + k - 1]
            if paired:
                theirs = jnp.concatenate([theirs[:, mine:], theirs[:, :mine]], axis=1)
            blocks.append(theirs)
        high = functools.reduce(jnp.maximum, [blk[0:1] for blk in blocks])
        scales = [jnp.exp2(blk[0:1] - high) for blk in blocks]
        sums = [
            functools.reduce(jnp.add, [blk[j : j + 1] * sc for blk, sc in zip(blocks, scales)])
            for j in ((1, 2, 3) if full else (1,))
        ]
        return high, sums

    def weigh(c0, width_):
        slope, bend = coefficients(c0, width_)
        tiles = range(width_ // 128)
        top = [spread8(vecs[1:2, c0 + t * 128 : c0 + (t + 1) * 128]) for t in tiles]
        gain = [spread8(vecs[2:3, c0 + t * 128 : c0 + (t + 1) * 128]) for t in tiles]

        def body(r, carry):
            rows_ = pl.ds(r, ROWS)
            nrm = fold(norms[rows_, :])
            for t in tiles:
                at = slice(c0 + t * 128, c0 + (t + 1) * 128)
                sc = slope[t][None] * fold(cross[rows_, at]) - bend[t][None] * nrm
                e = jnp.exp2(sc - top[t][None]) * gain[t][None]
                w[rows_, at] = e.reshape(ROWS, 128).astype(BF16)
            return carry

        over_rows(rows, body, 0)

    if paired:
        pcross, pnorms, given, taken = split
        given[...] = jnp.zeros_like(given)


        def score_slot(b):
            im_copies[b].wait()
            part = slice(b * LANES, (b + 1) * LANES)
            cross[:, part] = lax.dot_general(
                refs[...], im[part, :], nt, preferred_element_type=F32
            )

        handed = []
        for b in range(mine // LANES, n // LANES):
            score_slot(b)
            if not handed:
                pl.semaphore_wait(barrier, len(peers))
                handed.append(send(norms, pnorms, r_dev[1]))
            at = pl.ds((b - mine // LANES) * LANES, LANES)
            handed.append(send(cross.at[:, pl.ds(b * LANES, LANES)], pcross.at[:, at], r_dev[1]))
        for b in range(mine // LANES):
            score_slot(b)
        for copy in handed:
            copy.wait_recv()
        parts = [(cross, norms, 0), (pcross, pnorms, 0)]
        tiles = mine // 128
        for it in range(ITERS + 1):
            high = scores(parts, 0, mine, keep)
            sums = sums_of(parts, high, keep, it < ITERS)
            for t in range(tiles):
                at = slice(t * 128, (t + 1) * 128)
                total = sums[t]
                if it < ITERS:
                    along, weight = sums[tiles + t], sums[2 * tiles + t]
                    vecs[0:1, at] = (along / total + prior_weight * vecs[3:4, at]) / (
                        weight / total + prior_weight
                    )
                else:
                    a = vecs[0:1, at]
                    vecs[1:2, at] = high[t]
                    vecs[2:3, at] = a / total
                    given[0:1, at] = a
                    given[1:2, at] = high[t]
                    given[2:3, at] = a / total
        swap = send(given, taken, r_dev[1])
        weigh(0, mine)
        swap.wait_recv()
        vecs[0:3, mine:n] = taken[0:3, :]
        for k in range(n_ref):
            contrast_ref[:, lanes_of(k)] = vecs[0:1, k * mine : (k + 1) * mine]
        weigh(mine, mine)
        for copy in handed:
            copy.wait_send()
            sent.remove(copy)
    else:
        for copy in im_copies:
            copy.wait()
        score_block(refs, 0, rows, None)
        pl.semaphore_wait(barrier, len(peers))
        for it in range(ITERS):
            high, (total, along, weight) = statistics(it, True)
            vecs[0:1, :] = (along / total + prior_weight * vecs[3:4, :]) / (
                weight / total + prior_weight
            )
        high, (total,) = statistics(ITERS, False)
        vecs[1:2, :] = high
        vecs[2:3, :] = vecs[0:1, :] / total
        contrast_ref[...] = vecs[0:1, :]
        for c0 in range(0, n, BLOCK):
            weigh(c0, BLOCK)

    def weighted(r0s, c0, store):
        def body(b, carry):
            col = pl.multiple_of(b * LANES, LANES)
            lhs = [w[r0 : r0 + cnt, :] for r0, cnt in r0s]
            lhs = lhs[0] if len(lhs) == 1 else jnp.concatenate(lhs, axis=0)
            rhs = im[:, pl.ds(pl.multiple_of(c0 + col, LANES), LANES)]
            out = lax.dot_general(lhs, rhs, nn, preferred_element_type=F32)
            store(pl.ds(col, LANES), out[:qr], out[qr:])
            return carry

        lax.fori_loop(0, half // LANES, body, 0)

    def to_send(stream, first_is_far):
        def store(cols, lo, hi):
            far, near = (lo, hi) if first_is_far else (hi, lo)
            snd1[stream * 2, :, cols] = far.astype(BF16)
            snd1[stream * 2 + 1, :, cols] = near.astype(BF16)

        return store

    def to_keep(stream):
        def store(cols, lo, hi):
            acc[stream * 2, :, cols] = lo
            acc[stream * 2 + 1, :, cols] = hi

        return store

    low = [dz & -dz for dz in range(nz)]
    order = sorted(range(1, nz), key=lambda k: (low[k], -k)) + [0]
    early = [dz for dz in order if low[dz] == 1] or order
    late = [dz for dz in order if dz not in early]
    hop_dev = (x_dev, y_dev)
    step1 = {}

    def send1(s, j, dzs):
        for dz in dzs:
            part = pl.ds(dz * rb, rb)
            step1[s, j, dz] = send(
                snd1.at[s * 2 + j, part], rcv1.at[s * 2 + j, part], hop_dev[s]
            )

    weighted([(0, 2 * qr)], 0, to_send(0, False))
    send1(0, 0, early)
    send1(0, 1, early)
    weighted([(qr, 2 * qr)], half, to_send(1, True))
    send1(1, 0, early)
    send1(1, 1, early)
    weighted([(2 * qr, 2 * qr)], 0, to_keep(0))
    weighted([(0, qr), (3 * qr, qr)], half, to_keep(1))

    step2 = {}

    def send2(dzs):
        for dz in dzs:
            r0 = dz * rb
            part = pl.ds(r0, rb)
            for s in (1, 0):
                step1[s, 0, dz].wait_recv()
                snd2[s, r0 : r0 + rb, :] = (
                    acc[s * 2, r0 : r0 + rb, :] + rcv1[s * 2, r0 : r0 + rb, :].astype(F32)
                ).astype(BF16)
                step2[s, dz] = send(snd2.at[s, part], rcv2.at[s, part], hop_dev[1 - s])

    def gained(s, dz):
        step1[s, 1, dz].wait_recv()
        step2[s, dz].wait_recv()
        r0 = dz * rb
        return (
            acc[s * 2 + 1, r0 : r0 + rb, :]
            + rcv1[s * 2 + 1, r0 : r0 + rb, :].astype(F32)
            + rcv2[s, r0 : r0 + rb, :].astype(F32)
        )

    step3 = {}

    def complete(s, dz):
        total = gained(s, dz)
        for k in range(nz):
            if low[k] and k - low[k] == dz and (dz == 0 or low[k] < low[dz]):
                step3[s, k].wait_recv()
                total = total + rcv3[s, k - 1].astype(F32)
        return total

    def send3(dzs):
        for dz in dzs:
            for s in (0, 1):
                snd3[s, dz - 1] = complete(s, dz).astype(BF16)
                step3[s, dz] = send(
                    snd3.at[s, dz - 1], rcv3.at[s, dz - 1], z_dev[low[dz]]
                )

    send2(early)
    middle = [dz for dz in late if dz]
    final = [dz for dz in late if not dz]
    for j, dzs in ((0, middle), (1, middle), (0, final)):
        for s in (0, 1):
            send1(s, j, dzs)
    if late:
        send3(early)
    send2(middle)
    for s in (0, 1):
        send1(s, 1, final)
    send2(final)
    send3(middle)
    for s in (0, 1):
        acc[s * 2 + 1, 0:rb, :] = complete(s, 0)

    left, right = acc[1, 0:rb, :], acc[3, 0:rb, :]
    square = jnp.sum(left * left, axis=1, keepdims=True) + jnp.sum(
        right * right, axis=1, keepdims=True
    )
    factor = lax.rsqrt(square / width + epsilon)
    own = 3 * qr
    gath[own : own + rb, 0:half] = (left * factor).astype(BF16)
    gath[own : own + rb, half:width] = (right * factor).astype(BF16)

    def piece(q, dz, s):
        return gath.at[pl.ds(q * qr + dz * rb, rb), pl.ds(s * half, half)]

    def slot(q, dz):
        return gath.at[pl.ds(q * qr + dz * rb, rb)]

    along_z = {}

    def double(dz, bits):
        for bit in bits:
            along_z[dz + bit] = send(slot(3, dz), slot(3, dz + bit), z_dev[bit])

    bits = [1 << j for j in range(nz.bit_length() - 1)]
    into_x, into_y, last = {}, {}, []

    def spread(dz):
        into_y[dz] = [send(piece(3, dz, 0), piece(2, dz, 0), y_dev)]
        into_x[dz] = [send(piece(3, dz, 1), piece(0, dz, 1), x_dev)]
        into_y[dz].append(send(piece(3, dz, 1), piece(2, dz, 1), y_dev))
        into_x[dz].append(send(piece(3, dz, 0), piece(0, dz, 0), x_dev))

    def forward(dz):
        into_y[dz][0].wait_recv()
        last.append(send(piece(2, dz, 0), piece(1, dz, 0), x_dev))
        into_x[dz][0].wait_recv()
        last.append(send(piece(0, dz, 1), piece(1, dz, 1), y_dev))

    outs = []

    def finish(q):
        dx, dy = QUADS[q]
        for dz in range(nz):
            copy = pltpu.make_async_copy(
                slot(q, dz), newref_hbm.at[pl.ds(chip(dx, dy, dz) * rb, rb)],
                out_sem.at[q * nz + dz],
            )
            copy.start()
            outs.append(copy)
        square_sums(gath, q * qr, qr, 1.0 / width)

    double(0, bits)
    spread(0)
    arrivals = sorted(range(1, nz), key=lambda k: (k.bit_count(), k))
    before = 0
    for dz in arrivals:
        along_z[dz].wait_recv()
        double(dz, [bit for bit in bits if bit < low[dz]])
        spread(dz)
        forward(before)
        before = dz
    forward(before)
    for dz in range(nz):
        into_y[dz][1].wait_recv()
    finish(3)
    finish(2)
    score_block(gath, 2 * qr, 2 * qr, width ** (-0.5))
    for dz in range(nz):
        into_x[dz][1].wait_recv()
    finish(0)
    for copy in last:
        copy.wait_recv()
    finish(1)
    score_block(gath, 0, 2 * qr, width ** (-0.5))

    high, (total,) = statistics(ITERS + 1, False)
    loglik = high * math.log(2.0) + jnp.log(total) - math.log(rows * n_ref)
    if paired:
        for k in range(n_ref):
            loglik_ref[:, lanes_of(k)] = loglik[:, k * mine : (k + 1) * mine]
    else:
        loglik_ref[...] = loglik
    for copy in outs:
        copy.wait()
    for copy in sent:
        copy.wait_send()


def per_device(nz, n_ref, images, references, initial_contrast):
    n, width = images.shape
    rows = references.shape[0]
    rb = rows // (4 * nz)
    qr, half = nz * rb, width // 2
    steps = ITERS + 2
    paired = n_ref == 2 and n % (2 * LANES) == 0
    copies = 8 + steps * (n_ref - 1) + 6 * nz + 2 * (nz - 1) + (nz - 1) + 6 * nz
    peers = max(n_ref - 1, 1)
    flops = 6 * n * width * rows
    split = []
    if paired:
        split = [
            pltpu.VMEM((rows, n // 2), F32),
            pltpu.VMEM((rows, 128), F32),
            pltpu.VMEM((8, n // 2), F32),
            pltpu.VMEM((8, n // 2), F32),
        ]
    new_references, contrast, loglik = pl.pallas_call(
        functools.partial(kernel, nz, n_ref),
        out_shape=(
            pltpu.VMEM((rows, width), BF16),
            pltpu.VMEM((1, n), F32),
            pltpu.VMEM((1, n), F32),
        ),
        in_specs=[
            pl.BlockSpec(memory_space=pl.ANY),
            pl.BlockSpec(memory_space=pl.ANY),
            pl.BlockSpec(memory_space=pltpu.VMEM),
        ],
        out_specs=(
            pl.BlockSpec(memory_space=pltpu.VMEM),
            pl.BlockSpec(memory_space=pltpu.VMEM),
            pl.BlockSpec(memory_space=pltpu.VMEM),
        ),
        scratch_shapes=[
            pltpu.VMEM((n, width), BF16),
            pltpu.VMEM((rows, width), BF16),
            pltpu.VMEM((rows, 128), F32),
            pltpu.VMEM((rows, n), F32),
            pltpu.VMEM((rows, n), BF16),
            pltpu.VMEM((4, qr, half), BF16),
            pltpu.VMEM((4, qr, half), BF16),
            pltpu.VMEM((4, qr, half), F32),
            pltpu.VMEM((2, qr, half), BF16),
            pltpu.VMEM((2, qr, half), BF16),
            pltpu.VMEM((2, max(nz - 1, 1), rb, half), BF16),
            pltpu.VMEM((2, max(nz - 1, 1), rb, half), BF16),
            pltpu.VMEM((rows, width), BF16),
            pltpu.VMEM((steps, 4, n), F32),
            pltpu.VMEM((steps * peers, 4, n), F32),
            pltpu.VMEM((8, n), F32),
            pltpu.VMEM(((2 if paired else 1) * rows, BLOCK), F32),
            *split,
            pltpu.SemaphoreType.DMA((n // LANES,)),
            pltpu.SemaphoreType.DMA((4 * nz,)),
            pltpu.SemaphoreType.DMA((4 * nz,)),
            pltpu.SemaphoreType.DMA((copies,)),
            pltpu.SemaphoreType.DMA((copies,)),
        ],
        compiler_params=pltpu.CompilerParams(
            collective_id=0, has_side_effects=True, vmem_limit_bytes=56 * 1024 * 1024
        ),
        cost_estimate=pl.CostEstimate(
            flops=flops, bytes_accessed=2 * n * width, transcendentals=0
        ),
    )(images, references, initial_contrast[None, :])
    return (new_references, contrast[0], loglik[0])


def solution(mesh):
    n_img, n_ref = mesh.shape["img"], mesh.shape["ref"]
    placed = (P("img", None), P("ref", None), P("img"))
    return jax.shard_map(
        functools.partial(per_device, n_img // 4, n_ref),
        mesh=mesh,
        in_specs=placed,
        out_specs=(P("ref", None), P("img"), P("img")),
        check_vma=False,
    )
```

```python
import functools
import math

import jax
import jax.numpy as jnp
from jax import lax
from jax.experimental import pallas as pl
from jax.experimental.pallas import tpu as pltpu
from jax.sharding import PartitionSpec as P

ITERS = 3

sharpness = 2.0
prior_weight = 1.0
epsilon = 1e-06

MESH = pl.DeviceIdType.MESH
LANES = 256
BLOCK = 512
TILES = BLOCK // 128
ROWS = 64
LOG2E = math.log2(math.e)
QUADS = ((1, 0), (1, 1), (0, 1), (0, 0))
F32 = jnp.float32
BF16 = jnp.bfloat16


def kernel(
    nz, n_ref, im_hbm, ref_hbm, prior_hbm, newref_hbm, contrast_ref, loglik_ref,
    im, refs, norms, cross, w, snd1, rcv1, acc, snd2, rcv2, snd3, rcv3, gath,
    stat_snd, stat_rcv, vecs, keep, prior_sem,
    stat_ssem, stat_rsem, im_sem, ref_sem, out_sem, ssem, rsem,
):
    n, width = im.shape
    rows = refs.shape[0]
    rb = rows // (4 * nz)
    qr = nz * rb
    half = width // 2
    me = lax.axis_index("img")
    rme = lax.axis_index("ref")
    x, y, z = lax.rem(me, 2), lax.rem(me // 2, 2), me // 4
    counter = [0]

    def chip(dx, dy, dz):
        zz, bit = z, 1
        while bit < nz:
            if dz & bit:
                zz = zz + bit - 2 * bit * lax.rem(z // bit, 2)
            bit *= 2
        return zz * 4 + lax.rem(y + dy, 2) * 2 + lax.rem(x + dx, 2)

    def send(src, dst, dev):
        i = counter[0]
        counter[0] += 1
        copy = pltpu.make_async_remote_copy(
            src_ref=src, dst_ref=dst, send_sem=ssem.at[i], recv_sem=rsem.at[i],
            device_id=dev, device_id_type=MESH,
        )
        copy.start()
        sent.append(copy)
        return copy

    sent = []
    x_dev = {"img": chip(1, 0, 0)}
    y_dev = {"img": chip(0, 1, 0)}
    z_dev = [{"img": chip(0, 0, k)} for k in range(nz)]
    r_dev = [{"ref": lax.rem(rme + k, n_ref)} for k in range(n_ref)]

    barrier = pltpu.get_barrier_semaphore()
    peers = r_dev[1:] + [x_dev, y_dev] + [z_dev[k] for k in range(1, nz) if k & (k - 1) == 0]
    for dev in peers:
        pl.semaphore_signal(barrier, inc=1, device_id=dev, device_id_type=MESH)

    ref_copies = []
    for q, (dx, dy) in enumerate(QUADS):
        for dz in range(nz):
            s = q * nz + dz
            copy = pltpu.make_async_copy(
                ref_hbm.at[pl.ds(chip(dx, dy, dz) * rb, rb)],
                refs.at[pl.ds(s * rb, rb)], ref_sem.at[s],
            )
            copy.start()
            ref_copies.append(copy)
    im_copies = []
    for b in range(n // LANES):
        part = pl.ds(b * LANES, LANES)
        copy = pltpu.make_async_copy(im_hbm.at[part], im.at[part], im_sem.at[b])
        copy.start()
        im_copies.append(copy)
    prior_copy = pltpu.make_async_copy(prior_hbm, vecs.at[3:4, :], prior_sem)
    prior_copy.start()

    stat_snd[...] = jnp.zeros_like(stat_snd)

    def square_sums(source, r0, count, scale):
        block = source[r0 : r0 + count, :].astype(F32)
        total = jnp.sum(block * block, axis=1, keepdims=True) * scale
        norms[r0 : r0 + count, :] = jnp.broadcast_to(total, (count, 128))

    for s, copy in enumerate(ref_copies):
        copy.wait()
        square_sums(refs, s * rb, rb, 1.0)

    nt = (((1,), (1,)), ((), ()))
    nn = (((1,), (0,)), ((), ()))

    def score_block(source, r0, count, scale):
        def body(b, carry):
            part = pl.ds(pl.multiple_of(b * LANES, LANES), LANES)
            out = lax.dot_general(
                source[r0 : r0 + count, :], im[part, :], nt, preferred_element_type=F32
            )
            cross[r0 : r0 + count, part] = out if scale is None else out * scale
            return carry

        lax.fori_loop(0, n // LANES, body, 0)

    def fold(x):
        return x.reshape(x.shape[0] // 8, 8, 128)

    def spread8(x):
        return jnp.broadcast_to(x, (8, 128))

    def lanes(c0, width_=128):
        return pl.ds(pl.multiple_of(c0, 128), width_)

    def coefficients(c0, width_):
        a = vecs[0:1, lanes(c0, width_)]
        slope = (sharpness * LOG2E) * a
        bend = (0.5 * sharpness * LOG2E) * (a * a)
        tiles = range(0, width_, 128)
        return (
            [spread8(slope[:, t : t + 128]) for t in tiles],
            [spread8(bend[:, t : t + 128]) for t in tiles],
        )

    def over_rows(count, body, init):
        return lax.fori_loop(
            0, count // ROWS, lambda i, c: body(pl.multiple_of(i * ROWS, ROWS), c), init
        )

    def scores(c0):
        slope, bend = coefficients(c0, BLOCK)

        def body(r, high):
            part = pl.ds(r, ROWS)
            nrm = fold(norms[part, :])
            out = []
            for t in range(TILES):
                c = fold(cross[part, lanes(c0 + t * 128)])
                sc = slope[t][None] * c - bend[t][None] * nrm
                keep[part, t * 128 : (t + 1) * 128] = sc.reshape(ROWS, 128)
                out.append(jnp.maximum(high[t], jnp.max(sc, axis=0)))
            return tuple(out)

        high = over_rows(rows, body, (jnp.full((8, 128), -jnp.inf, F32),) * TILES)
        return [jnp.max(x, axis=0, keepdims=True) for x in high]

    def sums_of(c0, high, full):
        top = [spread8(x) for x in high]

        def body(r, carry):
            part = pl.ds(r, ROWS)
            nrm = fold(norms[part, :]) if full else None
            out = list(carry)
            for t in range(TILES):
                sc = fold(keep[part, t * 128 : (t + 1) * 128])
                e = jnp.exp2(sc - top[t][None])
                out[t] = out[t] + jnp.sum(e, axis=0)
                if full:
                    c = fold(cross[part, lanes(c0 + t * 128)])
                    out[TILES + t] = out[TILES + t] + jnp.sum(e * c, axis=0)
                    out[2 * TILES + t] = out[2 * TILES + t] + jnp.sum(e * nrm, axis=0)
            return tuple(out)

        zero = jnp.zeros((8, 128), F32)
        carry = over_rows(rows, body, (zero,) * (TILES * (3 if full else 1)))
        return [jnp.sum(x, axis=0, keepdims=True) for x in carry]

    def weigh(c0):
        slope, bend = coefficients(c0, BLOCK)
        top = [spread8(vecs[1:2, lanes(c0 + t * 128)]) for t in range(TILES)]
        gain = [spread8(vecs[2:3, lanes(c0 + t * 128)]) for t in range(TILES)]

        def body(r, carry):
            part = pl.ds(r, ROWS)
            nrm = fold(norms[part, :])
            for t in range(TILES):
                at = lanes(c0 + t * 128)
                sc = slope[t][None] * fold(cross[part, at]) - bend[t][None] * nrm
                e = jnp.exp2(sc - top[t][None]) * gain[t][None]
                w[part, at] = e.reshape(ROWS, 128).astype(BF16)
            return carry

        over_rows(rows, body, 0)

    blocks = n // BLOCK

    def stat_copy(it, h, k):
        slot = (it * blocks + h) * (n_ref - 1) + k - 1
        return pltpu.make_async_remote_copy(
            src_ref=stat_snd.at[it, h], dst_ref=stat_rcv.at[slot],
            send_sem=stat_ssem.at[slot], recv_sem=stat_rsem.at[slot],
            device_id=r_dev[k], device_id_type=MESH,
        )

    def local_stats(it, h, full):
        c0 = h * BLOCK
        high = scores(c0)
        sums = sums_of(c0, high, full)
        for t in range(TILES):
            at = slice(t * 128, (t + 1) * 128)
            stat_snd[it, h, 0:1, at] = high[t]
            for j in range(len(sums) // TILES):
                stat_snd[it, h, j + 1 : j + 2, at] = sums[j * TILES + t]
        for k in range(1, n_ref):
            stat_copy(it, h, k).start()

    def joint_stats(it, h, full):
        shares = [stat_snd[it, h]]
        for k in range(1, n_ref):
            stat_copy(it, h, k).wait_recv()
            shares.append(stat_rcv[(it * blocks + h) * (n_ref - 1) + k - 1])
        high = functools.reduce(jnp.maximum, [share[0:1] for share in shares])
        scales = [jnp.exp2(share[0:1] - high) for share in shares]
        sums = [
            functools.reduce(
                jnp.add, [share[j : j + 1] * sc for share, sc in zip(shares, scales)]
            )
            for j in ((1, 2, 3) if full else (1,))
        ]
        return high, sums

    def each(count, body):
        def step(i, carry):
            body(i)
            return carry

        lax.fori_loop(0, count, step, 0)


    prior_copy.wait()
    vecs[0:1, :] = vecs[3:4, :]

    def first_cross(b):
        part = pl.ds(pl.multiple_of(b * LANES, LANES), LANES)
        pltpu.make_async_copy(im_hbm.at[part], im.at[part], im_sem.at[b]).wait()
        cross[:, part] = lax.dot_general(
            refs[...], im[part, :], nt, preferred_element_type=F32
        )

    def refit(i):
        it, h = i // blocks, lax.rem(i, blocks)
        at = lanes(h * BLOCK, BLOCK)
        _, (total, along, weight) = joint_stats(it, h, True)
        vecs[0:1, at] = (along / total + prior_weight * vecs[3:4, at]) / (
            weight / total + prior_weight
        )
        local_stats(it + 1, h, True)

    def settle(h):
        at = lanes(h * BLOCK, BLOCK)
        high, (total,) = joint_stats(ITERS, h, False)
        vecs[1:2, at] = high
        vecs[2:3, at] = vecs[0:1, at] / total
        weigh(h * BLOCK)

    each(n // LANES, first_cross)
    pl.semaphore_wait(barrier, len(peers))
    each(blocks, lambda h: local_stats(0, h, True))
    each(ITERS * blocks, refit)
    each(blocks, settle)
    contrast_ref[...] = vecs[0:1, :]

    def weighted(r0s, c0, store):
        def body(b, carry):
            col = pl.multiple_of(b * LANES, LANES)
            lhs = [w[r0 : r0 + cnt, :] for r0, cnt in r0s]
            lhs = lhs[0] if len(lhs) == 1 else jnp.concatenate(lhs, axis=0)
            rhs = im[:, pl.ds(pl.multiple_of(c0 + col, LANES), LANES)]
            out = lax.dot_general(lhs, rhs, nn, preferred_element_type=F32)
            store(pl.ds(col, LANES), out[:qr], out[qr:])
            return carry

        lax.fori_loop(0, half // LANES, body, 0)

    def to_send(stream, first_is_far):
        def store(cols, lo, hi):
            far, near = (lo, hi) if first_is_far else (hi, lo)
            snd1[stream * 2, :, cols] = far.astype(BF16)
            snd1[stream * 2 + 1, :, cols] = near.astype(BF16)

        return store

    def to_keep(stream):
        def store(cols, lo, hi):
            acc[stream * 2, :, cols] = lo
            acc[stream * 2 + 1, :, cols] = hi

        return store

    low = [dz & -dz for dz in range(nz)]
    order = sorted(range(1, nz), key=lambda k: (low[k], -k)) + [0]
    early = [dz for dz in order if low[dz] == 1] or order
    late = [dz for dz in order if dz not in early]
    hop_dev = (x_dev, y_dev)
    step1 = {}

    def send1(s, j, dzs):
        for dz in dzs:
            part = pl.ds(dz * rb, rb)
            step1[s, j, dz] = send(
                snd1.at[s * 2 + j, part], rcv1.at[s * 2 + j, part], hop_dev[s]
            )

    weighted([(0, 2 * qr)], 0, to_send(0, False))
    send1(0, 0, early)
    send1(0, 1, early)
    weighted([(qr, 2 * qr)], half, to_send(1, True))
    send1(1, 0, early)
    send1(1, 1, early)
    weighted([(2 * qr, 2 * qr)], 0, to_keep(0))
    weighted([(0, qr), (3 * qr, qr)], half, to_keep(1))

    step2 = {}

    def send2(dzs):
        for dz in dzs:
            r0 = dz * rb
            part = pl.ds(r0, rb)
            for s in (1, 0):
                step1[s, 0, dz].wait_recv()
                snd2[s, r0 : r0 + rb, :] = (
                    acc[s * 2, r0 : r0 + rb, :] + rcv1[s * 2, r0 : r0 + rb, :].astype(F32)
                ).astype(BF16)
                step2[s, dz] = send(snd2.at[s, part], rcv2.at[s, part], hop_dev[1 - s])

    def gained(s, dz):
        step1[s, 1, dz].wait_recv()
        step2[s, dz].wait_recv()
        r0 = dz * rb
        return (
            acc[s * 2 + 1, r0 : r0 + rb, :]
            + rcv1[s * 2 + 1, r0 : r0 + rb, :].astype(F32)
            + rcv2[s, r0 : r0 + rb, :].astype(F32)
        )

    step3 = {}

    def complete(s, dz):
        total = gained(s, dz)
        for k in range(nz):
            if low[k] and k - low[k] == dz and (dz == 0 or low[k] < low[dz]):
                step3[s, k].wait_recv()
                total = total + rcv3[s, k - 1].astype(F32)
        return total

    def send3(dzs):
        for dz in dzs:
            for s in (0, 1):
                snd3[s, dz - 1] = complete(s, dz).astype(BF16)
                step3[s, dz] = send(
                    snd3.at[s, dz - 1], rcv3.at[s, dz - 1], z_dev[low[dz]]
                )

    send2(early)
    middle = [dz for dz in late if dz]
    final = [dz for dz in late if not dz]
    for j, dzs in ((0, middle), (1, middle), (0, final)):
        for s in (0, 1):
            send1(s, j, dzs)
    if late:
        send3(early)
    send2(middle)
    for s in (0, 1):
        send1(s, 1, final)
    send2(final)
    send3(middle)
    for s in (0, 1):
        acc[s * 2 + 1, 0:rb, :] = complete(s, 0)

    left, right = acc[1, 0:rb, :], acc[3, 0:rb, :]
    square = jnp.sum(left * left, axis=1, keepdims=True) + jnp.sum(
        right * right, axis=1, keepdims=True
    )
    factor = lax.rsqrt(square / width + epsilon)
    own = 3 * qr
    gath[own : own + rb, 0:half] = (left * factor).astype(BF16)
    gath[own : own + rb, half:width] = (right * factor).astype(BF16)

    def piece(q, dz, s):
        return gath.at[pl.ds(q * qr + dz * rb, rb), pl.ds(s * half, half)]

    def slot(q, dz):
        return gath.at[pl.ds(q * qr + dz * rb, rb)]

    along_z = {}

    def double(dz, bits):
        for bit in bits:
            along_z[dz + bit] = send(slot(3, dz), slot(3, dz + bit), z_dev[bit])

    bits = [1 << j for j in range(nz.bit_length() - 1)]
    into_x, into_y, last = {}, {}, []

    def spread(dz):
        into_y[dz] = [send(piece(3, dz, 0), piece(2, dz, 0), y_dev)]
        into_x[dz] = [send(piece(3, dz, 1), piece(0, dz, 1), x_dev)]
        into_y[dz].append(send(piece(3, dz, 1), piece(2, dz, 1), y_dev))
        into_x[dz].append(send(piece(3, dz, 0), piece(0, dz, 0), x_dev))

    def forward(dz):
        into_y[dz][0].wait_recv()
        last.append(send(piece(2, dz, 0), piece(1, dz, 0), x_dev))
        into_x[dz][0].wait_recv()
        last.append(send(piece(0, dz, 1), piece(1, dz, 1), y_dev))

    outs = []

    def finish(q):
        dx, dy = QUADS[q]
        for dz in range(nz):
            copy = pltpu.make_async_copy(
                slot(q, dz), newref_hbm.at[pl.ds(chip(dx, dy, dz) * rb, rb)],
                out_sem.at[q * nz + dz],
            )
            copy.start()
            outs.append(copy)
        square_sums(gath, q * qr, qr, 1.0 / width)

    double(0, bits)
    spread(0)
    arrivals = sorted(range(1, nz), key=lambda k: (k.bit_count(), k))
    before = 0
    for dz in arrivals:
        along_z[dz].wait_recv()
        double(dz, [bit for bit in bits if bit < low[dz]])
        spread(dz)
        forward(before)
        before = dz
    forward(before)
    for dz in range(nz):
        into_y[dz][1].wait_recv()
    finish(3)
    finish(2)
    score_block(gath, 2 * qr, 2 * qr, width ** (-0.5))
    for dz in range(nz):
        into_x[dz][1].wait_recv()
    finish(0)
    for copy in last:
        copy.wait_recv()
    finish(1)
    score_block(gath, 0, 2 * qr, width ** (-0.5))

    def final_likelihood(h):
        high, (total,) = joint_stats(ITERS + 1, h, False)
        loglik_ref[:, lanes(h * BLOCK, BLOCK)] = (
            high * math.log(2.0) + jnp.log(total) - math.log(rows * n_ref)
        )

    each(blocks, lambda h: local_stats(ITERS + 1, h, False))
    each(blocks, final_likelihood)
    for k in range(1, n_ref):
        each(
            (ITERS + 2) * blocks,
            lambda i: stat_copy(i // blocks, lax.rem(i, blocks), k).wait_send(),
        )
    for copy in outs:
        copy.wait()
    for copy in sent:
        copy.wait_send()


def per_device(nz, n_ref, images, references, initial_contrast):
    n, width = images.shape
    rows = references.shape[0]
    rb = rows // (4 * nz)
    qr, half = nz * rb, width // 2
    steps = ITERS + 2
    peers = max(n_ref - 1, 1)
    stat_copies = steps * (n // BLOCK) * peers
    copies = 6 * nz + 2 * (nz - 1) + (nz - 1) + 6 * nz
    flops = 6 * n * width * rows
    new_references, contrast, loglik = pl.pallas_call(
        functools.partial(kernel, nz, n_ref),
        out_shape=(
            pltpu.VMEM((rows, width), BF16),
            pltpu.VMEM((1, n), F32),
            pltpu.VMEM((1, n), F32),
        ),
        in_specs=[
            pl.BlockSpec(memory_space=pl.ANY),
            pl.BlockSpec(memory_space=pl.ANY),
            pl.BlockSpec(memory_space=pl.ANY),
        ],
        out_specs=(
            pl.BlockSpec(memory_space=pltpu.VMEM),
            pl.BlockSpec(memory_space=pltpu.VMEM),
            pl.BlockSpec(memory_space=pltpu.VMEM),
        ),
        scratch_shapes=[
            pltpu.VMEM((n, width), BF16),
            pltpu.VMEM((rows, width), BF16),
            pltpu.VMEM((rows, 128), F32),
            pltpu.VMEM((rows, n), F32),
            pltpu.VMEM((rows, n), BF16),
            pltpu.VMEM((4, qr, half), BF16),
            pltpu.VMEM((4, qr, half), BF16),
            pltpu.VMEM((4, qr, half), F32),
            pltpu.VMEM((2, qr, half), BF16),
            pltpu.VMEM((2, qr, half), BF16),
            pltpu.VMEM((2, max(nz - 1, 1), rb, half), BF16),
            pltpu.VMEM((2, max(nz - 1, 1), rb, half), BF16),
            pltpu.VMEM((rows, width), BF16),
            pltpu.VMEM((steps, n // BLOCK, 4, BLOCK), F32),
            pltpu.VMEM((stat_copies, 4, BLOCK), F32),
            pltpu.VMEM((8, n), F32),
            pltpu.VMEM((rows, BLOCK), F32),
            pltpu.SemaphoreType.DMA(()),
            pltpu.SemaphoreType.DMA((stat_copies,)),
            pltpu.SemaphoreType.DMA((stat_copies,)),
            pltpu.SemaphoreType.DMA((n // LANES,)),
            pltpu.SemaphoreType.DMA((4 * nz,)),
            pltpu.SemaphoreType.DMA((4 * nz,)),
            pltpu.SemaphoreType.DMA((copies,)),
            pltpu.SemaphoreType.DMA((copies,)),
        ],
        compiler_params=pltpu.CompilerParams(
            collective_id=0, has_side_effects=True, vmem_limit_bytes=56 * 1024 * 1024
        ),
        cost_estimate=pl.CostEstimate(
            flops=flops, bytes_accessed=2 * n * width, transcendentals=0
        ),
    )(images, references, initial_contrast[None, :])
    return (new_references, contrast[0], loglik[0])


def solution(mesh):
    n_img, n_ref = mesh.shape["img"], mesh.shape["ref"]
    placed = (P("img", None), P("ref", None), P("img"))
    return jax.shard_map(
        functools.partial(per_device, n_img // 4, n_ref),
        mesh=mesh,
        in_specs=placed,
        out_specs=(P("ref", None), P("img"), P("img")),
        check_vma=False,
    )
```

```python
import functools
import math

import jax
import jax.numpy as jnp
from jax import lax
from jax.experimental import pallas as pl
from jax.experimental.pallas import tpu as pltpu
from jax.sharding import PartitionSpec as P

ITERS = 3

sharpness = 2.0
prior_weight = 1.0
epsilon = 1e-06

MESH = pl.DeviceIdType.MESH
LANES = 256
BLOCK = 512
TILES = BLOCK // 128
ROWS = 64
LOG2E = math.log2(math.e)
QUADS = ((1, 0), (1, 1), (0, 1), (0, 0))
F32 = jnp.float32
BF16 = jnp.bfloat16

RATE = 46.5e3
HOP = 2.1
FAR = 0.6
BACKLOG = 0.5
STEP = 0.12
SCORE = 0.5
PIECES = 2


def plan(groups, nz, block, pieces):
    unit = block / RATE
    zs = range(1, nz)
    todo = {}
    for g in range(groups):
        for s in (0, 1):
            for j in (0, 1):
                todo["S1", g, s, j] = (2, g, 0), (), [(("s1", g, s, j), "xy"[s], unit * nz)]
            todo["S2", g, s] = (
                (1, g, 0), [("s1", g, s, 0)], [(("s2", g, s), "yx"[s], unit * nz)]
            )
        met = [("s1", g, s, 1) for s in (0, 1)] + [("s2", g, s) for s in (0, 1)]
        met_z = [("z", g, k) for k in zs]
        weight = {k: 2 * unit * (1.0 if k == 1 else 1.5) for k in zs}
        todo["Z", g] = (0, g, 0), met, [(("z", g, k), "z", weight[k]) for k in zs]
        todo["A", g] = (0, g, 0), met + met_z, [(("az", g, k), "z", weight[k]) for k in zs]
        every = []
        for k in range(nz):
            base = [("az", g, k)] if k else [("A", g)]
            outs = [[(("y", g, k, 0), "y", unit), (("x", g, k, 1), "x", unit)]]
            outs.append([(("y", g, k, 1), "y", unit), (("x", g, k, 0), "x", unit)])
            outs.append([(("fx", g, k), "x", unit), (("fy", g, k), "y", unit)])
            todo["P", g, k] = (4, g, 0), base, outs[0]
            todo["F", g, k] = (4, g, 1), [("y", g, k, 0), ("x", g, k, 1)], outs[1 + 1]
            todo["Q", g, k] = (4, g, 2), base, outs[1]
            every += [name for out in outs for name, _, _ in out]
        for p in range(pieces):
            todo["G", g, p] = (5, g, p), every, []
    clock, order, arrived = 0.0, [], {}
    free = dict.fromkeys("xyz", 0.0)
    while todo:
        best = None
        for name, (rank, waits, out) in todo.items():
            if all(wait in arrived for wait in waits):
                start = max([arrived[wait] for wait in waits], default=0.0)
                start = max([start, clock] + [free[link] - BACKLOG for _, link, _ in out])
                if best is None or (start, rank, name) < best:
                    best = (start, rank, name)
        start, _, name = best
        out = todo.pop(name)[2]
        clock = start + (SCORE if name[0] == "G" else STEP)
        arrived[name] = clock
        for message, link, length in out:
            free[link] = max(free[link], clock) + length
            arrived[message] = free[link] + HOP
            if link == "z" and message[2] > 1:
                arrived[message] += FAR
        order.append(name)
    return order


def kernel(
    nz, n_ref, im_hbm, ref_hbm, prior_hbm, newref, contrast_ref, loglik_ref,
    im, refs, norms, cross, w, snd1, rcv1, acc, snd2, rcv2, snd3, rcv3, own,
    stat_snd, stat_rcv, vecs, keep, prior_sem,
    stat_ssem, stat_rsem, im_sem, ref_sem, ssem, rsem,
):
    n, width = im.shape
    rows = refs.shape[0]
    groups = own.shape[0]
    rg = own.shape[1]
    gr = nz * rg
    qr = groups * gr
    half = width // 2
    me = lax.axis_index("img")
    rme = lax.axis_index("ref")
    x, y, z = lax.rem(me, 2), lax.rem(me // 2, 2), me // 4
    def chip(dx, dy, dz):
        zz, bit = z, 1
        while bit < nz:
            if dz & bit:
                zz = zz + bit - 2 * bit * lax.rem(z // bit, 2)
            bit *= 2
        return zz * 4 + lax.rem(y + dy, 2) * 2 + lax.rem(x + dx, 2)

    def send(src, dst, dev, kind, slot):
        pltpu.make_async_remote_copy(
            src_ref=src, dst_ref=dst, send_sem=ssem.at[kind], recv_sem=rsem.at[slot],
            device_id=dev, device_id_type=MESH,
        ).start()

    x_dev = {"img": chip(1, 0, 0)}
    y_dev = {"img": chip(0, 1, 0)}
    z_dev = [{"img": chip(0, 0, k)} for k in range(nz)]
    r_dev = [{"ref": lax.rem(rme + k, n_ref)} for k in range(n_ref)]

    barrier = pltpu.get_barrier_semaphore()
    peers = r_dev[1:] + [x_dev, y_dev] + z_dev[1:]
    for dev in peers:
        pl.semaphore_signal(barrier, inc=1, device_id=dev, device_id_type=MESH)

    ref_copies = []
    per_ref = rows // ref_sem.shape[0]
    for s in range(ref_sem.shape[0]):
        part = pl.ds(s * per_ref, per_ref)
        copy = pltpu.make_async_copy(ref_hbm.at[part], refs.at[part], ref_sem.at[s])
        copy.start()
        ref_copies.append(copy)
    for b in range(n // LANES):
        part = pl.ds(b * LANES, LANES)
        pltpu.make_async_copy(im_hbm.at[part], im.at[part], im_sem.at[b]).start()
    prior_copy = pltpu.make_async_copy(prior_hbm, vecs.at[3:4, :], prior_sem)
    prior_copy.start()

    stat_snd[...] = jnp.zeros_like(stat_snd)

    def square_sums(source, r0, count, scale):
        block = source[pl.ds(r0, count), :].astype(F32)
        total = jnp.sum(block * block, axis=1, keepdims=True) * scale
        norms[pl.ds(r0, count), :] = jnp.broadcast_to(total, (count, 128))

    for s, copy in enumerate(ref_copies):
        copy.wait()
        for r0 in range(s * per_ref, (s + 1) * per_ref, 32):
            square_sums(refs, r0, 32, 1.0)

    nt = (((1,), (1,)), ((), ()))
    nn = (((1,), (0,)), ((), ()))

    def fold(x):
        return x.reshape(x.shape[0] // 8, 8, 128)

    def spread8(x):
        return jnp.broadcast_to(x, (8, 128))

    at_chip = {
        (dx, dy, dz): chip(dx, dy, dz) * rg for dx, dy in QUADS for dz in range(nz)
    }

    def row0(g, where):
        return pl.multiple_of(g * (4 * gr) + at_chip[where], 8)

    def lanes(c0, width_=128):
        return pl.ds(pl.multiple_of(c0, 128), width_)

    def coefficients(c0, width_):
        a = vecs[0:1, lanes(c0, width_)]
        slope = (sharpness * LOG2E) * a
        bend = (0.5 * sharpness * LOG2E) * (a * a)
        tiles = range(0, width_, 128)
        return (
            [spread8(slope[:, t : t + 128]) for t in tiles],
            [spread8(bend[:, t : t + 128]) for t in tiles],
        )

    def over_rows(count, body, init):
        return lax.fori_loop(
            0, count // ROWS, lambda i, c: body(pl.multiple_of(i * ROWS, ROWS), c), init
        )

    def scores(c0):
        slope, bend = coefficients(c0, BLOCK)

        def body(r, high):
            part = pl.ds(r, ROWS)
            nrm = fold(norms[part, :])
            out = []
            for t in range(TILES):
                c = fold(cross[part, lanes(c0 + t * 128)])
                sc = slope[t][None] * c - bend[t][None] * nrm
                keep[part, t * 128 : (t + 1) * 128] = sc.reshape(ROWS, 128)
                out.append(jnp.maximum(high[t], jnp.max(sc, axis=0)))
            return tuple(out)

        high = over_rows(rows, body, (jnp.full((8, 128), -jnp.inf, F32),) * TILES)
        return [jnp.max(x, axis=0, keepdims=True) for x in high]

    def sums_of(c0, high, full):
        top = [spread8(x) for x in high]

        def body(r, carry):
            part = pl.ds(r, ROWS)
            nrm = fold(norms[part, :]) if full else None
            out = list(carry)
            for t in range(TILES):
                sc = fold(keep[part, t * 128 : (t + 1) * 128])
                e = jnp.exp2(sc - top[t][None])
                out[t] = out[t] + jnp.sum(e, axis=0)
                if full:
                    c = fold(cross[part, lanes(c0 + t * 128)])
                    out[TILES + t] = out[TILES + t] + jnp.sum(e * c, axis=0)
                    out[2 * TILES + t] = out[2 * TILES + t] + jnp.sum(e * nrm, axis=0)
            return tuple(out)

        zero = jnp.zeros((8, 128), F32)
        carry = over_rows(rows, body, (zero,) * (TILES * (3 if full else 1)))
        return [jnp.sum(x, axis=0, keepdims=True) for x in carry]

    def weigh(c0):
        slope, bend = coefficients(c0, BLOCK)
        top = [spread8(vecs[1:2, lanes(c0 + t * 128)]) for t in range(TILES)]
        gain = [spread8(vecs[2:3, lanes(c0 + t * 128)]) for t in range(TILES)]

        def body(g, carry):
            for q in range(4):
                parts = [pl.ds(row0(g, QUADS[q] + (dz,)), rg) for dz in range(nz)]
                nrm = [norms[part, :].reshape(rg // 8, 8, 128) for part in parts]
                to = pl.ds(pl.multiple_of(q * qr + g * gr, 8), gr)
                for t in range(TILES):
                    at = lanes(c0 + t * 128)
                    e = []
                    for part, norm in zip(parts, nrm):
                        c = cross[part, at].reshape(rg // 8, 8, 128)
                        sc = slope[t][None] * c - bend[t][None] * norm
                        e.append((jnp.exp2(sc - top[t][None]) * gain[t][None]).reshape(rg, 128))
                    w[to, at] = jnp.concatenate(e, axis=0).astype(BF16)
            return carry

        lax.fori_loop(0, groups, body, 0)

    blocks = n // BLOCK

    def stat_copy(it, h, k):
        slot = (it * blocks + h) * (n_ref - 1) + k - 1
        return pltpu.make_async_remote_copy(
            src_ref=stat_snd.at[it, h], dst_ref=stat_rcv.at[slot],
            send_sem=stat_ssem.at[k - 1],
            recv_sem=stat_rsem.at[(lax.rem(it, 2) * blocks + h) * (n_ref - 1) + k - 1],
            device_id=r_dev[k], device_id_type=MESH,
        )

    def local_stats(it, h, full):
        c0 = h * BLOCK
        high = scores(c0)
        sums = sums_of(c0, high, full)
        for t in range(TILES):
            at = slice(t * 128, (t + 1) * 128)
            stat_snd[it, h, 0:1, at] = high[t]
            for j in range(len(sums) // TILES):
                stat_snd[it, h, j + 1 : j + 2, at] = sums[j * TILES + t]
        for k in range(1, n_ref):
            stat_copy(it, h, k).start()

    def joint_stats(it, h, full):
        shares = [stat_snd[it, h]]
        for k in range(1, n_ref):
            stat_copy(it, h, k).wait_recv()
            shares.append(stat_rcv[(it * blocks + h) * (n_ref - 1) + k - 1])
        high = functools.reduce(jnp.maximum, [share[0:1] for share in shares])
        scales = [jnp.exp2(share[0:1] - high) for share in shares]
        sums = [
            functools.reduce(
                jnp.add, [share[j : j + 1] * sc for share, sc in zip(shares, scales)]
            )
            for j in ((1, 2, 3) if full else (1,))
        ]
        return high, sums

    def each(count, body):
        def step(i, carry):
            body(i)
            return carry

        lax.fori_loop(0, count, step, 0)


    prior_copy.wait()
    vecs[0:1, :] = vecs[3:4, :]

    def first_cross(b):
        part = pl.ds(pl.multiple_of(b * LANES, LANES), LANES)
        pltpu.make_async_copy(im_hbm.at[part], im.at[part], im_sem.at[b]).wait()
        cross[:, part] = lax.dot_general(
            refs[...], im[part, :], nt, preferred_element_type=F32
        )

    def refit(i):
        it, h = i // blocks, lax.rem(i, blocks)
        at = lanes(h * BLOCK, BLOCK)
        _, (total, along, weight) = joint_stats(it, h, True)
        vecs[0:1, at] = (along / total + prior_weight * vecs[3:4, at]) / (
            weight / total + prior_weight
        )
        local_stats(it + 1, h, True)

    def settle(h):
        at = lanes(h * BLOCK, BLOCK)
        high, (total,) = joint_stats(ITERS, h, False)
        vecs[1:2, at] = high
        vecs[2:3, at] = vecs[0:1, at] / total
        weigh(h * BLOCK)

    each(n // LANES, first_cross)
    pl.semaphore_wait(barrier, len(peers))
    each(blocks, lambda h: local_stats(0, h, True))
    each(ITERS * blocks, refit)
    each(blocks, settle)
    contrast_ref[...] = vecs[0:1, :]

    def weighted(r0s, c0, store):
        def body(b, carry):
            col = pl.multiple_of(b * LANES, LANES)
            lhs = [w[r0 : r0 + cnt, :] for r0, cnt in r0s]
            lhs = lhs[0] if len(lhs) == 1 else jnp.concatenate(lhs, axis=0)
            rhs = im[:, pl.ds(pl.multiple_of(c0 + col, LANES), LANES)]
            out = lax.dot_general(lhs, rhs, nn, preferred_element_type=F32)
            store(pl.ds(col, LANES), out[:qr], out[qr:])
            return carry

        lax.fori_loop(0, half // LANES, body, 0)

    def to_send(stream, first_is_far):
        def store(cols, lo, hi):
            far, near = (lo, hi) if first_is_far else (hi, lo)
            snd1[stream * 2, :, cols] = far.astype(BF16)
            snd1[stream * 2 + 1, :, cols] = near.astype(BF16)

        return store

    def to_keep(stream):
        def store(cols, lo, hi):
            acc[stream * 2, :, cols] = lo
            acc[stream * 2 + 1, :, cols] = hi

        return store

    hop_dev = (x_dev, y_dev)
    landed = set()
    kinds = {"s1": 0, "s2": 1, "z": 2, "az": 3, "y": 4, "x": 4, "fx": 5, "fy": 5}
    per_group = 2 + 1 + (nz - 1) + 2 * nz + 2

    def slot_of(name):
        kind, g = name[:2]
        if kind == "s1" and name[3] == 0:
            at = name[2]
        elif kind in ("s1", "s2"):
            at = 2
        elif kind == "z":
            at = 3
        elif kind == "az":
            at = 3 + name[2]
        elif kind in ("x", "y") and name[3] == (kind == "x"):
            at = 3 + nz + 2 * name[2] + (kind == "x")
        else:
            at = 3 + 3 * nz
        return g * per_group + at

    def put(name, src, dst, dev):
        send(src, dst, dev, kinds[name[0]], slot_of(name))

    def arrive(name, like):
        slot = slot_of(name)
        if slot not in landed:
            landed.add(slot)
            pltpu.make_async_copy(like, like, rsem.at[slot]).wait()

    def send1(g, s, j):
        part = pl.ds(g * gr, gr)
        put(("s1", g, s, j), snd1.at[s * 2 + j, part], rcv1.at[s * 2 + j, part], hop_dev[s])

    def send2(g, s):
        part = pl.ds(g * gr, gr)
        arrive(("s1", g, s, 0), rcv1.at[s * 2, part])
        snd2[s, part, :] = (acc[s * 2, part, :] + rcv1[s * 2, part, :].astype(F32)).astype(BF16)
        put(("s2", g, s), snd2.at[s, part], rcv2.at[s, part], hop_dev[1 - s])

    def send3(g):
        part = pl.ds(g * gr, gr)
        arrive(("s2", g, 0), rcv1.at[:, part])
        for s in (0, 1):
            total = (
                acc[s * 2 + 1, part, :]
                + rcv1[s * 2 + 1, part, :].astype(F32)
                + rcv2[s, part, :].astype(F32)
            )
            cols = slice(s * half, (s + 1) * half)
            own[g, :, cols] = total[0:rg]
            for k in range(1, nz):
                snd3[g, k - 1, :, cols] = total[k * rg : (k + 1) * rg].astype(BF16)
        for k in range(1, nz):
            put(("z", g, k), snd3.at[g, k - 1], rcv3.at[g, k - 1], z_dev[k])

    def finish(g):
        total = own[g]
        if nz > 1:
            arrive(("z", g, 1), rcv3.at[g])
        for k in range(1, nz):
            total = total + rcv3[g, k - 1].astype(F32)
        square = jnp.sum(total * total, axis=1, keepdims=True)
        mine = pl.ds(row0(g, (0, 0, 0)), rg)
        newref[mine, :] = (total * lax.rsqrt(square / width + epsilon)).astype(BF16)
        for k in range(1, nz):
            put(("az", g, k), newref.at[mine], newref.at[mine], z_dev[k])

    def piece(g, where, side):
        return newref.at[pl.ds(row0(g, where), rg), pl.ds(side * half, half)]

    def pass_on(name, g, where, side, dev):
        part = piece(g, where, side)
        put(name, part, part, dev)

    def spread_first(g, k):
        if k:
            arrive(("az", g, k), newref.at[pl.ds(row0(g, (0, 0, k)), rg)])
        pass_on(("y", g, k, 0), g, (0, 0, k), 0, y_dev)
        pass_on(("x", g, k, 1), g, (0, 0, k), 1, x_dev)

    def spread_second(g, k):
        if k:
            arrive(("az", g, k), newref.at[pl.ds(row0(g, (0, 0, k)), rg)])
        pass_on(("y", g, k, 1), g, (0, 0, k), 1, y_dev)
        pass_on(("x", g, k, 0), g, (0, 0, k), 0, x_dev)

    def forward(g, k):
        arrive(("y", g, k, 0), piece(g, (0, 1, k), 0))
        pass_on(("fx", g, k), g, (0, 1, k), 0, x_dev)
        arrive(("x", g, k, 1), piece(g, (1, 0, k), 1))
        pass_on(("fy", g, k), g, (1, 0, k), 1, y_dev)

    def score_group(g, p):
        r0, count = g * 4 * gr, 4 * gr
        if p == 0:
            arrive(("fx", g, 0), newref.at[pl.ds(r0, 2 * gr)])

            def squares(i):
                square_sums(newref, pl.multiple_of(r0 + i * 32, 32), 32, 1.0 / width)

            each(count // 32, squares)

        def body(i):
            part = pl.ds(pl.multiple_of((p * per_piece + i) * LANES, LANES), LANES)
            out = lax.dot_general(
                newref[r0 : r0 + count, :], im[part, :], nt, preferred_element_type=F32
            )
            cross[r0 : r0 + count, part] = out * width ** (-0.5)

        each(per_piece, body)

    per_piece = n // LANES // PIECES
    steps = {
        "S1": send1, "S2": send2, "Z": send3, "A": finish, "P": spread_first,
        "Q": spread_second, "F": forward, "G": score_group,
    }
    order = plan(groups, nz, rg * width, PIECES)
    first = [name for name in order if name[0] == "S1" and name[1] < 2]
    rest = [name for name in order if name not in first]

    weighted([(0, 2 * qr)], 0, to_send(0, False))
    for name in first:
        if name[2] == 0:
            send1(*name[1:])
    weighted([(qr, 2 * qr)], half, to_send(1, True))
    for name in first:
        if name[2] == 1:
            send1(*name[1:])
    weighted([(2 * qr, 2 * qr)], 0, to_keep(0))
    weighted([(0, qr), (3 * qr, qr)], half, to_keep(1))
    for name in rest:
        steps[name[0]](*name[1:])

    def final_likelihood(h):
        high, (total,) = joint_stats(ITERS + 1, h, False)
        loglik_ref[:, lanes(h * BLOCK, BLOCK)] = (
            high * math.log(2.0) + jnp.log(total) - math.log(rows * n_ref)
        )

    each(blocks, lambda h: local_stats(ITERS + 1, h, False))
    each(blocks, final_likelihood)
    def all_sent(like, sem):
        pltpu.make_async_copy(like, like, sem).wait()

    for k in range(1, n_ref):
        all_sent(stat_snd, stat_ssem.at[k - 1])
    for kind, like in enumerate((snd1, snd2, snd3, snd3)):
        all_sent(like, ssem.at[kind])
    all_sent(newref.at[pl.ds(0, 2 * qr)], ssem.at[4])
    all_sent(newref.at[pl.ds(0, qr)], ssem.at[5])


def per_device(nz, n_ref, images, references, initial_contrast):
    n, width = images.shape
    rows = references.shape[0]
    groups = max(1, min(4, rows // (32 * nz)))
    rg = rows // (4 * nz * groups)
    qr, half = nz * rg * groups, width // 2
    steps = ITERS + 2
    peers = max(n_ref - 1, 1)
    stat_copies = steps * (n // BLOCK) * peers
    arrivals = groups * (2 + 1 + (nz - 1) + 2 * nz + 2)
    flops = 6 * n * width * rows
    new_references, contrast, loglik = pl.pallas_call(
        functools.partial(kernel, nz, n_ref),
        out_shape=(
            pltpu.VMEM((rows, width), BF16),
            pltpu.VMEM((1, n), F32),
            pltpu.VMEM((1, n), F32),
        ),
        in_specs=[
            pl.BlockSpec(memory_space=pl.ANY),
            pl.BlockSpec(memory_space=pl.ANY),
            pl.BlockSpec(memory_space=pl.ANY),
        ],
        out_specs=(
            pl.BlockSpec(memory_space=pltpu.VMEM),
            pl.BlockSpec(memory_space=pltpu.VMEM),
            pl.BlockSpec(memory_space=pltpu.VMEM),
        ),
        scratch_shapes=[
            pltpu.VMEM((n, width), BF16),
            pltpu.VMEM((rows, width), BF16),
            pltpu.VMEM((rows, 128), F32),
            pltpu.VMEM((rows, n), F32),
            pltpu.VMEM((rows, n), BF16),
            pltpu.VMEM((4, qr, half), BF16),
            pltpu.VMEM((4, qr, half), BF16),
            pltpu.VMEM((4, qr, half), F32),
            pltpu.VMEM((2, qr, half), BF16),
            pltpu.VMEM((2, qr, half), BF16),
            pltpu.VMEM((groups, max(nz - 1, 1), rg, width), BF16),
            pltpu.VMEM((groups, max(nz - 1, 1), rg, width), BF16),
            pltpu.VMEM((groups, rg, width), F32),
            pltpu.VMEM((steps, n // BLOCK, 4, BLOCK), F32),
            pltpu.VMEM((stat_copies, 4, BLOCK), F32),
            pltpu.VMEM((8, n), F32),
            pltpu.VMEM((rows, BLOCK), F32),
            pltpu.SemaphoreType.DMA(()),
            pltpu.SemaphoreType.DMA((peers,)),
            pltpu.SemaphoreType.DMA((2 * (n // BLOCK) * peers,)),
            pltpu.SemaphoreType.DMA((n // LANES,)),
            pltpu.SemaphoreType.DMA((4,)),
            pltpu.SemaphoreType.DMA((6,)),
            pltpu.SemaphoreType.DMA((arrivals,)),
        ],
        compiler_params=pltpu.CompilerParams(
            collective_id=0, has_side_effects=True, vmem_limit_bytes=56 * 1024 * 1024
        ),
        cost_estimate=pl.CostEstimate(
            flops=flops, bytes_accessed=2 * n * width, transcendentals=0
        ),
    )(images, references, initial_contrast[None, :])
    return (new_references, contrast[0], loglik[0])


def solution(mesh):
    n_img, n_ref = mesh.shape["img"], mesh.shape["ref"]
    placed = (P("img", None), P("ref", None), P("img"))
    return jax.shard_map(
        functools.partial(per_device, n_img // 4, n_ref),
        mesh=mesh,
        in_specs=placed,
        out_specs=(P("ref", None), P("img"), P("img")),
        check_vma=False,
    )
```

```python
import functools
import math

import jax
import jax.numpy as jnp
from jax import lax
from jax.experimental import pallas as pl
from jax.experimental.pallas import tpu as pltpu
from jax.sharding import PartitionSpec as P

ITERS = 3

sharpness = 2.0
prior_weight = 1.0
epsilon = 1e-06

MESH = pl.DeviceIdType.MESH
LANES = 256
BLOCK = 512
TILES = BLOCK // 128
ROWS = 128
LOG2E = math.log2(math.e)
QUADS = ((1, 0), (1, 1), (0, 1), (0, 0))
F32 = jnp.float32
BF16 = jnp.bfloat16

RATE = 46.5e3
HOP = 2.1
FAR = 0.6
BACKLOG = 0.5
STEP = 0.12
SCORE = 0.6
PAIR = 2


def plan(groups, nz, block, pieces, pair):
    unit = block / RATE
    zs = range(1, nz)
    todo = {}
    for g in range(groups):
        for s in (0, 1):
            for j in (0, 1):
                todo["S1", g, s, j] = (2, g, 0), (), [(("s1", g, s, j), "xy"[s], unit * nz)]
            todo["S2", g, s] = (
                (1, g, 0), [("s1", g, s, 0)], [(("s2", g, s), "yx"[s], unit * nz)]
            )
        met = [("s1", g, s, 1) for s in (0, 1)] + [("s2", g, s) for s in (0, 1)]
        met_z = [("z", g, k) for k in zs]
        weight = {k: 2 * unit * (1.0 if k == 1 else 1.5) for k in zs}
        todo["Z", g] = (0, g, 0), met, [(("z", g, k), "z", weight[k]) for k in zs]
        todo["A", g] = (0, g, 0), met + met_z, [(("az", g, k), "z", weight[k]) for k in zs]
        every = []
        for k in range(nz):
            base = [("az", g, k)] if k else [("A", g)]
            outs = [[(("y", g, k, 0), "y", unit), (("x", g, k, 1), "x", unit)]]
            outs.append([(("y", g, k, 1), "y", unit), (("x", g, k, 0), "x", unit)])
            outs.append([(("fx", g, k), "x", unit), (("fy", g, k), "y", unit)])
            todo["P", g, k] = (4, g, 0), base, outs[0]
            todo["F", g, k] = (4, g, 1), [("y", g, k, 0), ("x", g, k, 1)], outs[1 + 1]
            todo["Q", g, k] = (4, g, 2), base, outs[1]
            every += [name for out in outs for name, _, _ in out]
        todo["N", g] = (5, g, 0), every, []
        if g % pair == pair - 1:
            for p in range(pieces):
                todo["G", g // pair, p] = (6, g, p), [("N", i) for i in range(g + 1)], []
    clock, order, arrived = 0.0, [], {}
    free = dict.fromkeys("xyz", 0.0)
    while todo:
        best = None
        for name, (rank, waits, out) in todo.items():
            if all(wait in arrived for wait in waits):
                start = max([arrived[wait] for wait in waits], default=0.0)
                start = max([start, clock] + [free[link] - BACKLOG for _, link, _ in out])
                if best is None or (start, rank, name) < best:
                    best = (start, rank, name)
        start, _, name = best
        out = todo.pop(name)[2]
        clock = start + (SCORE if name[0] == "G" else STEP)
        arrived[name] = clock
        for message, link, length in out:
            free[link] = max(free[link], clock) + length
            arrived[message] = free[link] + HOP
            if link == "z" and message[2] > 1:
                arrived[message] += FAR
        order.append(name)
    return order


def kernel(
    nz, n_ref, im_hbm, ref_hbm, prior_hbm, newref, contrast_ref, loglik_ref,
    im, refs, norms, cross, w, snd1, rcv1, acc, snd2, rcv2, snd3, rcv3, own,
    stat_snd, stat_rcv, vecs, keep, prior_sem,
    stat_ssem, stat_rsem, im_sem, ref_sem, ssem, rsem,
):
    n, width = im.shape
    rows = refs.shape[0]
    groups = own.shape[0]
    rg = own.shape[1]
    gr = nz * rg
    qr = groups * gr
    half = width // 2
    me = lax.axis_index("img")
    rme = lax.axis_index("ref")
    x, y, z = lax.rem(me, 2), lax.rem(me // 2, 2), me // 4
    def chip(dx, dy, dz):
        zz, bit = z, 1
        while bit < nz:
            if dz & bit:
                zz = zz + bit - 2 * bit * lax.rem(z // bit, 2)
            bit *= 2
        return zz * 4 + lax.rem(y + dy, 2) * 2 + lax.rem(x + dx, 2)

    def send(src, dst, dev, kind, slot):
        pltpu.make_async_remote_copy(
            src_ref=src, dst_ref=dst, send_sem=ssem.at[kind], recv_sem=rsem.at[slot],
            device_id=dev, device_id_type=MESH,
        ).start()

    x_dev = {"img": chip(1, 0, 0)}
    y_dev = {"img": chip(0, 1, 0)}
    z_dev = [{"img": chip(0, 0, k)} for k in range(nz)]
    r_dev = [{"ref": lax.rem(rme + k, n_ref)} for k in range(n_ref)]

    barrier = pltpu.get_barrier_semaphore()
    peers = r_dev[1:] + [x_dev, y_dev] + z_dev[1:]
    for dev in peers:
        pl.semaphore_signal(barrier, inc=1, device_id=dev, device_id_type=MESH)

    ref_copies = []
    per_ref = rows // ref_sem.shape[0]
    for s in range(ref_sem.shape[0]):
        part = pl.ds(s * per_ref, per_ref)
        copy = pltpu.make_async_copy(ref_hbm.at[part], refs.at[part], ref_sem.at[s])
        copy.start()
        ref_copies.append(copy)
    for b in range(n // LANES):
        part = pl.ds(b * LANES, LANES)
        pltpu.make_async_copy(im_hbm.at[part], im.at[part], im_sem.at[b]).start()
    prior_copy = pltpu.make_async_copy(prior_hbm, vecs.at[3:4, :], prior_sem)
    prior_copy.start()

    stat_snd[...] = jnp.zeros_like(stat_snd)

    def square_sums(source, r0, count, scale):
        block = source[pl.ds(r0, count), :].astype(F32)
        total = jnp.sum(block * block, axis=1, keepdims=True) * scale
        norms[pl.ds(r0, count), :] = jnp.broadcast_to(total, (count, 128))

    for s, copy in enumerate(ref_copies):
        copy.wait()
        for r0 in range(s * per_ref, (s + 1) * per_ref, 32):
            square_sums(refs, r0, 32, 1.0)

    nt = (((1,), (1,)), ((), ()))
    nn = (((1,), (0,)), ((), ()))

    def fold(x):
        return x.reshape(x.shape[0] // 8, 8, 128)

    def spread8(x):
        return jnp.broadcast_to(x, (8, 128))

    at_chip = {
        (dx, dy, dz): chip(dx, dy, dz) * rg for dx, dy in QUADS for dz in range(nz)
    }

    def row0(g, where):
        return pl.multiple_of(g * (4 * gr) + at_chip[where], 8)

    def lanes(c0, width_=128):
        return pl.ds(pl.multiple_of(c0, 128), width_)

    def coefficients(c0, width_):
        a = vecs[0:1, lanes(c0, width_)]
        slope = (sharpness * LOG2E) * a
        bend = (0.5 * sharpness * LOG2E) * (a * a)
        tiles = range(0, width_, 128)
        return (
            [spread8(slope[:, t : t + 128]) for t in tiles],
            [spread8(bend[:, t : t + 128]) for t in tiles],
        )

    def over_rows(count, body, init):
        return lax.fori_loop(
            0, count // ROWS, lambda i, c: body(pl.multiple_of(i * ROWS, ROWS), c), init
        )

    def scores(c0):
        slope, bend = coefficients(c0, BLOCK)

        def body(r, high):
            part = pl.ds(r, ROWS)
            nrm = fold(norms[part, :])
            out = []
            for t in range(TILES):
                c = fold(cross[part, lanes(c0 + t * 128)])
                sc = slope[t][None] * c - bend[t][None] * nrm
                keep[part, t * 128 : (t + 1) * 128] = sc.reshape(ROWS, 128)
                out.append(jnp.maximum(high[t], jnp.max(sc, axis=0)))
            return tuple(out)

        high = over_rows(rows, body, (jnp.full((8, 128), -jnp.inf, F32),) * TILES)
        return [jnp.max(x, axis=0, keepdims=True) for x in high]

    def sums_of(c0, high, full):
        top = [spread8(x) for x in high]

        def body(r, carry):
            part = pl.ds(r, ROWS)
            nrm = fold(norms[part, :]) if full else None
            out = list(carry)
            for t in range(TILES):
                sc = fold(keep[part, t * 128 : (t + 1) * 128])
                e = jnp.exp2(sc - top[t][None])
                out[t] = out[t] + jnp.sum(e, axis=0)
                if full:
                    c = fold(cross[part, lanes(c0 + t * 128)])
                    out[TILES + t] = out[TILES + t] + jnp.sum(e * c, axis=0)
                    out[2 * TILES + t] = out[2 * TILES + t] + jnp.sum(e * nrm, axis=0)
            return tuple(out)

        zero = jnp.zeros((8, 128), F32)
        carry = over_rows(rows, body, (zero,) * (TILES * (3 if full else 1)))
        return [jnp.sum(x, axis=0, keepdims=True) for x in carry]

    def weigh(c0):
        slope, bend = coefficients(c0, BLOCK)
        top = [spread8(vecs[1:2, lanes(c0 + t * 128)]) for t in range(TILES)]
        gain = [spread8(vecs[2:3, lanes(c0 + t * 128)]) for t in range(TILES)]

        def body(g, carry):
            for q in range(4):
                parts = [pl.ds(row0(g, QUADS[q] + (dz,)), rg) for dz in range(nz)]
                nrm = [norms[part, :].reshape(rg // 8, 8, 128) for part in parts]
                to = pl.ds(pl.multiple_of(q * qr + g * gr, 8), gr)
                for t in range(TILES):
                    at = lanes(c0 + t * 128)
                    e = []
                    for part, norm in zip(parts, nrm):
                        c = cross[part, at].reshape(rg // 8, 8, 128)
                        sc = slope[t][None] * c - bend[t][None] * norm
                        e.append((jnp.exp2(sc - top[t][None]) * gain[t][None]).reshape(rg, 128))
                    w[to, at] = jnp.concatenate(e, axis=0).astype(BF16)
            return carry

        lax.fori_loop(0, groups, body, 0)

    blocks = n // BLOCK

    def stat_copy(it, h, k):
        slot = (it * blocks + h) * (n_ref - 1) + k - 1
        return pltpu.make_async_remote_copy(
            src_ref=stat_snd.at[it, h], dst_ref=stat_rcv.at[slot],
            send_sem=stat_ssem.at[k - 1],
            recv_sem=stat_rsem.at[(lax.rem(it, 2) * blocks + h) * (n_ref - 1) + k - 1],
            device_id=r_dev[k], device_id_type=MESH,
        )

    def local_stats(it, h, full):
        c0 = h * BLOCK
        high = scores(c0)
        sums = sums_of(c0, high, full)
        for t in range(TILES):
            at = slice(t * 128, (t + 1) * 128)
            stat_snd[it, h, 0:1, at] = high[t]
            for j in range(len(sums) // TILES):
                stat_snd[it, h, j + 1 : j + 2, at] = sums[j * TILES + t]
        for k in range(1, n_ref):
            stat_copy(it, h, k).start()

    def joint_stats(it, h, full):
        shares = [stat_snd[it, h]]
        for k in range(1, n_ref):
            stat_copy(it, h, k).wait_recv()
            shares.append(stat_rcv[(it * blocks + h) * (n_ref - 1) + k - 1])
        high = functools.reduce(jnp.maximum, [share[0:1] for share in shares])
        scales = [jnp.exp2(share[0:1] - high) for share in shares]
        sums = [
            functools.reduce(
                jnp.add, [share[j : j + 1] * sc for share, sc in zip(shares, scales)]
            )
            for j in ((1, 2, 3) if full else (1,))
        ]
        return high, sums

    def each(count, body):
        def step(i, carry):
            body(i)
            return carry

        lax.fori_loop(0, count, step, 0)


    prior_copy.wait()
    vecs[0:1, :] = vecs[3:4, :]

    def first_cross(b):
        part = pl.ds(pl.multiple_of(b * LANES, LANES), LANES)
        pltpu.make_async_copy(im_hbm.at[part], im.at[part], im_sem.at[b]).wait()
        cross[:, part] = lax.dot_general(
            refs[...], im[part, :], nt, preferred_element_type=F32
        )

    def refit(i):
        it, h = i // blocks, lax.rem(i, blocks)
        at = lanes(h * BLOCK, BLOCK)
        _, (total, along, weight) = joint_stats(it, h, True)
        vecs[0:1, at] = (along / total + prior_weight * vecs[3:4, at]) / (
            weight / total + prior_weight
        )
        local_stats(it + 1, h, True)

    def settle(h):
        at = lanes(h * BLOCK, BLOCK)
        high, (total,) = joint_stats(ITERS, h, False)
        vecs[1:2, at] = high
        vecs[2:3, at] = vecs[0:1, at] / total
        weigh(h * BLOCK)

    each(n // LANES, first_cross)
    pl.semaphore_wait(barrier, len(peers))
    each(blocks, lambda h: local_stats(0, h, True))
    each(ITERS * blocks, refit)
    each(blocks, settle)
    contrast_ref[...] = vecs[0:1, :]

    def weighted(r0s, c0, store):
        def body(b, carry):
            col = pl.multiple_of(b * LANES, LANES)
            lhs = [w[r0 : r0 + cnt, :] for r0, cnt in r0s]
            lhs = lhs[0] if len(lhs) == 1 else jnp.concatenate(lhs, axis=0)
            rhs = im[:, pl.ds(pl.multiple_of(c0 + col, LANES), LANES)]
            out = lax.dot_general(lhs, rhs, nn, preferred_element_type=F32)
            store(pl.ds(col, LANES), out[:qr], out[qr:])
            return carry

        lax.fori_loop(0, half // LANES, body, 0)

    def to_send(stream, first_is_far):
        def store(cols, lo, hi):
            far, near = (lo, hi) if first_is_far else (hi, lo)
            snd1[stream * 2, :, cols] = far.astype(BF16)
            snd1[stream * 2 + 1, :, cols] = near.astype(BF16)

        return store

    def to_keep(stream):
        def store(cols, lo, hi):
            acc[stream * 2, :, cols] = lo
            acc[stream * 2 + 1, :, cols] = hi

        return store

    hop_dev = (x_dev, y_dev)
    landed = set()
    kinds = {"s1": 0, "s2": 1, "z": 2, "az": 3, "y": 4, "x": 4, "fx": 5, "fy": 5}
    per_group = 2 + 1 + (nz - 1) + 2 * nz + 2

    def slot_of(name):
        kind, g = name[:2]
        if kind == "s1" and name[3] == 0:
            at = name[2]
        elif kind in ("s1", "s2"):
            at = 2
        elif kind == "z":
            at = 3
        elif kind == "az":
            at = 3 + name[2]
        elif kind in ("x", "y") and name[3] == (kind == "x"):
            at = 3 + nz + 2 * name[2] + (kind == "x")
        else:
            at = 3 + 3 * nz
        return g * per_group + at

    def put(name, src, dst, dev):
        send(src, dst, dev, kinds[name[0]], slot_of(name))

    def arrive(name, like):
        slot = slot_of(name)
        if slot not in landed:
            landed.add(slot)
            pltpu.make_async_copy(like, like, rsem.at[slot]).wait()

    def send1(g, s, j):
        part = pl.ds(g * gr, gr)
        put(("s1", g, s, j), snd1.at[s * 2 + j, part], rcv1.at[s * 2 + j, part], hop_dev[s])

    def send2(g, s):
        part = pl.ds(g * gr, gr)
        arrive(("s1", g, s, 0), rcv1.at[s * 2, part])
        snd2[s, part, :] = (acc[s * 2, part, :] + rcv1[s * 2, part, :].astype(F32)).astype(BF16)
        put(("s2", g, s), snd2.at[s, part], rcv2.at[s, part], hop_dev[1 - s])

    def send3(g):
        part = pl.ds(g * gr, gr)
        arrive(("s2", g, 0), rcv1.at[:, part])
        for s in (0, 1):
            total = (
                acc[s * 2 + 1, part, :]
                + rcv1[s * 2 + 1, part, :].astype(F32)
                + rcv2[s, part, :].astype(F32)
            )
            cols = slice(s * half, (s + 1) * half)
            own[g, :, cols] = total[0:rg]
            for k in range(1, nz):
                snd3[g, k - 1, :, cols] = total[k * rg : (k + 1) * rg].astype(BF16)
        for k in range(1, nz):
            put(("z", g, k), snd3.at[g, k - 1], rcv3.at[g, k - 1], z_dev[k])

    def finish(g):
        total = own[g]
        if nz > 1:
            arrive(("z", g, 1), rcv3.at[g])
        for k in range(1, nz):
            total = total + rcv3[g, k - 1].astype(F32)
        square = jnp.sum(total * total, axis=1, keepdims=True)
        mine = pl.ds(row0(g, (0, 0, 0)), rg)
        newref[mine, :] = (total * lax.rsqrt(square / width + epsilon)).astype(BF16)
        for k in range(1, nz):
            put(("az", g, k), newref.at[mine], newref.at[mine], z_dev[k])

    def piece(g, where, side):
        return newref.at[pl.ds(row0(g, where), rg), pl.ds(side * half, half)]

    def pass_on(name, g, where, side, dev):
        part = piece(g, where, side)
        put(name, part, part, dev)

    def spread_first(g, k):
        if k:
            arrive(("az", g, k), newref.at[pl.ds(row0(g, (0, 0, k)), rg)])
        pass_on(("y", g, k, 0), g, (0, 0, k), 0, y_dev)
        pass_on(("x", g, k, 1), g, (0, 0, k), 1, x_dev)

    def spread_second(g, k):
        if k:
            arrive(("az", g, k), newref.at[pl.ds(row0(g, (0, 0, k)), rg)])
        pass_on(("y", g, k, 1), g, (0, 0, k), 1, y_dev)
        pass_on(("x", g, k, 0), g, (0, 0, k), 0, x_dev)

    def forward(g, k):
        arrive(("y", g, k, 0), piece(g, (0, 1, k), 0))
        pass_on(("fx", g, k), g, (0, 1, k), 0, x_dev)
        arrive(("x", g, k, 1), piece(g, (1, 0, k), 1))
        pass_on(("fy", g, k), g, (1, 0, k), 1, y_dev)

    def new_norms(g):
        arrive(("fx", g, 0), newref.at[pl.ds(g * 4 * gr, 2 * gr)])

        def squares(i):
            square_sums(newref, pl.multiple_of(g * 4 * gr + i * 64, 64), 64, 1.0 / width)

        each(4 * gr // 64, squares)

    pair = PAIR if groups % PAIR == 0 else 1
    per_block = BLOCK // LANES

    def likelihoods(c, h):
        r0, count = c * pair * 4 * gr, pair * 4 * gr
        chunks = [slice(r, min(r + ROWS, count)) for r in range(0, count, ROWS)]

        def body(i):
            c0 = h * BLOCK + i * LANES
            part = pl.ds(pl.multiple_of(c0, LANES), LANES)
            out = lax.dot_general(
                newref[r0 : r0 + count, :], im[part, :], nt, preferred_element_type=F32
            )
            slope, bend = coefficients(c0, LANES)
            slope = [x * width ** (-0.5) for x in slope]
            to = pl.ds(pl.multiple_of(i * LANES, 128), LANES)
            highs, totals = [], []
            for t in range(LANES // 128):
                sc = []
                for rr in chunks:
                    nrm = fold(norms[r0 + rr.start : r0 + rr.stop, :])
                    sc.append(
                        slope[t][None] * fold(out[rr, t * 128 : (t + 1) * 128])
                        - bend[t][None] * nrm
                    )
                high = functools.reduce(jnp.maximum, [jnp.max(x, axis=0) for x in sc])
                high = jnp.max(high, axis=0, keepdims=True)
                total = functools.reduce(
                    jnp.add, [jnp.sum(jnp.exp2(x - spread8(high)[None]), axis=0) for x in sc]
                )
                highs.append(high)
                totals.append(jnp.sum(total, axis=0, keepdims=True))
            high = jnp.concatenate(highs, axis=1)
            total = jnp.concatenate(totals, axis=1)
            if c > 0:
                before, sum_before = stat_snd[ITERS + 1, h, 0:1, to], stat_snd[ITERS + 1, h, 1:2, to]
                top = jnp.maximum(before, high)
                total = sum_before * jnp.exp2(before - top) + total * jnp.exp2(high - top)
                high = top
            stat_snd[ITERS + 1, h, 0:1, to] = high
            stat_snd[ITERS + 1, h, 1:2, to] = total

        each(per_block, body)
        if c == groups // pair - 1:
            for k in range(1, n_ref):
                stat_copy(ITERS + 1, h, k).start()

    steps = {
        "S1": send1, "S2": send2, "Z": send3, "A": finish, "P": spread_first,
        "Q": spread_second, "F": forward, "N": new_norms, "G": likelihoods,
    }
    order = plan(groups, nz, rg * width, blocks, pair)
    first = [name for name in order if name[0] == "S1" and name[1] < 2]
    rest = [name for name in order if name not in first]

    weighted([(0, 2 * qr)], 0, to_send(0, False))
    for name in first:
        if name[2] == 0:
            send1(*name[1:])
    weighted([(qr, 2 * qr)], half, to_send(1, True))
    for name in first:
        if name[2] == 1:
            send1(*name[1:])
    weighted([(2 * qr, 2 * qr)], 0, to_keep(0))
    weighted([(0, qr), (3 * qr, qr)], half, to_keep(1))
    for name in rest:
        steps[name[0]](*name[1:])

    def final_likelihood(h):
        high, (total,) = joint_stats(ITERS + 1, h, False)
        loglik_ref[:, lanes(h * BLOCK, BLOCK)] = (
            high * math.log(2.0) + jnp.log(total) - math.log(rows * n_ref)
        )

    each(blocks, final_likelihood)
    def all_sent(like, sem):
        pltpu.make_async_copy(like, like, sem).wait()

    for k in range(1, n_ref):
        all_sent(stat_snd, stat_ssem.at[k - 1])
    for kind, like in enumerate((snd1, snd2, snd3, snd3)):
        all_sent(like, ssem.at[kind])
    all_sent(newref.at[pl.ds(0, 2 * qr)], ssem.at[4])
    all_sent(newref.at[pl.ds(0, qr)], ssem.at[5])


def put_out(new_vmem, contrast_vmem, loglik_vmem, new_hbm, contrast_hbm, loglik_hbm, sem):
    pairs = ((new_vmem, new_hbm), (contrast_vmem, contrast_hbm), (loglik_vmem, loglik_hbm))
    copies = [pltpu.make_async_copy(a, b, sem.at[i]) for i, (a, b) in enumerate(pairs)]
    for copy in copies:
        copy.start()
    for copy in copies:
        copy.wait()


def per_device(nz, n_ref, images, references, initial_contrast):
    n, width = images.shape
    rows = references.shape[0]
    groups = max(1, min(4, rows // (32 * nz)))
    rg = rows // (4 * nz * groups)
    qr, half = nz * rg * groups, width // 2
    steps = ITERS + 2
    peers = max(n_ref - 1, 1)
    stat_copies = steps * (n // BLOCK) * peers
    arrivals = groups * (2 + 1 + (nz - 1) + 2 * nz + 2)
    flops = 6 * n * width * rows
    new_references, contrast, loglik = pl.pallas_call(
        functools.partial(kernel, nz, n_ref),
        out_shape=(
            pltpu.VMEM((rows, width), BF16),
            pltpu.VMEM((1, n), F32),
            pltpu.VMEM((1, n), F32),
        ),
        in_specs=[
            pl.BlockSpec(memory_space=pl.ANY),
            pl.BlockSpec(memory_space=pl.ANY),
            pl.BlockSpec(memory_space=pl.ANY),
        ],
        out_specs=(
            pl.BlockSpec(memory_space=pltpu.VMEM),
            pl.BlockSpec(memory_space=pltpu.VMEM),
            pl.BlockSpec(memory_space=pltpu.VMEM),
        ),
        scratch_shapes=[
            pltpu.VMEM((n, width), BF16),
            pltpu.VMEM((rows, width), BF16),
            pltpu.VMEM((rows, 128), F32),
            pltpu.VMEM((rows, n), F32),
            pltpu.VMEM((rows, n), BF16),
            pltpu.VMEM((4, qr, half), BF16),
            pltpu.VMEM((4, qr, half), BF16),
            pltpu.VMEM((4, qr, half), F32),
            pltpu.VMEM((2, qr, half), BF16),
            pltpu.VMEM((2, qr, half), BF16),
            pltpu.VMEM((groups, max(nz - 1, 1), rg, width), BF16),
            pltpu.VMEM((groups, max(nz - 1, 1), rg, width), BF16),
            pltpu.VMEM((groups, rg, width), F32),
            pltpu.VMEM((steps, n // BLOCK, 4, BLOCK), F32),
            pltpu.VMEM((stat_copies, 4, BLOCK), F32),
            pltpu.VMEM((8, n), F32),
            pltpu.VMEM((rows, BLOCK), F32),
            pltpu.SemaphoreType.DMA(()),
            pltpu.SemaphoreType.DMA((peers,)),
            pltpu.SemaphoreType.DMA((2 * (n // BLOCK) * peers,)),
            pltpu.SemaphoreType.DMA((n // LANES,)),
            pltpu.SemaphoreType.DMA((4,)),
            pltpu.SemaphoreType.DMA((6,)),
            pltpu.SemaphoreType.DMA((arrivals,)),
        ],
        compiler_params=pltpu.CompilerParams(
            collective_id=0, has_side_effects=True, vmem_limit_bytes=56 * 1024 * 1024
        ),
        cost_estimate=pl.CostEstimate(
            flops=flops, bytes_accessed=2 * n * width, transcendentals=0
        ),
    )(images, references, initial_contrast[None, :])
    anywhere = pl.BlockSpec(memory_space=pl.ANY)
    new_references, contrast, loglik = pl.pallas_call(
        put_out,
        out_shape=(
            jax.ShapeDtypeStruct((rows, width), BF16),
            jax.ShapeDtypeStruct((1, n), F32),
            jax.ShapeDtypeStruct((1, n), F32),
        ),
        in_specs=[pl.BlockSpec(memory_space=pltpu.VMEM)] * 3,
        out_specs=(anywhere,) * 3,
        scratch_shapes=[pltpu.SemaphoreType.DMA((3,))],
    )(*(pltpu.with_memory_space_constraint(v, pltpu.VMEM) for v in (new_references, contrast, loglik)))
    return (new_references, contrast[0], loglik[0])


def solution(mesh):
    n_img, n_ref = mesh.shape["img"], mesh.shape["ref"]
    placed = (P("img", None), P("ref", None), P("img"))
    return jax.shard_map(
        functools.partial(per_device, n_img // 4, n_ref),
        mesh=mesh,
        in_specs=placed,
        out_specs=(P("ref", None), P("img"), P("img")),
        check_vma=False,
    )
```

```python
import functools
import math

import jax
import jax.numpy as jnp
from jax import lax
from jax.experimental import pallas as pl
from jax.experimental.pallas import tpu as pltpu
from jax.sharding import PartitionSpec as P

ITERS = 3

sharpness = 2.0
prior_weight = 1.0
epsilon = 1e-06

MESH = pl.DeviceIdType.MESH
LANES = 256
BLOCK = 512
TILES = BLOCK // 128
ROWS = 128
LOG2E = math.log2(math.e)
QUADS = ((1, 0), (1, 1), (0, 1), (0, 0))
F32 = jnp.float32
BF16 = jnp.bfloat16

RATE = 48e3
HOP = 3.0
FAR = 0.3
BACKLOG = 0.7
EAGER = 1
DIRECT = 1
COST = {"W": 1.27, "S2": 0.04, "Z": 0.06, "A": 0.11, "N": 0.2, "G": 1.1}
PAIR = 2


def low(k):
    return k & -k


def plan(groups, nz, block, pieces, pair):
    unit = block / RATE
    zs = range(1, nz)
    bits = [1 << j for j in range(nz.bit_length() - 1)]
    todo = {("W", s): ((-1, s, 0), [("W", s - 1)] if s else [], []) for s in range(4)}
    for g in range(groups):
        for s in (0, 1):
            for j in (0, 1):
                todo["S1", g, s, j] = (
                    (-2 if g < EAGER else 2, g, j), [("W", s)],
                    [(("s1", g, s, j), "xy"[s], unit * nz)],
                )
            todo["S2", g, s] = (
                (1, g, 0), [("s1", g, s, 0), ("W", 3)], [(("s2", g, s), "yx"[s], unit * nz)]
            )
        met = [("s1", g, s, 1) for s in (0, 1)] + [("s2", g, s) for s in (0, 1)]
        met_z = [("z", g, k) for k in zs]
        if g < DIRECT:
            weight = {k: 2 * unit * (1.0 if k == 1 else 1.5) for k in zs}
            todo["Z", g, 0] = (0, g, 0), met, [(("z", g, k), "z", weight[k]) for k in zs]
            az = zs
        else:
            weight = dict.fromkeys(zs, 2 * unit)
            for bit in bits:
                inner = [("z", g, k) for k in zs if low(k) < bit and k > low(k)]
                todo["Z", g, bit] = (
                    (0, g, bit), met + inner,
                    [(("z", g, k), "z", weight[k]) for k in zs if low(k) == bit][::-1],
                )
            az = bits[::-1]
            for k in zs:
                if low(k) > 1:
                    todo["T", g, k] = (
                        (0, g, 0), [("az", g, k)],
                        [(("az", g, k + b), "z", weight[k]) for b in az if b < low(k)],
                    )
        todo["A", g] = (0, g, 0), met + met_z, [(("az", g, k), "z", weight[k]) for k in az]
        every = []
        for k in range(nz):
            base = [("az", g, k)] if k else [("A", g)]
            outs = [[(("y", g, k, 0), "y", unit), (("x", g, k, 1), "x", unit)]]
            outs.append([(("y", g, k, 1), "y", unit), (("x", g, k, 0), "x", unit)])
            outs.append([(("fx", g, k), "x", unit), (("fy", g, k), "y", unit)])
            todo["P", g, k] = (4, g, 0), base, outs[0]
            todo["F", g, k] = (4, g, 1), [("y", g, k, 0), ("x", g, k, 1)], outs[1 + 1]
            todo["Q", g, k] = (4, g, 2), base, outs[1]
            every += [name for out in outs for name, _, _ in out]
        todo["N", g] = (5, g, 0), every, []
        if g % pair == pair - 1:
            for p in range(pieces):
                todo["G", g // pair, p] = (6, g, p), [("N", i) for i in range(g + 1)], []
    clock, order, arrived = 0.0, [], {}
    free = dict.fromkeys("xyz", 0.0)
    while todo:
        best = None
        for name, (rank, waits, out) in todo.items():
            if all(wait in arrived for wait in waits):
                start = max([arrived[wait] for wait in waits], default=0.0)
                start = max(start, clock)
                if rank[0] > -2:
                    start = max([start] + [free[link] - BACKLOG for _, link, _ in out])
                if best is None or (start, rank, name) < best:
                    best = (start, rank, name)
        start, _, name = best
        out = todo.pop(name)[2]
        clock = start + COST.get(name[0], 0.02)
        arrived[name] = clock
        for message, link, length in out:
            free[link] = max(free[link], clock) + length
            arrived[message] = free[link] + HOP
            if link == "z":
                far = message[2] if message[1] < DIRECT else low(message[2])
                arrived[message] += FAR if far > 1 else 0.0
        order.append(name)
    return order


def kernel(
    nz, n_ref, im_hbm, ref_hbm, prior_hbm, newref, contrast_ref, loglik_ref,
    im, refs, norms, cross, w, snd1, rcv1, acc, snd2, rcv2, snd3, rcv3, own,
    stat_snd, stat_rcv, vecs, keep, prior_sem,
    stat_ssem, stat_rsem, im_sem, ref_sem, ssem, rsem,
):
    n, width = im.shape
    rows = refs.shape[0]
    groups = own.shape[0]
    rg = own.shape[2]
    gr = nz * rg
    qr = groups * gr
    half = width // 2
    me = lax.axis_index("img")
    rme = lax.axis_index("ref")
    x, y, z = lax.rem(me, 2), lax.rem(me // 2, 2), me // 4
    def chip(dx, dy, dz):
        zz, bit = z, 1
        while bit < nz:
            if dz & bit:
                zz = zz + bit - 2 * bit * lax.rem(z // bit, 2)
            bit *= 2
        return zz * 4 + lax.rem(y + dy, 2) * 2 + lax.rem(x + dx, 2)

    def send(src, dst, dev, kind, slot):
        pltpu.make_async_remote_copy(
            src_ref=src, dst_ref=dst, send_sem=ssem.at[kind], recv_sem=rsem.at[slot],
            device_id=dev, device_id_type=MESH,
        ).start()

    x_dev = {"img": chip(1, 0, 0)}
    y_dev = {"img": chip(0, 1, 0)}
    z_dev = [{"img": chip(0, 0, k)} for k in range(nz)]
    r_dev = [{"ref": lax.rem(rme + k, n_ref)} for k in range(n_ref)]

    barrier = pltpu.get_barrier_semaphore()
    peers = r_dev[1:] + [x_dev, y_dev] + z_dev[1:]
    for dev in peers:
        pl.semaphore_signal(barrier, inc=1, device_id=dev, device_id_type=MESH)

    ref_copies = []
    per_ref = rows // ref_sem.shape[0]
    for s in range(ref_sem.shape[0]):
        part = pl.ds(s * per_ref, per_ref)
        copy = pltpu.make_async_copy(ref_hbm.at[part], refs.at[part], ref_sem.at[s])
        copy.start()
        ref_copies.append(copy)
    for b in range(n // LANES):
        part = pl.ds(b * LANES, LANES)
        pltpu.make_async_copy(im_hbm.at[part], im.at[part], im_sem.at[b]).start()
    prior_copy = pltpu.make_async_copy(prior_hbm, vecs.at[3:4, :], prior_sem)
    prior_copy.start()

    stat_snd[...] = jnp.zeros_like(stat_snd)

    def square_sums(source, r0, count, scale):
        block = source[pl.ds(r0, count), :].astype(F32)
        total = jnp.sum(block * block, axis=1, keepdims=True) * scale
        norms[pl.ds(r0, count), :] = jnp.broadcast_to(total, (count, 128))

    for s, copy in enumerate(ref_copies):
        copy.wait()
        for r0 in range(s * per_ref, (s + 1) * per_ref, 32):
            square_sums(refs, r0, 32, 1.0)

    nt = (((1,), (1,)), ((), ()))
    nn = (((1,), (0,)), ((), ()))

    def fold(x):
        return x.reshape(x.shape[0] // 8, 8, 128)

    def spread8(x):
        return jnp.broadcast_to(x, (8, 128))

    at_chip = {
        (dx, dy, dz): chip(dx, dy, dz) * rg for dx, dy in QUADS for dz in range(nz)
    }

    def row0(g, where):
        return pl.multiple_of(g * (4 * gr) + at_chip[where], 8)

    def lanes(c0, width_=128):
        return pl.ds(pl.multiple_of(c0, 128), width_)

    def coefficients(c0, width_):
        a = vecs[0:1, lanes(c0, width_)]
        slope = (sharpness * LOG2E) * a
        bend = (0.5 * sharpness * LOG2E) * (a * a)
        tiles = range(0, width_, 128)
        return (
            [spread8(slope[:, t : t + 128]) for t in tiles],
            [spread8(bend[:, t : t + 128]) for t in tiles],
        )

    def over_rows(count, body, init):
        return lax.fori_loop(
            0, count // ROWS, lambda i, c: body(pl.multiple_of(i * ROWS, ROWS), c), init
        )

    def scores(c0):
        slope, bend = coefficients(c0, BLOCK)

        def body(r, high):
            part = pl.ds(r, ROWS)
            nrm = fold(norms[part, :])
            out = []
            for t in range(TILES):
                c = fold(cross[part, lanes(c0 + t * 128)])
                sc = slope[t][None] * c - bend[t][None] * nrm
                keep[part, t * 128 : (t + 1) * 128] = sc.reshape(ROWS, 128)
                out.append(jnp.maximum(high[t], jnp.max(sc, axis=0)))
            return tuple(out)

        high = over_rows(rows, body, (jnp.full((8, 128), -jnp.inf, F32),) * TILES)
        return [jnp.max(x, axis=0, keepdims=True) for x in high]

    def sums_of(c0, high, full):
        top = [spread8(x) for x in high]

        def body(r, carry):
            part = pl.ds(r, ROWS)
            nrm = fold(norms[part, :]) if full else None
            out = list(carry)
            for t in range(TILES):
                sc = fold(keep[part, t * 128 : (t + 1) * 128])
                e = jnp.exp2(sc - top[t][None])
                out[t] = out[t] + jnp.sum(e, axis=0)
                if full:
                    c = fold(cross[part, lanes(c0 + t * 128)])
                    out[TILES + t] = out[TILES + t] + jnp.sum(e * c, axis=0)
                    out[2 * TILES + t] = out[2 * TILES + t] + jnp.sum(e * nrm, axis=0)
            return tuple(out)

        zero = jnp.zeros((8, 128), F32)
        carry = over_rows(rows, body, (zero,) * (TILES * (3 if full else 1)))
        return [jnp.sum(x, axis=0, keepdims=True) for x in carry]

    def weigh(c0):
        slope, bend = coefficients(c0, BLOCK)
        top = [spread8(vecs[1:2, lanes(c0 + t * 128)]) for t in range(TILES)]
        gain = [spread8(vecs[2:3, lanes(c0 + t * 128)]) for t in range(TILES)]

        def body(g, carry):
            for q in range(4):
                parts = [pl.ds(row0(g, QUADS[q] + (dz,)), rg) for dz in range(nz)]
                nrm = [norms[part, :].reshape(rg // 8, 8, 128) for part in parts]
                to = pl.ds(pl.multiple_of(q * qr + g * gr, 8), gr)
                for t in range(TILES):
                    at = lanes(c0 + t * 128)
                    e = []
                    for part, norm in zip(parts, nrm):
                        c = cross[part, at].reshape(rg // 8, 8, 128)
                        sc = slope[t][None] * c - bend[t][None] * norm
                        e.append((jnp.exp2(sc - top[t][None]) * gain[t][None]).reshape(rg, 128))
                    w[to, at] = jnp.concatenate(e, axis=0).astype(BF16)
            return carry

        lax.fori_loop(0, groups, body, 0)

    blocks = n // BLOCK

    def stat_copy(it, h, k):
        slot = (it * blocks + h) * (n_ref - 1) + k - 1
        return pltpu.make_async_remote_copy(
            src_ref=stat_snd.at[it, h], dst_ref=stat_rcv.at[slot],
            send_sem=stat_ssem.at[k - 1],
            recv_sem=stat_rsem.at[(lax.rem(it, 2) * blocks + h) * (n_ref - 1) + k - 1],
            device_id=r_dev[k], device_id_type=MESH,
        )

    def local_stats(it, h, full):
        c0 = h * BLOCK
        high = scores(c0)
        sums = sums_of(c0, high, full)
        for t in range(TILES):
            at = slice(t * 128, (t + 1) * 128)
            stat_snd[it, h, 0:1, at] = high[t]
            for j in range(len(sums) // TILES):
                stat_snd[it, h, j + 1 : j + 2, at] = sums[j * TILES + t]
        for k in range(1, n_ref):
            stat_copy(it, h, k).start()

    def joint_stats(it, h, full):
        shares = [stat_snd[it, h]]
        for k in range(1, n_ref):
            stat_copy(it, h, k).wait_recv()
            shares.append(stat_rcv[(it * blocks + h) * (n_ref - 1) + k - 1])
        high = functools.reduce(jnp.maximum, [share[0:1] for share in shares])
        scales = [jnp.exp2(share[0:1] - high) for share in shares]
        sums = [
            functools.reduce(
                jnp.add, [share[j : j + 1] * sc for share, sc in zip(shares, scales)]
            )
            for j in ((1, 2, 3) if full else (1,))
        ]
        return high, sums

    def each(count, body):
        def step(i, carry):
            body(i)
            return carry

        lax.fori_loop(0, count, step, 0)


    prior_copy.wait()
    vecs[0:1, :] = vecs[3:4, :]

    def first_cross(b):
        part = pl.ds(pl.multiple_of(b * LANES, LANES), LANES)
        pltpu.make_async_copy(im_hbm.at[part], im.at[part], im_sem.at[b]).wait()
        cross[:, part] = lax.dot_general(
            refs[...], im[part, :], nt, preferred_element_type=F32
        )

    def refit(i):
        it, h = i // blocks, lax.rem(i, blocks)
        at = lanes(h * BLOCK, BLOCK)
        _, (total, along, weight) = joint_stats(it, h, True)
        vecs[0:1, at] = (along / total + prior_weight * vecs[3:4, at]) / (
            weight / total + prior_weight
        )
        local_stats(it + 1, h, True)

    def settle(h):
        at = lanes(h * BLOCK, BLOCK)
        high, (total,) = joint_stats(ITERS, h, False)
        vecs[1:2, at] = high
        vecs[2:3, at] = vecs[0:1, at] / total
        weigh(h * BLOCK)

    each(n // LANES, first_cross)
    pl.semaphore_wait(barrier, len(peers))
    each(blocks, lambda h: local_stats(0, h, True))
    each(ITERS * blocks, refit)
    each(blocks, settle)
    contrast_ref[...] = vecs[0:1, :]

    def weighted(r0s, c0, store):
        def body(b, carry):
            col = pl.multiple_of(b * LANES, LANES)
            lhs = [w[r0 : r0 + cnt, :] for r0, cnt in r0s]
            lhs = lhs[0] if len(lhs) == 1 else jnp.concatenate(lhs, axis=0)
            rhs = im[:, pl.ds(pl.multiple_of(c0 + col, LANES), LANES)]
            out = lax.dot_general(lhs, rhs, nn, preferred_element_type=F32)
            store(pl.ds(col, LANES), out[:qr], out[qr:])
            return carry

        lax.fori_loop(0, half // LANES, body, 0)

    def to_send(stream, first_is_far):
        def store(cols, lo, hi):
            far, near = (lo, hi) if first_is_far else (hi, lo)
            snd1[stream * 2, :, cols] = far.astype(BF16)
            snd1[stream * 2 + 1, :, cols] = near.astype(BF16)

        return store

    def to_keep(stream):
        def store(cols, lo, hi):
            acc[stream * 2, :, cols] = lo
            acc[stream * 2 + 1, :, cols] = hi

        return store

    hop_dev = (x_dev, y_dev)
    landed = set()
    kinds = {"s1": 0, "s2": 1, "z": 2, "az": 3, "y": 4, "x": 4, "fx": 5, "fy": 5}
    per_group = 4 * nz + 2
    bits = [1 << j for j in range(nz.bit_length() - 1)]

    def slot_of(name):
        kind, g = name[:2]
        if kind == "s1" and name[3] == 0:
            at = name[2]
        elif kind in ("s1", "s2"):
            at = 2
        elif kind == "z":
            at = 2 + name[2]
        elif kind == "az":
            at = 1 + nz + name[2]
        elif kind in ("x", "y") and name[3] == (kind == "x"):
            at = 1 + 2 * nz + 2 * name[2] + (kind == "x")
        else:
            at = 1 + 4 * nz
        return g * per_group + at

    def put(name, src, dst, dev):
        send(src, dst, dev, kinds[name[0]], slot_of(name))

    def arrive(name, like):
        slot = slot_of(name)
        if slot not in landed:
            landed.add(slot)
            pltpu.make_async_copy(like, like, rsem.at[slot]).wait()

    def send1(g, s, j):
        part = pl.ds(g * gr, gr)
        put(("s1", g, s, j), snd1.at[s * 2 + j, part], rcv1.at[s * 2 + j, part], hop_dev[s])

    def send2(g, s):
        part = pl.ds(g * gr, gr)
        arrive(("s1", g, s, 0), rcv1.at[s * 2, part])
        snd2[s, part, :] = (acc[s * 2, part, :] + rcv1[s * 2, part, :].astype(F32)).astype(BF16)
        put(("s2", g, s), snd2.at[s, part], rcv2.at[s, part], hop_dev[1 - s])

    def send3(g, bit):
        part = pl.ds(g * gr, gr)
        if bit < 2:
            arrive(("s2", g, 0), rcv1.at[:, part])
            for s in (0, 1):
                total = (
                    acc[s * 2 + 1, part, :]
                    + rcv1[s * 2 + 1, part, :].astype(F32)
                    + rcv2[s, part, :].astype(F32)
                )
                cols = slice(s * half, (s + 1) * half)
                for k in range(nz):
                    block = total[k * rg : (k + 1) * rg]
                    if k and (bit == 0 or low(k) == 1):
                        snd3[g, k - 1, :, cols] = block.astype(BF16)
                    else:
                        own[g, k, :, cols] = block
        for k in range(nz - 1, 0, -1):
            if bit and low(k) != bit:
                continue
            if bit > 1:
                total = own[g, k]
                for c in bits:
                    if c < bit:
                        arrive(("z", g, k + c), rcv3.at[g, 0])
                        total = total + rcv3[g, k + c - 1].astype(F32)
                snd3[g, k - 1] = total.astype(BF16)
            put(("z", g, k), snd3.at[g, k - 1], rcv3.at[g, k - 1], z_dev[bit or k])

    def finish(g):
        total = own[g, 0]
        for k in range(1, nz) if g < DIRECT else bits:
            arrive(("z", g, k), rcv3.at[g, 0])
            total = total + rcv3[g, k - 1].astype(F32)
        square = jnp.sum(total * total, axis=1, keepdims=True)
        mine = pl.ds(row0(g, (0, 0, 0)), rg)
        newref[mine, :] = (total * lax.rsqrt(square / width + epsilon)).astype(BF16)
        for k in range(1, nz) if g < DIRECT else bits[::-1]:
            put(("az", g, k), newref.at[mine], newref.at[mine], z_dev[k])

    def relay(g, k):
        part = newref.at[pl.ds(row0(g, (0, 0, k)), rg)]
        arrive(("az", g, k), part)
        for bit in bits[::-1]:
            if bit < low(k):
                put(("az", g, k + bit), part, part, z_dev[bit])

    def piece(g, where, side):
        return newref.at[pl.ds(row0(g, where), rg), pl.ds(side * half, half)]

    def pass_on(name, g, where, side, dev):
        part = piece(g, where, side)
        put(name, part, part, dev)

    def spread_first(g, k):
        if k:
            arrive(("az", g, k), newref.at[pl.ds(row0(g, (0, 0, k)), rg)])
        pass_on(("y", g, k, 0), g, (0, 0, k), 0, y_dev)
        pass_on(("x", g, k, 1), g, (0, 0, k), 1, x_dev)

    def spread_second(g, k):
        if k:
            arrive(("az", g, k), newref.at[pl.ds(row0(g, (0, 0, k)), rg)])
        pass_on(("y", g, k, 1), g, (0, 0, k), 1, y_dev)
        pass_on(("x", g, k, 0), g, (0, 0, k), 0, x_dev)

    def forward(g, k):
        arrive(("y", g, k, 0), piece(g, (0, 1, k), 0))
        pass_on(("fx", g, k), g, (0, 1, k), 0, x_dev)
        arrive(("x", g, k, 1), piece(g, (1, 0, k), 1))
        pass_on(("fy", g, k), g, (1, 0, k), 1, y_dev)

    def new_norms(g):
        arrive(("fx", g, 0), newref.at[pl.ds(g * 4 * gr, 2 * gr)])

        def squares(i):
            square_sums(newref, pl.multiple_of(g * 4 * gr + i * 64, 64), 64, 1.0 / width)

        each(4 * gr // 64, squares)

    pair = PAIR if groups % PAIR == 0 else 1
    per_block = BLOCK // LANES

    def likelihoods(c, h):
        r0, count = c * pair * 4 * gr, pair * 4 * gr
        chunks = [slice(r, min(r + ROWS, count)) for r in range(0, count, ROWS)]

        def body(i):
            c0 = h * BLOCK + i * LANES
            part = pl.ds(pl.multiple_of(c0, LANES), LANES)
            out = lax.dot_general(
                newref[r0 : r0 + count, :], im[part, :], nt, preferred_element_type=F32
            )
            slope, bend = coefficients(c0, LANES)
            slope = [x * width ** (-0.5) for x in slope]
            to = pl.ds(pl.multiple_of(i * LANES, 128), LANES)
            highs, totals = [], []
            for t in range(LANES // 128):
                sc = []
                for rr in chunks:
                    nrm = fold(norms[r0 + rr.start : r0 + rr.stop, :])
                    sc.append(
                        slope[t][None] * fold(out[rr, t * 128 : (t + 1) * 128])
                        - bend[t][None] * nrm
                    )
                high = functools.reduce(jnp.maximum, [jnp.max(x, axis=0) for x in sc])
                high = jnp.max(high, axis=0, keepdims=True)
                total = functools.reduce(
                    jnp.add, [jnp.sum(jnp.exp2(x - spread8(high)[None]), axis=0) for x in sc]
                )
                highs.append(high)
                totals.append(jnp.sum(total, axis=0, keepdims=True))
            high = jnp.concatenate(highs, axis=1)
            total = jnp.concatenate(totals, axis=1)
            if c > 0:
                before, sum_before = stat_snd[ITERS + 1, h, 0:1, to], stat_snd[ITERS + 1, h, 1:2, to]
                top = jnp.maximum(before, high)
                total = sum_before * jnp.exp2(before - top) + total * jnp.exp2(high - top)
                high = top
            stat_snd[ITERS + 1, h, 0:1, to] = high
            stat_snd[ITERS + 1, h, 1:2, to] = total

        each(per_block, body)
        if c == groups // pair - 1:
            for k in range(1, n_ref):
                stat_copy(ITERS + 1, h, k).start()

    steps = {
        "S1": send1, "S2": send2, "Z": send3, "A": finish, "T": relay, "P": spread_first,
        "Q": spread_second, "F": forward, "N": new_norms, "G": likelihoods,
    }
    order = plan(groups, nz, rg * width, blocks, pair)
    sums = (
        functools.partial(weighted, [(0, 2 * qr)], 0, to_send(0, False)),
        functools.partial(weighted, [(qr, 2 * qr)], half, to_send(1, True)),
        functools.partial(weighted, [(2 * qr, 2 * qr)], 0, to_keep(0)),
        functools.partial(weighted, [(0, qr), (3 * qr, qr)], half, to_keep(1)),
    )
    steps["W"] = lambda part: sums[part]()
    rest = order
    for name in rest:
        steps[name[0]](*name[1:])

    def final_likelihood(h):
        high, (total,) = joint_stats(ITERS + 1, h, False)
        loglik_ref[:, lanes(h * BLOCK, BLOCK)] = (
            high * math.log(2.0) + jnp.log(total) - math.log(rows * n_ref)
        )

    each(blocks, final_likelihood)
    def all_sent(like, sem):
        pltpu.make_async_copy(like, like, sem).wait()

    for k in range(1, n_ref):
        all_sent(stat_snd, stat_ssem.at[k - 1])
    for kind, like in enumerate((snd1, snd2, snd3, snd3)):
        all_sent(like, ssem.at[kind])
    all_sent(newref.at[pl.ds(0, 2 * qr)], ssem.at[4])
    all_sent(newref.at[pl.ds(0, qr)], ssem.at[5])


def put_out(new_vmem, contrast_vmem, loglik_vmem, new_hbm, contrast_hbm, loglik_hbm, sem):
    pairs = ((new_vmem, new_hbm), (contrast_vmem, contrast_hbm), (loglik_vmem, loglik_hbm))
    copies = [pltpu.make_async_copy(a, b, sem.at[i]) for i, (a, b) in enumerate(pairs)]
    for copy in copies:
        copy.start()
    for copy in copies:
        copy.wait()


def per_device(nz, n_ref, images, references, initial_contrast):
    n, width = images.shape
    rows = references.shape[0]
    groups = max(1, min(4, rows // (32 * nz)))
    rg = rows // (4 * nz * groups)
    qr, half = nz * rg * groups, width // 2
    steps = ITERS + 2
    peers = max(n_ref - 1, 1)
    stat_copies = steps * (n // BLOCK) * peers
    arrivals = groups * (4 * nz + 2)
    flops = 6 * n * width * rows
    new_references, contrast, loglik = pl.pallas_call(
        functools.partial(kernel, nz, n_ref),
        out_shape=(
            pltpu.VMEM((rows, width), BF16),
            pltpu.VMEM((1, n), F32),
            pltpu.VMEM((1, n), F32),
        ),
        in_specs=[
            pl.BlockSpec(memory_space=pl.ANY),
            pl.BlockSpec(memory_space=pl.ANY),
            pl.BlockSpec(memory_space=pl.ANY),
        ],
        out_specs=(
            pl.BlockSpec(memory_space=pltpu.VMEM),
            pl.BlockSpec(memory_space=pltpu.VMEM),
            pl.BlockSpec(memory_space=pltpu.VMEM),
        ),
        scratch_shapes=[
            pltpu.VMEM((n, width), BF16),
            pltpu.VMEM((rows, width), BF16),
            pltpu.VMEM((rows, 128), F32),
            pltpu.VMEM((rows, n), F32),
            pltpu.VMEM((rows, n), BF16),
            pltpu.VMEM((4, qr, half), BF16),
            pltpu.VMEM((4, qr, half), BF16),
            pltpu.VMEM((4, qr, half), F32),
            pltpu.VMEM((2, qr, half), BF16),
            pltpu.VMEM((2, qr, half), BF16),
            pltpu.VMEM((groups, max(nz - 1, 1), rg, width), BF16),
            pltpu.VMEM((groups, max(nz - 1, 1), rg, width), BF16),
            pltpu.VMEM((groups, nz, rg, width), F32),
            pltpu.VMEM((steps, n // BLOCK, 4, BLOCK), F32),
            pltpu.VMEM((stat_copies, 4, BLOCK), F32),
            pltpu.VMEM((8, n), F32),
            pltpu.VMEM((rows, BLOCK), F32),
            pltpu.SemaphoreType.DMA(()),
            pltpu.SemaphoreType.DMA((peers,)),
            pltpu.SemaphoreType.DMA((2 * (n // BLOCK) * peers,)),
            pltpu.SemaphoreType.DMA((n // LANES,)),
            pltpu.SemaphoreType.DMA((4,)),
            pltpu.SemaphoreType.DMA((6,)),
            pltpu.SemaphoreType.DMA((arrivals,)),
        ],
        compiler_params=pltpu.CompilerParams(
            collective_id=0, has_side_effects=True, vmem_limit_bytes=56 * 1024 * 1024
        ),
        cost_estimate=pl.CostEstimate(
            flops=flops, bytes_accessed=2 * n * width, transcendentals=0
        ),
    )(images, references, initial_contrast[None, :])
    anywhere = pl.BlockSpec(memory_space=pl.ANY)
    new_references, contrast, loglik = pl.pallas_call(
        put_out,
        out_shape=(
            jax.ShapeDtypeStruct((rows, width), BF16),
            jax.ShapeDtypeStruct((1, n), F32),
            jax.ShapeDtypeStruct((1, n), F32),
        ),
        in_specs=[pl.BlockSpec(memory_space=pltpu.VMEM)] * 3,
        out_specs=(anywhere,) * 3,
        scratch_shapes=[pltpu.SemaphoreType.DMA((3,))],
    )(*(pltpu.with_memory_space_constraint(v, pltpu.VMEM) for v in (new_references, contrast, loglik)))
    return (new_references, contrast[0], loglik[0])


def solution(mesh):
    n_img, n_ref = mesh.shape["img"], mesh.shape["ref"]
    placed = (P("img", None), P("ref", None), P("img"))
    return jax.shard_map(
        functools.partial(per_device, n_img // 4, n_ref),
        mesh=mesh,
        in_specs=placed,
        out_specs=(P("ref", None), P("img"), P("img")),
        check_vma=False,
    )
```

```python
import functools
import math

import jax
import jax.numpy as jnp
from jax import lax
from jax.experimental import pallas as pl
from jax.experimental.pallas import tpu as pltpu
from jax.sharding import PartitionSpec as P

ITERS = 3

sharpness = 2.0
prior_weight = 1.0
epsilon = 1e-06

MESH = pl.DeviceIdType.MESH
LANES = 256
AHEAD = 2
BLOCK = 512
TILES = BLOCK // 128
ROWS = 128
LOG2E = math.log2(math.e)
QUADS = ((1, 0), (1, 1), (0, 1), (0, 0))
F32 = jnp.float32
BF16 = jnp.bfloat16

RATE = 46.5e3
HOP = 2.7
FAR = 0.0
BACKLOG = 0.9
EAGER = 1
DIRECT = 1
RANK = {"S1": 2, "S2": 1, "P": 4, "F": 4, "Q": 4}
COST = {"W": 1.27, "S2": 0.04, "Z": 0.06, "A": 0.11, "N": 0.2, "G": 1.1}
PAIR = 2


def low(k):
    return k & -k


def plan(groups, nz, block, pieces, pair):
    unit = block / RATE
    zs = range(1, nz)
    bits = [1 << j for j in range(nz.bit_length() - 1)]
    todo = {("W", s): ((-1, s, 0), [("W", s - 1)] if s else [], []) for s in range(4)}
    for g in range(groups):
        for s in (0, 1):
            for j in (0, 1):
                todo["S1", g, s, j] = (
                    (-2 if g < EAGER else RANK["S1"], g, j), [("W", s)],
                    [(("s1", g, s, j), "xy"[s], unit * nz)],
                )
            todo["S2", g, s] = (
                (RANK["S2"], g, 0), [("s1", g, s, 0), ("W", 3)], [(("s2", g, s), "yx"[s], unit * nz)]
            )
        met = [("s1", g, s, 1) for s in (0, 1)] + [("s2", g, s) for s in (0, 1)]
        met_z = [("z", g, k) for k in zs]
        if g < DIRECT:
            weight = {k: 2 * unit * (1.0 if k == 1 else 1.5) for k in zs}
            todo["Z", g, 0] = (0, g, 0), met, [(("z", g, k), "z", weight[k]) for k in zs]
            az = zs
        else:
            weight = dict.fromkeys(zs, 2 * unit)
            for bit in bits:
                inner = [("z", g, k) for k in zs if low(k) < bit and k > low(k)]
                todo["Z", g, bit] = (
                    (0, g, bit), met + inner,
                    [(("z", g, k), "z", weight[k]) for k in zs if low(k) == bit][::-1],
                )
            az = bits[::-1]
            for k in zs:
                if low(k) > 1:
                    todo["T", g, k] = (
                        (0, g, 0), [("az", g, k)],
                        [(("az", g, k + b), "z", weight[k]) for b in az if b < low(k)],
                    )
        todo["A", g] = (0, g, 0), met + met_z, [(("az", g, k), "z", weight[k]) for k in az]
        every = []
        for k in range(nz):
            base = [("az", g, k)] if k else [("A", g)]
            outs = [[(("y", g, k, 0), "y", unit), (("x", g, k, 1), "x", unit)]]
            outs.append([(("y", g, k, 1), "y", unit), (("x", g, k, 0), "x", unit)])
            outs.append([(("fx", g, k), "x", unit), (("fy", g, k), "y", unit)])
            todo["P", g, k] = (RANK["P"], g, 0), base, outs[0]
            todo["F", g, k] = (RANK["F"], g, 1), [("y", g, k, 0), ("x", g, k, 1)], outs[1 + 1]
            todo["Q", g, k] = (RANK["Q"], g, 2), base, outs[1]
            every += [name for out in outs for name, _, _ in out]
        todo["N", g] = (5, g, 0), every, []
        if g % pair == pair - 1:
            for p in range(pieces):
                todo["G", g // pair, p] = (6, g, p), [("N", i) for i in range(g + 1)], []
    clock, order, arrived = 0.0, [], {}
    free = dict.fromkeys("xyz", 0.0)
    while todo:
        best = None
        for name, (rank, waits, out) in todo.items():
            if all(wait in arrived for wait in waits):
                start = max([arrived[wait] for wait in waits], default=0.0)
                start = max(start, clock)
                if rank[0] > -2:
                    start = max([start] + [free[link] - BACKLOG for _, link, _ in out])
                if best is None or (start, rank, name) < best:
                    best = (start, rank, name)
        start, _, name = best
        out = todo.pop(name)[2]
        clock = start + COST.get(name[0], 0.02)
        arrived[name] = clock
        for message, link, length in out:
            free[link] = max(free[link], clock) + length
            arrived[message] = free[link] + HOP
            if link == "z":
                far = message[2] if message[1] < DIRECT else low(message[2])
                arrived[message] += FAR if far > 1 else 0.0
        order.append(name)
    return order


def kernel(
    nz, n_ref, im_hbm, ref_hbm, prior_hbm, newref, contrast_ref, loglik_ref,
    im, refs, norms, cross, w, snd1, rcv1, acc, snd2, rcv2, snd3, rcv3, own,
    stat_snd, stat_rcv, vecs, keep, prior_sem,
    stat_ssem, stat_rsem, im_sem, ref_sem, ssem, rsem,
):
    n, width = im.shape
    rows = refs.shape[0]
    groups = own.shape[0]
    rg = own.shape[2]
    gr = nz * rg
    qr = groups * gr
    half = width // 2
    me = lax.axis_index("img")
    rme = lax.axis_index("ref")
    x, y, z = lax.rem(me, 2), lax.rem(me // 2, 2), me // 4
    def chip(dx, dy, dz):
        zz, bit = z, 1
        while bit < nz:
            if dz & bit:
                zz = zz + bit - 2 * bit * lax.rem(z // bit, 2)
            bit *= 2
        return zz * 4 + lax.rem(y + dy, 2) * 2 + lax.rem(x + dx, 2)

    def send(src, dst, dev, kind, slot):
        pltpu.make_async_remote_copy(
            src_ref=src, dst_ref=dst, send_sem=ssem.at[kind], recv_sem=rsem.at[slot],
            device_id=dev, device_id_type=MESH,
        ).start()

    x_dev = {"img": chip(1, 0, 0)}
    y_dev = {"img": chip(0, 1, 0)}
    z_dev = [{"img": chip(0, 0, k)} for k in range(nz)]
    r_dev = [{"ref": lax.rem(rme + k, n_ref)} for k in range(n_ref)]

    barrier = pltpu.get_barrier_semaphore()
    peers = r_dev[1:] + [x_dev, y_dev] + z_dev[1:]
    for dev in peers:
        pl.semaphore_signal(barrier, inc=1, device_id=dev, device_id_type=MESH)

    ref_copies = []
    per_ref = rows // ref_sem.shape[0]
    for s in range(ref_sem.shape[0]):
        part = pl.ds(s * per_ref, per_ref)
        copy = pltpu.make_async_copy(ref_hbm.at[part], refs.at[part], ref_sem.at[s])
        copy.start()
        ref_copies.append(copy)
    def load_images(b):
        part = pl.ds(pl.multiple_of(b * LANES, LANES), LANES)
        return pltpu.make_async_copy(im_hbm.at[part], im.at[part], im_sem.at[b])

    ahead = min(AHEAD, n // LANES)
    for b in range(ahead):
        load_images(b).start()
    prior_copy = pltpu.make_async_copy(prior_hbm, vecs.at[3:4, :], prior_sem)
    prior_copy.start()

    stat_snd[...] = jnp.zeros_like(stat_snd)

    def square_sums(source, r0, count, scale):
        block = source[pl.ds(r0, count), :].astype(F32)
        total = jnp.sum(block * block, axis=1, keepdims=True) * scale
        norms[pl.ds(r0, count), :] = jnp.broadcast_to(total, (count, 128))

    for copy in ref_copies:
        copy.wait()
    for b in range(ahead, n // LANES):
        load_images(b).start()
    per_block = rows // (n // LANES)

    nt = (((1,), (1,)), ((), ()))
    nn = (((1,), (0,)), ((), ()))

    def fold(x):
        return x.reshape(x.shape[0] // 8, 8, 128)

    def spread8(x):
        return jnp.broadcast_to(x, (8, 128))

    at_chip = {
        (dx, dy, dz): chip(dx, dy, dz) * rg for dx, dy in QUADS for dz in range(nz)
    }

    def row0(g, where):
        return pl.multiple_of(g * (4 * gr) + at_chip[where], 8)

    def lanes(c0, width_=128):
        return pl.ds(pl.multiple_of(c0, 128), width_)

    def coefficients(c0, width_):
        a = vecs[0:1, lanes(c0, width_)]
        slope = (sharpness * LOG2E) * a
        bend = (0.5 * sharpness * LOG2E) * (a * a)
        tiles = range(0, width_, 128)
        return (
            [spread8(slope[:, t : t + 128]) for t in tiles],
            [spread8(bend[:, t : t + 128]) for t in tiles],
        )

    def over_rows(count, body, init):
        return lax.fori_loop(
            0, count // ROWS, lambda i, c: body(pl.multiple_of(i * ROWS, ROWS), c), init
        )

    def scores(c0):
        slope, bend = coefficients(c0, BLOCK)

        def body(r, high):
            part = pl.ds(r, ROWS)
            nrm = fold(norms[part, :])
            out = []
            for t in range(TILES):
                c = fold(cross[part, lanes(c0 + t * 128)])
                sc = slope[t][None] * c - bend[t][None] * nrm
                keep[part, t * 128 : (t + 1) * 128] = sc.reshape(ROWS, 128)
                out.append(jnp.maximum(high[t], jnp.max(sc, axis=0)))
            return tuple(out)

        high = over_rows(rows, body, (jnp.full((8, 128), -jnp.inf, F32),) * TILES)
        return [jnp.max(x, axis=0, keepdims=True) for x in high]

    def sums_of(c0, high, full):
        top = [spread8(x) for x in high]

        def body(r, carry):
            part = pl.ds(r, ROWS)
            nrm = fold(norms[part, :]) if full else None
            out = list(carry)
            for t in range(TILES):
                sc = fold(keep[part, t * 128 : (t + 1) * 128])
                e = jnp.exp2(sc - top[t][None])
                out[t] = out[t] + jnp.sum(e, axis=0)
                if full:
                    c = fold(cross[part, lanes(c0 + t * 128)])
                    out[TILES + t] = out[TILES + t] + jnp.sum(e * c, axis=0)
                    out[2 * TILES + t] = out[2 * TILES + t] + jnp.sum(e * nrm, axis=0)
            return tuple(out)

        zero = jnp.zeros((8, 128), F32)
        carry = over_rows(rows, body, (zero,) * (TILES * (3 if full else 1)))
        return [jnp.sum(x, axis=0, keepdims=True) for x in carry]

    def weigh(c0):
        slope, bend = coefficients(c0, BLOCK)
        top = [spread8(vecs[1:2, lanes(c0 + t * 128)]) for t in range(TILES)]
        gain = [spread8(vecs[2:3, lanes(c0 + t * 128)]) for t in range(TILES)]

        def body(g, carry):
            for q in range(4):
                parts = [pl.ds(row0(g, QUADS[q] + (dz,)), rg) for dz in range(nz)]
                nrm = [norms[part, :].reshape(rg // 8, 8, 128) for part in parts]
                to = pl.ds(pl.multiple_of(q * qr + g * gr, 8), gr)
                for t in range(TILES):
                    at = lanes(c0 + t * 128)
                    e = []
                    for part, norm in zip(parts, nrm):
                        c = cross[part, at].reshape(rg // 8, 8, 128)
                        sc = slope[t][None] * c - bend[t][None] * norm
                        e.append((jnp.exp2(sc - top[t][None]) * gain[t][None]).reshape(rg, 128))
                    w[to, at] = jnp.concatenate(e, axis=0).astype(BF16)
            return carry

        lax.fori_loop(0, groups, body, 0)

    blocks = n // BLOCK

    def stat_copy(it, h, k):
        slot = (it * blocks + h) * (n_ref - 1) + k - 1
        return pltpu.make_async_remote_copy(
            src_ref=stat_snd.at[it, h], dst_ref=stat_rcv.at[slot],
            send_sem=stat_ssem.at[k - 1],
            recv_sem=stat_rsem.at[(lax.rem(it, 2) * blocks + h) * (n_ref - 1) + k - 1],
            device_id=r_dev[k], device_id_type=MESH,
        )

    def local_stats(it, h, full, first=False):
        c0 = h * BLOCK
        high = scores(c0)
        sums = sums_of(c0, high, full)
        for t in range(TILES):
            at = slice(t * 128, (t + 1) * 128)
            stat_snd[it, h, 0:1, at] = high[t]
            for j in range(len(sums) // TILES):
                stat_snd[it, h, j + 1 : j + 2, at] = sums[j * TILES + t]
        if first:

            @pl.when(h == 0)
            def _():
                pl.semaphore_wait(barrier, len(peers))

        for k in range(1, n_ref):
            stat_copy(it, h, k).start()

    def joint_stats(it, h, full):
        shares = [stat_snd[it, h]]
        for k in range(1, n_ref):
            stat_copy(it, h, k).wait_recv()
            shares.append(stat_rcv[(it * blocks + h) * (n_ref - 1) + k - 1])
        high = functools.reduce(jnp.maximum, [share[0:1] for share in shares])
        scales = [jnp.exp2(share[0:1] - high) for share in shares]
        sums = [
            functools.reduce(
                jnp.add, [share[j : j + 1] * sc for share, sc in zip(shares, scales)]
            )
            for j in ((1, 2, 3) if full else (1,))
        ]
        return high, sums

    def each(count, body):
        def step(i, carry):
            body(i)
            return carry

        lax.fori_loop(0, count, step, 0)


    prior_copy.wait()
    vecs[0:1, :] = vecs[3:4, :]

    def first_cross(b):
        part = pl.ds(pl.multiple_of(b * LANES, LANES), LANES)
        load_images(b).wait()
        for r in range(0, per_block, 32):
            square_sums(refs, pl.multiple_of(b * per_block + r, 32), 32, 1.0)
        cross[:, part] = lax.dot_general(
            refs[...], im[part, :], nt, preferred_element_type=F32
        )

    def refit(i):
        it, h = i // blocks, lax.rem(i, blocks)
        at = lanes(h * BLOCK, BLOCK)
        _, (total, along, weight) = joint_stats(it, h, True)
        vecs[0:1, at] = (along / total + prior_weight * vecs[3:4, at]) / (
            weight / total + prior_weight
        )
        local_stats(it + 1, h, True)

    def settle(h):
        at = lanes(h * BLOCK, BLOCK)
        high, (total,) = joint_stats(ITERS, h, False)
        vecs[1:2, at] = high
        vecs[2:3, at] = vecs[0:1, at] / total
        weigh(h * BLOCK)

    each(n // LANES, first_cross)
    each(blocks, lambda h: local_stats(0, h, True, True))
    each(ITERS * blocks, refit)
    each(blocks, settle)
    contrast_ref[...] = vecs[0:1, :]

    def weighted(r0s, c0, store):
        def body(b, carry):
            col = pl.multiple_of(b * LANES, LANES)
            lhs = [w[r0 : r0 + cnt, :] for r0, cnt in r0s]
            lhs = lhs[0] if len(lhs) == 1 else jnp.concatenate(lhs, axis=0)
            rhs = im[:, pl.ds(pl.multiple_of(c0 + col, LANES), LANES)]
            out = lax.dot_general(lhs, rhs, nn, preferred_element_type=F32)
            store(pl.ds(col, LANES), out[:qr], out[qr:])
            return carry

        lax.fori_loop(0, half // LANES, body, 0)

    def to_send(stream, first_is_far):
        def store(cols, lo, hi):
            far, near = (lo, hi) if first_is_far else (hi, lo)
            snd1[stream * 2, :, cols] = far.astype(BF16)
            snd1[stream * 2 + 1, :, cols] = near.astype(BF16)

        return store

    def to_keep(stream):
        def store(cols, lo, hi):
            acc[stream * 2, :, cols] = lo
            acc[stream * 2 + 1, :, cols] = hi

        return store

    hop_dev = (x_dev, y_dev)
    landed = set()
    kinds = {"s1": 0, "s2": 1, "z": 2, "az": 3, "y": 4, "x": 4, "fx": 5, "fy": 5}
    per_group = 3 * nz + 2
    bits = [1 << j for j in range(nz.bit_length() - 1)]

    def slot_of(name):
        kind, g = name[:2]
        if kind == "s1" and name[3] == 0:
            at = name[2]
        elif kind in ("s1", "s2"):
            at = 2
        elif kind == "z":
            at = 2 + name[2]
        elif kind == "az":
            at = 1 + nz + name[2]
        elif kind in ("x", "y") and name[3] == (kind == "x"):
            at = 1 + 2 * nz + name[2]
        else:
            at = 1 + 3 * nz
        return g * per_group + at

    def put(name, src, dst, dev):
        send(src, dst, dev, kinds[name[0]], slot_of(name))

    def arrive(name, like):
        slot = slot_of(name)
        if slot not in landed:
            landed.add(slot)
            pltpu.make_async_copy(like, like, rsem.at[slot]).wait()

    def send1(g, s, j):
        part = pl.ds(g * gr, gr)
        put(("s1", g, s, j), snd1.at[s * 2 + j, part], rcv1.at[s * 2 + j, part], hop_dev[s])

    def send2(g, s):
        part = pl.ds(g * gr, gr)
        arrive(("s1", g, s, 0), rcv1.at[s * 2, part])
        snd2[s, part, :] = (acc[s * 2, part, :] + rcv1[s * 2, part, :].astype(F32)).astype(BF16)
        put(("s2", g, s), snd2.at[s, part], rcv2.at[s, part], hop_dev[1 - s])

    def send3(g, bit):
        part = pl.ds(g * gr, gr)
        if bit < 2:
            arrive(("s2", g, 0), rcv1.at[:, part])
            for s in (0, 1):
                total = (
                    acc[s * 2 + 1, part, :]
                    + rcv1[s * 2 + 1, part, :].astype(F32)
                    + rcv2[s, part, :].astype(F32)
                )
                cols = slice(s * half, (s + 1) * half)
                for k in range(nz):
                    block = total[k * rg : (k + 1) * rg]
                    if k and (bit == 0 or low(k) == 1):
                        snd3[g, k - 1, :, cols] = block.astype(BF16)
                    else:
                        own[g, k, :, cols] = block
        for k in range(nz - 1, 0, -1):
            if bit and low(k) != bit:
                continue
            if bit > 1:
                total = own[g, k]
                for c in bits:
                    if c < bit:
                        arrive(("z", g, k + c), rcv3.at[g, 0])
                        total = total + rcv3[g, k + c - 1].astype(F32)
                snd3[g, k - 1] = total.astype(BF16)
            put(("z", g, k), snd3.at[g, k - 1], rcv3.at[g, k - 1], z_dev[bit or k])

    def finish(g):
        total = own[g, 0]
        for k in range(1, nz) if g < DIRECT else bits:
            arrive(("z", g, k), rcv3.at[g, 0])
            total = total + rcv3[g, k - 1].astype(F32)
        square = jnp.sum(total * total, axis=1, keepdims=True)
        mine = pl.ds(row0(g, (0, 0, 0)), rg)
        newref[mine, :] = (total * lax.rsqrt(square / width + epsilon)).astype(BF16)
        for k in range(1, nz) if g < DIRECT else bits[::-1]:
            put(("az", g, k), newref.at[mine], newref.at[mine], z_dev[k])

    def relay(g, k):
        part = newref.at[pl.ds(row0(g, (0, 0, k)), rg)]
        arrive(("az", g, k), part)
        for bit in bits[::-1]:
            if bit < low(k):
                put(("az", g, k + bit), part, part, z_dev[bit])

    def piece(g, where, side):
        return newref.at[pl.ds(row0(g, where), rg), pl.ds(side * half, half)]

    def pass_on(name, g, where, side, dev):
        part = piece(g, where, side)
        put(name, part, part, dev)

    def spread_first(g, k):
        if k:
            arrive(("az", g, k), newref.at[pl.ds(row0(g, (0, 0, k)), rg)])
        pass_on(("y", g, k, 0), g, (0, 0, k), 0, y_dev)
        pass_on(("x", g, k, 1), g, (0, 0, k), 1, x_dev)

    def spread_second(g, k):
        if k:
            arrive(("az", g, k), newref.at[pl.ds(row0(g, (0, 0, k)), rg)])
        pass_on(("y", g, k, 1), g, (0, 0, k), 1, y_dev)
        pass_on(("x", g, k, 0), g, (0, 0, k), 0, x_dev)

    def forward(g, k):
        arrive(("y", g, k, 0), newref.at[pl.ds(row0(g, (0, 1, k)), rg)])
        pass_on(("fx", g, k), g, (0, 1, k), 0, x_dev)
        pass_on(("fy", g, k), g, (1, 0, k), 1, y_dev)

    def new_norms(g):
        arrive(("fx", g, 0), newref.at[pl.ds(g * 4 * gr, 2 * gr)])

        def squares(i):
            square_sums(newref, pl.multiple_of(g * 4 * gr + i * 64, 64), 64, 1.0 / width)

        each(4 * gr // 64, squares)

    pair = PAIR if groups % PAIR == 0 else 1
    per_slot = BLOCK // LANES

    def likelihoods(c, h):
        r0, count = c * pair * 4 * gr, pair * 4 * gr
        chunks = [slice(r, min(r + ROWS, count)) for r in range(0, count, ROWS)]

        def body(i):
            c0 = h * BLOCK + i * LANES
            part = pl.ds(pl.multiple_of(c0, LANES), LANES)
            out = lax.dot_general(
                newref[r0 : r0 + count, :], im[part, :], nt, preferred_element_type=F32
            )
            slope, bend = coefficients(c0, LANES)
            slope = [x * width ** (-0.5) for x in slope]
            to = pl.ds(pl.multiple_of(i * LANES, 128), LANES)
            highs, totals = [], []
            for t in range(LANES // 128):
                sc = []
                for rr in chunks:
                    nrm = fold(norms[r0 + rr.start : r0 + rr.stop, :])
                    sc.append(
                        slope[t][None] * fold(out[rr, t * 128 : (t + 1) * 128])
                        - bend[t][None] * nrm
                    )
                high = functools.reduce(jnp.maximum, [jnp.max(x, axis=0) for x in sc])
                high = jnp.max(high, axis=0, keepdims=True)
                total = functools.reduce(
                    jnp.add, [jnp.sum(jnp.exp2(x - spread8(high)[None]), axis=0) for x in sc]
                )
                highs.append(high)
                totals.append(jnp.sum(total, axis=0, keepdims=True))
            high = jnp.concatenate(highs, axis=1)
            total = jnp.concatenate(totals, axis=1)
            if c > 0:
                before, sum_before = stat_snd[ITERS + 1, h, 0:1, to], stat_snd[ITERS + 1, h, 1:2, to]
                top = jnp.maximum(before, high)
                total = sum_before * jnp.exp2(before - top) + total * jnp.exp2(high - top)
                high = top
            stat_snd[ITERS + 1, h, 0:1, to] = high
            stat_snd[ITERS + 1, h, 1:2, to] = total

        for i in range(per_slot):
            body(i)
        if c == groups // pair - 1:
            for k in range(1, n_ref):
                stat_copy(ITERS + 1, h, k).start()

    steps = {
        "S1": send1, "S2": send2, "Z": send3, "A": finish, "T": relay, "P": spread_first,
        "Q": spread_second, "F": forward, "N": new_norms, "G": likelihoods,
    }
    order = plan(groups, nz, rg * width, blocks, pair)
    sums = (
        functools.partial(weighted, [(0, 2 * qr)], 0, to_send(0, False)),
        functools.partial(weighted, [(qr, 2 * qr)], half, to_send(1, True)),
        functools.partial(weighted, [(2 * qr, 2 * qr)], 0, to_keep(0)),
        functools.partial(weighted, [(0, qr), (3 * qr, qr)], half, to_keep(1)),
    )
    steps["W"] = lambda part: sums[part]()
    rest = order
    for name in rest:
        steps[name[0]](*name[1:])

    def final_likelihood(h):
        high, (total,) = joint_stats(ITERS + 1, h, False)
        loglik_ref[:, lanes(h * BLOCK, BLOCK)] = (
            high * math.log(2.0) + jnp.log(total) - math.log(rows * n_ref)
        )

    each(blocks, final_likelihood)
    def all_sent(like, sem):
        pltpu.make_async_copy(like, like, sem).wait()

    for k in range(1, n_ref):
        all_sent(stat_snd, stat_ssem.at[k - 1])
    for kind, like in enumerate((snd1, snd2, snd3, snd3)):
        all_sent(like, ssem.at[kind])
    all_sent(newref.at[pl.ds(0, 2 * qr)], ssem.at[4])
    all_sent(newref.at[pl.ds(0, qr)], ssem.at[5])


def put_out(new_vmem, contrast_vmem, loglik_vmem, new_hbm, contrast_hbm, loglik_hbm, sem):
    pairs = ((new_vmem, new_hbm), (contrast_vmem, contrast_hbm), (loglik_vmem, loglik_hbm))
    copies = [pltpu.make_async_copy(a, b, sem.at[i]) for i, (a, b) in enumerate(pairs)]
    for copy in copies:
        copy.start()
    for copy in copies:
        copy.wait()


def per_device(nz, n_ref, images, references, initial_contrast):
    n, width = images.shape
    rows = references.shape[0]
    groups = max(1, min(4, rows // (32 * nz)))
    rg = rows // (4 * nz * groups)
    qr, half = nz * rg * groups, width // 2
    steps = ITERS + 2
    peers = max(n_ref - 1, 1)
    stat_copies = steps * (n // BLOCK) * peers
    arrivals = groups * (3 * nz + 2)
    flops = 6 * n * width * rows
    new_references, contrast, loglik = pl.pallas_call(
        functools.partial(kernel, nz, n_ref),
        out_shape=(
            pltpu.VMEM((rows, width), BF16),
            pltpu.VMEM((1, n), F32),
            pltpu.VMEM((1, n), F32),
        ),
        in_specs=[
            pl.BlockSpec(memory_space=pl.ANY),
            pl.BlockSpec(memory_space=pl.ANY),
            pl.BlockSpec(memory_space=pl.ANY),
        ],
        out_specs=(
            pl.BlockSpec(memory_space=pltpu.VMEM),
            pl.BlockSpec(memory_space=pltpu.VMEM),
            pl.BlockSpec(memory_space=pltpu.VMEM),
        ),
        scratch_shapes=[
            pltpu.VMEM((n, width), BF16),
            pltpu.VMEM((rows, width), BF16),
            pltpu.VMEM((rows, 128), F32),
            pltpu.VMEM((rows, n), F32),
            pltpu.VMEM((rows, n), BF16),
            pltpu.VMEM((4, qr, half), BF16),
            pltpu.VMEM((4, qr, half), BF16),
            pltpu.VMEM((4, qr, half), F32),
            pltpu.VMEM((2, qr, half), BF16),
            pltpu.VMEM((2, qr, half), BF16),
            pltpu.VMEM((groups, max(nz - 1, 1), rg, width), BF16),
            pltpu.VMEM((groups, max(nz - 1, 1), rg, width), BF16),
            pltpu.VMEM((groups, nz, rg, width), F32),
            pltpu.VMEM((steps, n // BLOCK, 4, BLOCK), F32),
            pltpu.VMEM((stat_copies, 4, BLOCK), F32),
            pltpu.VMEM((8, n), F32),
            pltpu.VMEM((rows, BLOCK), F32),
            pltpu.SemaphoreType.DMA(()),
            pltpu.SemaphoreType.DMA((peers,)),
            pltpu.SemaphoreType.DMA((2 * (n // BLOCK) * peers,)),
            pltpu.SemaphoreType.DMA((n // LANES,)),
            pltpu.SemaphoreType.DMA((4,)),
            pltpu.SemaphoreType.DMA((6,)),
            pltpu.SemaphoreType.DMA((arrivals,)),
        ],
        compiler_params=pltpu.CompilerParams(
            collective_id=0, has_side_effects=True, vmem_limit_bytes=56 * 1024 * 1024
        ),
        cost_estimate=pl.CostEstimate(
            flops=flops, bytes_accessed=2 * n * width, transcendentals=0
        ),
    )(images, references, initial_contrast[None, :])
    anywhere = pl.BlockSpec(memory_space=pl.ANY)
    new_references, contrast, loglik = pl.pallas_call(
        put_out,
        out_shape=(
            jax.ShapeDtypeStruct((rows, width), BF16),
            jax.ShapeDtypeStruct((1, n), F32),
            jax.ShapeDtypeStruct((1, n), F32),
        ),
        in_specs=[pl.BlockSpec(memory_space=pltpu.VMEM)] * 3,
        out_specs=(anywhere,) * 3,
        scratch_shapes=[pltpu.SemaphoreType.DMA((3,))],
    )(*(pltpu.with_memory_space_constraint(v, pltpu.VMEM) for v in (new_references, contrast, loglik)))
    return (new_references, contrast[0], loglik[0])


def solution(mesh):
    n_img, n_ref = mesh.shape["img"], mesh.shape["ref"]
    placed = (P("img", None), P("ref", None), P("img"))
    return jax.shard_map(
        functools.partial(per_device, n_img // 4, n_ref),
        mesh=mesh,
        in_specs=placed,
        out_specs=(P("ref", None), P("img"), P("img")),
        check_vma=False,
    )
```

```python
import functools
import math

import jax
import jax.numpy as jnp
from jax import lax
from jax.experimental import pallas as pl
from jax.experimental.pallas import tpu as pltpu
from jax.sharding import PartitionSpec as P

ITERS = 3

sharpness = 2.0
prior_weight = 1.0
epsilon = 1e-06

MESH = pl.DeviceIdType.MESH
LANES = 256
AHEAD = 2
BLOCK = 512
TILES = BLOCK // 128
ROWS = 128
LOG2E = math.log2(math.e)
QUADS = ((1, 0), (1, 1), (0, 1), (0, 0))
F32 = jnp.float32
BF16 = jnp.bfloat16

RATE = 48e3
HOP = 2.7
FAR = 0.0
BACKLOG = 0.9
EAGER = 1
DIRECT = 1
RANK = {"S1": 2, "S2": 1, "P": 4, "F": 4, "Q": 4}
COST = {"W": 1.1, "S2": 0.04, "Z": 0.06, "A": 0.11, "N": 0.2, "G": 1.1}
PAIR = 2


def low(k):
    return k & -k


def plan(groups, nz, block, pieces, pair):
    unit = block / RATE
    zs = range(1, nz)
    bits = [1 << j for j in range(nz.bit_length() - 1)]
    todo = {("W", s): ((-1, s, 0), [("W", s - 1)] if s else [], []) for s in range(4)}
    for g in range(groups):
        for s in (0, 1):
            for j in (0, 1):
                todo["S1", g, s, j] = (
                    (-2 if g < EAGER else RANK["S1"], g, j), [("W", s)],
                    [(("s1", g, s, j), "xy"[s], unit * nz)],
                )
            todo["S2", g, s] = (
                (RANK["S2"], g, 0), [("s1", g, s, 0), ("W", 3)], [(("s2", g, s), "yx"[s], unit * nz)]
            )
        met = [("s1", g, s, 1) for s in (0, 1)] + [("s2", g, s) for s in (0, 1)]
        met_z = [("z", g, k) for k in zs]
        if g < DIRECT:
            weight = {k: 2 * unit * (1.0 if k == 1 else 1.5) for k in zs}
            todo["Z", g, 0] = (0, g, 0), met, [(("z", g, k), "z", weight[k]) for k in zs]
            az = zs
        else:
            weight = dict.fromkeys(zs, 2 * unit)
            for bit in bits:
                inner = [("z", g, k) for k in zs if low(k) < bit and k > low(k)]
                todo["Z", g, bit] = (
                    (0, g, bit), met + inner,
                    [(("z", g, k), "z", weight[k]) for k in zs if low(k) == bit][::-1],
                )
            az = bits[::-1]
            for k in zs:
                if low(k) > 1:
                    todo["T", g, k] = (
                        (0, g, 0), [("az", g, k)],
                        [(("az", g, k + b), "z", weight[k]) for b in az if b < low(k)],
                    )
        todo["A", g] = (0, g, 0), met + met_z, [(("az", g, k), "z", weight[k]) for k in az]
        every = []
        for k in range(nz):
            base = [("az", g, k)] if k else [("A", g)]
            outs = [[(("y", g, k, 0), "y", unit), (("x", g, k, 1), "x", unit)]]
            outs.append([(("y", g, k, 1), "y", unit), (("x", g, k, 0), "x", unit)])
            outs.append([(("fx", g, k), "x", unit), (("fy", g, k), "y", unit)])
            todo["P", g, k] = (RANK["P"], g, 0), base, outs[0]
            todo["F", g, k] = (RANK["F"], g, 1), [("y", g, k, 0), ("x", g, k, 1)], outs[1 + 1]
            todo["Q", g, k] = (RANK["Q"], g, 2), base, outs[1]
            every += [name for out in outs for name, _, _ in out]
        todo["N", g] = (5, g, 0), every, []
        if g % pair == pair - 1:
            for p in range(pieces):
                todo["G", g // pair, p] = (6, g, p), [("N", i) for i in range(g + 1)], []
    clock, order, arrived = 0.0, [], {}
    free = dict.fromkeys("xyz", 0.0)
    while todo:
        best = None
        for name, (rank, waits, out) in todo.items():
            if all(wait in arrived for wait in waits):
                start = max([arrived[wait] for wait in waits], default=0.0)
                start = max(start, clock)
                if rank[0] > -2:
                    start = max([start] + [free[link] - BACKLOG for _, link, _ in out])
                if best is None or (start, rank, name) < best:
                    best = (start, rank, name)
        start, _, name = best
        out = todo.pop(name)[2]
        clock = start + COST.get(name[0], 0.02)
        arrived[name] = clock
        for message, link, length in out:
            free[link] = max(free[link], clock) + length
            arrived[message] = free[link] + HOP
            if link == "z":
                far = message[2] if message[1] < DIRECT else low(message[2])
                arrived[message] += FAR if far > 1 else 0.0
        order.append(name)
    return order


def kernel(
    nz, n_ref, im_hbm, ref_hbm, prior_hbm, newref, contrast_ref, loglik_ref,
    im, refs, norms, cross, w, snd1, rcv1, acc, snd2, rcv2, snd3, rcv3, own,
    stat_snd, stat_rcv, vecs, keep, prior_sem,
    stat_ssem, stat_rsem, im_sem, ref_sem, ssem, rsem,
):
    n, width = im.shape
    rows = refs.shape[0]
    groups = own.shape[0]
    rg = own.shape[2]
    gr = nz * rg
    qr = groups * gr
    half = width // 2
    me = lax.axis_index("img")
    rme = lax.axis_index("ref")
    x, y, z = lax.rem(me, 2), lax.rem(me // 2, 2), me // 4
    def chip(dx, dy, dz):
        zz, bit = z, 1
        while bit < nz:
            if dz & bit:
                zz = zz + bit - 2 * bit * lax.rem(z // bit, 2)
            bit *= 2
        return zz * 4 + lax.rem(y + dy, 2) * 2 + lax.rem(x + dx, 2)

    def send(src, dst, dev, kind, slot):
        pltpu.make_async_remote_copy(
            src_ref=src, dst_ref=dst, send_sem=ssem.at[kind], recv_sem=rsem.at[slot],
            device_id=dev, device_id_type=MESH,
        ).start()

    x_dev = {"img": chip(1, 0, 0)}
    y_dev = {"img": chip(0, 1, 0)}
    z_dev = [{"img": chip(0, 0, k)} for k in range(nz)]
    r_dev = [{"ref": lax.rem(rme + k, n_ref)} for k in range(n_ref)]

    barrier = pltpu.get_barrier_semaphore()
    peers = r_dev[1:] + [x_dev, y_dev] + z_dev[1:]
    for dev in peers:
        pl.semaphore_signal(barrier, inc=1, device_id=dev, device_id_type=MESH)

    ref_copies = []
    per_ref = rows // ref_sem.shape[0]
    for s in range(ref_sem.shape[0]):
        part = pl.ds(s * per_ref, per_ref)
        copy = pltpu.make_async_copy(ref_hbm.at[part], refs.at[part], ref_sem.at[s])
        copy.start()
        ref_copies.append(copy)
    def load_images(b):
        part = pl.ds(pl.multiple_of(b * LANES, LANES), LANES)
        return pltpu.make_async_copy(im_hbm.at[part], im.at[part], im_sem.at[b])

    ahead = min(AHEAD, n // LANES)
    for b in range(ahead):
        load_images(b).start()
    prior_copy = pltpu.make_async_copy(prior_hbm, vecs.at[3:4, :], prior_sem)
    prior_copy.start()

    stat_snd[...] = jnp.zeros_like(stat_snd)

    def square_sums(source, r0, count, scale):
        block = source[pl.ds(r0, count), :].astype(F32)
        total = jnp.sum(block * block, axis=1, keepdims=True) * scale
        norms[pl.ds(r0, count), :] = jnp.broadcast_to(total, (count, 128))

    for copy in ref_copies:
        copy.wait()
    for b in range(ahead, n // LANES):
        load_images(b).start()
    per_block = rows // (n // LANES)

    nt = (((1,), (1,)), ((), ()))
    nn = (((1,), (0,)), ((), ()))

    def fold(x):
        return x.reshape(x.shape[0] // 8, 8, 128)

    def spread8(x):
        return jnp.broadcast_to(x, (8, 128))

    at_chip = {
        (dx, dy, dz): chip(dx, dy, dz) * rg for dx, dy in QUADS for dz in range(nz)
    }

    def row0(g, where):
        return pl.multiple_of(g * (4 * gr) + at_chip[where], 8)

    def lanes(c0, width_=128):
        return pl.ds(pl.multiple_of(c0, 128), width_)

    def coefficients(c0, width_):
        a = vecs[0:1, lanes(c0, width_)]
        slope = (sharpness * LOG2E) * a
        bend = (0.5 * sharpness * LOG2E) * (a * a)
        tiles = range(0, width_, 128)
        return (
            [spread8(slope[:, t : t + 128]) for t in tiles],
            [spread8(bend[:, t : t + 128]) for t in tiles],
        )

    def over_rows(count, body, init):
        return lax.fori_loop(
            0, count // ROWS, lambda i, c: body(pl.multiple_of(i * ROWS, ROWS), c), init
        )

    def scores(c0):
        slope, bend = coefficients(c0, BLOCK)

        def body(r, high):
            part = pl.ds(r, ROWS)
            nrm = fold(norms[part, :])
            out = []
            for t in range(TILES):
                c = fold(cross[part, lanes(c0 + t * 128)])
                sc = slope[t][None] * c - bend[t][None] * nrm
                keep[part, t * 128 : (t + 1) * 128] = sc.reshape(ROWS, 128)
                out.append(jnp.maximum(high[t], jnp.max(sc, axis=0)))
            return tuple(out)

        high = over_rows(rows, body, (jnp.full((8, 128), -jnp.inf, F32),) * TILES)
        return [jnp.max(x, axis=0, keepdims=True) for x in high]

    def sums_of(c0, high, full):
        top = [spread8(x) for x in high]

        def body(r, carry):
            part = pl.ds(r, ROWS)
            nrm = fold(norms[part, :]) if full else None
            out = list(carry)
            for t in range(TILES):
                sc = fold(keep[part, t * 128 : (t + 1) * 128])
                e = jnp.exp2(sc - top[t][None])
                out[t] = out[t] + jnp.sum(e, axis=0)
                if full:
                    c = fold(cross[part, lanes(c0 + t * 128)])
                    out[TILES + t] = out[TILES + t] + jnp.sum(e * c, axis=0)
                    out[2 * TILES + t] = out[2 * TILES + t] + jnp.sum(e * nrm, axis=0)
            return tuple(out)

        zero = jnp.zeros((8, 128), F32)
        carry = over_rows(rows, body, (zero,) * (TILES * (3 if full else 1)))
        return [jnp.sum(x, axis=0, keepdims=True) for x in carry]

    def weigh(c0):
        slope, bend = coefficients(c0, BLOCK)
        top = [spread8(vecs[1:2, lanes(c0 + t * 128)]) for t in range(TILES)]
        gain = [spread8(vecs[2:3, lanes(c0 + t * 128)]) for t in range(TILES)]

        def body(g, carry):
            for q in range(4):
                parts = [pl.ds(row0(g, QUADS[q] + (dz,)), rg) for dz in range(nz)]
                nrm = [norms[part, :].reshape(rg // 8, 8, 128) for part in parts]
                to = pl.ds(pl.multiple_of(q * qr + g * gr, 8), gr)
                for t in range(TILES):
                    at = lanes(c0 + t * 128)
                    e = []
                    for part, norm in zip(parts, nrm):
                        c = cross[part, at].reshape(rg // 8, 8, 128)
                        sc = slope[t][None] * c - bend[t][None] * norm
                        e.append((jnp.exp2(sc - top[t][None]) * gain[t][None]).reshape(rg, 128))
                    w[to, at] = jnp.concatenate(e, axis=0).astype(BF16)
            return carry

        lax.fori_loop(0, groups, body, 0)

    blocks = n // BLOCK

    def stat_copy(it, h, k):
        slot = (it * blocks + h) * (n_ref - 1) + k - 1
        return pltpu.make_async_remote_copy(
            src_ref=stat_snd.at[it, h], dst_ref=stat_rcv.at[slot],
            send_sem=stat_ssem.at[k - 1],
            recv_sem=stat_rsem.at[(lax.rem(it, 2) * blocks + h) * (n_ref - 1) + k - 1],
            device_id=r_dev[k], device_id_type=MESH,
        )

    def local_stats(it, h, full, first=False):
        c0 = h * BLOCK
        high = scores(c0)
        sums = sums_of(c0, high, full)
        for t in range(TILES):
            at = slice(t * 128, (t + 1) * 128)
            stat_snd[it, h, 0:1, at] = high[t]
            for j in range(len(sums) // TILES):
                stat_snd[it, h, j + 1 : j + 2, at] = sums[j * TILES + t]
        if first:

            @pl.when(h == 0)
            def _():
                pl.semaphore_wait(barrier, len(peers))

        for k in range(1, n_ref):
            stat_copy(it, h, k).start()

    def joint_stats(it, h, full):
        shares = [stat_snd[it, h]]
        for k in range(1, n_ref):
            stat_copy(it, h, k).wait_recv()
            shares.append(stat_rcv[(it * blocks + h) * (n_ref - 1) + k - 1])
        high = functools.reduce(jnp.maximum, [share[0:1] for share in shares])
        scales = [jnp.exp2(share[0:1] - high) for share in shares]
        sums = [
            functools.reduce(
                jnp.add, [share[j : j + 1] * sc for share, sc in zip(shares, scales)]
            )
            for j in ((1, 2, 3) if full else (1,))
        ]
        return high, sums

    def each(count, body):
        def step(i, carry):
            body(i)
            return carry

        lax.fori_loop(0, count, step, 0)


    prior_copy.wait()
    vecs[0:1, :] = vecs[3:4, :]

    def first_cross(b):
        part = pl.ds(pl.multiple_of(b * LANES, LANES), LANES)
        load_images(b).wait()
        for r in range(0, per_block, 32):
            square_sums(refs, pl.multiple_of(b * per_block + r, 32), 32, 1.0)
        cross[:, part] = lax.dot_general(
            refs[...], im[part, :], nt, preferred_element_type=F32
        )

    def refit(i):
        it, h = i // blocks, lax.rem(i, blocks)
        at = lanes(h * BLOCK, BLOCK)
        _, (total, along, weight) = joint_stats(it, h, True)
        vecs[0:1, at] = (along / total + prior_weight * vecs[3:4, at]) / (
            weight / total + prior_weight
        )
        local_stats(it + 1, h, True)

    def settle(h):
        at = lanes(h * BLOCK, BLOCK)
        high, (total,) = joint_stats(ITERS, h, False)
        vecs[1:2, at] = high
        vecs[2:3, at] = vecs[0:1, at] / total
        weigh(h * BLOCK)

    each(n // LANES, first_cross)
    each(blocks, lambda h: local_stats(0, h, True, True))
    each(ITERS * blocks, refit)
    each(blocks, settle)
    contrast_ref[...] = vecs[0:1, :]

    def weighted(r0s, c0, store):
        def body(b, carry):
            col = pl.multiple_of(b * LANES, LANES)
            lhs = [w[r0 : r0 + cnt, :] for r0, cnt in r0s]
            lhs = lhs[0] if len(lhs) == 1 else jnp.concatenate(lhs, axis=0)
            rhs = im[:, pl.ds(pl.multiple_of(c0 + col, LANES), LANES)]
            out = lax.dot_general(lhs, rhs, nn, preferred_element_type=F32)
            store(pl.ds(col, LANES), out[:qr], out[qr:])
            return carry

        for b in range(half // LANES):
            body(b, 0)

    def to_send(stream, first_is_far):
        def store(cols, lo, hi):
            far, near = (lo, hi) if first_is_far else (hi, lo)
            snd1[stream * 2, :, cols] = far.astype(BF16)
            snd1[stream * 2 + 1, :, cols] = near.astype(BF16)

        return store

    def to_keep(stream):
        def store(cols, lo, hi):
            acc[stream * 2, :, cols] = lo
            acc[stream * 2 + 1, :, cols] = hi

        return store

    hop_dev = (x_dev, y_dev)
    landed = set()
    kinds = {"s1": 0, "s2": 1, "z": 2, "az": 3, "y": 4, "x": 4, "fx": 5, "fy": 5}
    per_group = 3 * nz + 2
    bits = [1 << j for j in range(nz.bit_length() - 1)]

    def slot_of(name):
        kind, g = name[:2]
        if kind == "s1" and name[3] == 0:
            at = name[2]
        elif kind in ("s1", "s2"):
            at = 2
        elif kind == "z":
            at = 2 + name[2]
        elif kind == "az":
            at = 1 + nz + name[2]
        elif kind in ("x", "y") and name[3] == (kind == "x"):
            at = 1 + 2 * nz + name[2]
        else:
            at = 1 + 3 * nz
        return g * per_group + at

    def put(name, src, dst, dev):
        send(src, dst, dev, kinds[name[0]], slot_of(name))

    def arrive(name, like):
        slot = slot_of(name)
        if slot not in landed:
            landed.add(slot)
            pltpu.make_async_copy(like, like, rsem.at[slot]).wait()

    def send1(g, s, j):
        part = pl.ds(g * gr, gr)
        put(("s1", g, s, j), snd1.at[s * 2 + j, part], rcv1.at[s * 2 + j, part], hop_dev[s])

    def send2(g, s):
        part = pl.ds(g * gr, gr)
        arrive(("s1", g, s, 0), rcv1.at[s * 2, part])
        snd2[s, part, :] = (acc[s * 2, part, :] + rcv1[s * 2, part, :].astype(F32)).astype(BF16)
        put(("s2", g, s), snd2.at[s, part], rcv2.at[s, part], hop_dev[1 - s])

    def send3(g, bit):
        part = pl.ds(g * gr, gr)
        if bit < 2:
            arrive(("s2", g, 0), rcv1.at[:, part])
            for s in (0, 1):
                total = (
                    acc[s * 2 + 1, part, :]
                    + rcv1[s * 2 + 1, part, :].astype(F32)
                    + rcv2[s, part, :].astype(F32)
                )
                cols = slice(s * half, (s + 1) * half)
                for k in range(nz):
                    block = total[k * rg : (k + 1) * rg]
                    if k and (bit == 0 or low(k) == 1):
                        snd3[g, k - 1, :, cols] = block.astype(BF16)
                    else:
                        own[g, k, :, cols] = block
        for k in range(nz - 1, 0, -1):
            if bit and low(k) != bit:
                continue
            if bit > 1:
                total = own[g, k]
                for c in bits:
                    if c < bit:
                        arrive(("z", g, k + c), rcv3.at[g, 0])
                        total = total + rcv3[g, k + c - 1].astype(F32)
                snd3[g, k - 1] = total.astype(BF16)
            put(("z", g, k), snd3.at[g, k - 1], rcv3.at[g, k - 1], z_dev[bit or k])

    def finish(g):
        total = own[g, 0]
        for k in range(1, nz) if g < DIRECT else bits:
            arrive(("z", g, k), rcv3.at[g, 0])
            total = total + rcv3[g, k - 1].astype(F32)
        square = jnp.sum(total * total, axis=1, keepdims=True)
        mine = pl.ds(row0(g, (0, 0, 0)), rg)
        newref[mine, :] = (total * lax.rsqrt(square / width + epsilon)).astype(BF16)
        for k in range(1, nz) if g < DIRECT else bits[::-1]:
            put(("az", g, k), newref.at[mine], newref.at[mine], z_dev[k])

    def relay(g, k):
        part = newref.at[pl.ds(row0(g, (0, 0, k)), rg)]
        arrive(("az", g, k), part)
        for bit in bits[::-1]:
            if bit < low(k):
                put(("az", g, k + bit), part, part, z_dev[bit])

    def piece(g, where, side):
        return newref.at[pl.ds(row0(g, where), rg), pl.ds(side * half, half)]

    def pass_on(name, g, where, side, dev):
        part = piece(g, where, side)
        put(name, part, part, dev)

    def spread_first(g, k):
        if k:
            arrive(("az", g, k), newref.at[pl.ds(row0(g, (0, 0, k)), rg)])
        pass_on(("y", g, k, 0), g, (0, 0, k), 0, y_dev)
        pass_on(("x", g, k, 1), g, (0, 0, k), 1, x_dev)

    def spread_second(g, k):
        if k:
            arrive(("az", g, k), newref.at[pl.ds(row0(g, (0, 0, k)), rg)])
        pass_on(("y", g, k, 1), g, (0, 0, k), 1, y_dev)
        pass_on(("x", g, k, 0), g, (0, 0, k), 0, x_dev)

    def forward(g, k):
        arrive(("y", g, k, 0), newref.at[pl.ds(row0(g, (0, 1, k)), rg)])
        pass_on(("fx", g, k), g, (0, 1, k), 0, x_dev)
        pass_on(("fy", g, k), g, (1, 0, k), 1, y_dev)

    def new_norms(g):
        arrive(("fx", g, 0), newref.at[pl.ds(g * 4 * gr, 2 * gr)])

        step = math.gcd(4 * gr, 128)

        def squares(i):
            square_sums(newref, pl.multiple_of(g * 4 * gr + i * step, 8), step, 1.0 / width)

        each(4 * gr // step, squares)

    pair = PAIR if groups % PAIR == 0 else 1
    per_slot = BLOCK // LANES

    def likelihoods(c, h):
        r0, count = c * pair * 4 * gr, pair * 4 * gr
        chunks = [slice(r, min(r + ROWS, count)) for r in range(0, count, ROWS)]

        def body(i):
            c0 = h * BLOCK + i * LANES
            part = pl.ds(pl.multiple_of(c0, LANES), LANES)
            out = lax.dot_general(
                newref[r0 : r0 + count, :], im[part, :], nt, preferred_element_type=F32
            )
            slope, bend = coefficients(c0, LANES)
            slope = [x * width ** (-0.5) for x in slope]
            to = pl.ds(pl.multiple_of(i * LANES, 128), LANES)
            highs, totals = [], []
            for t in range(LANES // 128):
                sc = []
                for rr in chunks:
                    nrm = fold(norms[r0 + rr.start : r0 + rr.stop, :])
                    sc.append(
                        slope[t][None] * fold(out[rr, t * 128 : (t + 1) * 128])
                        - bend[t][None] * nrm
                    )
                high = functools.reduce(jnp.maximum, [jnp.max(x, axis=0) for x in sc])
                high = jnp.max(high, axis=0, keepdims=True)
                total = functools.reduce(
                    jnp.add, [jnp.sum(jnp.exp2(x - spread8(high)[None]), axis=0) for x in sc]
                )
                highs.append(high)
                totals.append(jnp.sum(total, axis=0, keepdims=True))
            high = jnp.concatenate(highs, axis=1)
            total = jnp.concatenate(totals, axis=1)
            if c > 0:
                before, sum_before = stat_snd[ITERS + 1, h, 0:1, to], stat_snd[ITERS + 1, h, 1:2, to]
                top = jnp.maximum(before, high)
                total = sum_before * jnp.exp2(before - top) + total * jnp.exp2(high - top)
                high = top
            stat_snd[ITERS + 1, h, 0:1, to] = high
            stat_snd[ITERS + 1, h, 1:2, to] = total

        for i in range(per_slot):
            body(i)
        if c == groups // pair - 1:
            for k in range(1, n_ref):
                stat_copy(ITERS + 1, h, k).start()

    steps = {
        "S1": send1, "S2": send2, "Z": send3, "A": finish, "T": relay, "P": spread_first,
        "Q": spread_second, "F": forward, "N": new_norms, "G": likelihoods,
    }
    order = plan(groups, nz, rg * width, blocks, pair)
    sums = (
        functools.partial(weighted, [(0, 2 * qr)], 0, to_send(0, False)),
        functools.partial(weighted, [(qr, 2 * qr)], half, to_send(1, True)),
        functools.partial(weighted, [(2 * qr, 2 * qr)], 0, to_keep(0)),
        functools.partial(weighted, [(0, qr), (3 * qr, qr)], half, to_keep(1)),
    )
    steps["W"] = lambda part: sums[part]()
    rest = order
    for name in rest:
        steps[name[0]](*name[1:])

    def final_likelihood(h):
        high, (total,) = joint_stats(ITERS + 1, h, False)
        loglik_ref[:, lanes(h * BLOCK, BLOCK)] = (
            high * math.log(2.0) + jnp.log(total) - math.log(rows * n_ref)
        )

    each(blocks, final_likelihood)
    def all_sent(like, sem):
        pltpu.make_async_copy(like, like, sem).wait()

    for k in range(1, n_ref):
        all_sent(stat_snd, stat_ssem.at[k - 1])
    for kind, like in enumerate((snd1, snd2, snd3, snd3)):
        all_sent(like, ssem.at[kind])
    all_sent(newref.at[pl.ds(0, 2 * qr)], ssem.at[4])
    all_sent(newref.at[pl.ds(0, qr)], ssem.at[5])


def put_out(new_vmem, contrast_vmem, loglik_vmem, new_hbm, contrast_hbm, loglik_hbm, sem):
    pairs = ((new_vmem, new_hbm), (contrast_vmem, contrast_hbm), (loglik_vmem, loglik_hbm))
    copies = [pltpu.make_async_copy(a, b, sem.at[i]) for i, (a, b) in enumerate(pairs)]
    for copy in copies:
        copy.start()
    for copy in copies:
        copy.wait()


def per_device(nz, n_ref, images, references, initial_contrast):
    n, width = images.shape
    rows = references.shape[0]
    groups = max(1, min(4, rows // (32 * nz)))
    rg = rows // (4 * nz * groups)
    qr, half = nz * rg * groups, width // 2
    steps = ITERS + 2
    peers = max(n_ref - 1, 1)
    stat_copies = steps * (n // BLOCK) * peers
    arrivals = groups * (3 * nz + 2)
    flops = 6 * n * width * rows
    new_references, contrast, loglik = pl.pallas_call(
        functools.partial(kernel, nz, n_ref),
        out_shape=(
            pltpu.VMEM((rows, width), BF16),
            pltpu.VMEM((1, n), F32),
            pltpu.VMEM((1, n), F32),
        ),
        in_specs=[
            pl.BlockSpec(memory_space=pl.ANY),
            pl.BlockSpec(memory_space=pl.ANY),
            pl.BlockSpec(memory_space=pl.ANY),
        ],
        out_specs=(
            pl.BlockSpec(memory_space=pltpu.VMEM),
            pl.BlockSpec(memory_space=pltpu.VMEM),
            pl.BlockSpec(memory_space=pltpu.VMEM),
        ),
        scratch_shapes=[
            pltpu.VMEM((n, width), BF16),
            pltpu.VMEM((rows, width), BF16),
            pltpu.VMEM((rows, 128), F32),
            pltpu.VMEM((rows, n), F32),
            pltpu.VMEM((rows, n), BF16),
            pltpu.VMEM((4, qr, half), BF16),
            pltpu.VMEM((4, qr, half), BF16),
            pltpu.VMEM((4, qr, half), F32),
            pltpu.VMEM((2, qr, half), BF16),
            pltpu.VMEM((2, qr, half), BF16),
            pltpu.VMEM((groups, max(nz - 1, 1), rg, width), BF16),
            pltpu.VMEM((groups, max(nz - 1, 1), rg, width), BF16),
            pltpu.VMEM((groups, nz, rg, width), F32),
            pltpu.VMEM((steps, n // BLOCK, 4, BLOCK), F32),
            pltpu.VMEM((stat_copies, 4, BLOCK), F32),
            pltpu.VMEM((8, n), F32),
            pltpu.VMEM((rows, BLOCK), F32),
            pltpu.SemaphoreType.DMA(()),
            pltpu.SemaphoreType.DMA((peers,)),
            pltpu.SemaphoreType.DMA((2 * (n // BLOCK) * peers,)),
            pltpu.SemaphoreType.DMA((n // LANES,)),
            pltpu.SemaphoreType.DMA((4,)),
            pltpu.SemaphoreType.DMA((6,)),
            pltpu.SemaphoreType.DMA((arrivals,)),
        ],
        compiler_params=pltpu.CompilerParams(
            collective_id=0, has_side_effects=True, vmem_limit_bytes=56 * 1024 * 1024
        ),
        cost_estimate=pl.CostEstimate(
            flops=flops, bytes_accessed=2 * n * width, transcendentals=0
        ),
    )(images, references, initial_contrast[None, :])
    anywhere = pl.BlockSpec(memory_space=pl.ANY)
    new_references, contrast, loglik = pl.pallas_call(
        put_out,
        out_shape=(
            jax.ShapeDtypeStruct((rows, width), BF16),
            jax.ShapeDtypeStruct((1, n), F32),
            jax.ShapeDtypeStruct((1, n), F32),
        ),
        in_specs=[pl.BlockSpec(memory_space=pltpu.VMEM)] * 3,
        out_specs=(anywhere,) * 3,
        scratch_shapes=[pltpu.SemaphoreType.DMA((3,))],
    )(*(pltpu.with_memory_space_constraint(v, pltpu.VMEM) for v in (new_references, contrast, loglik)))
    return (new_references, contrast[0], loglik[0])


def solution(mesh):
    n_img, n_ref = mesh.shape["img"], mesh.shape["ref"]
    placed = (P("img", None), P("ref", None), P("img"))
    return jax.shard_map(
        functools.partial(per_device, n_img // 4, n_ref),
        mesh=mesh,
        in_specs=placed,
        out_specs=(P("ref", None), P("img"), P("img")),
        check_vma=False,
    )
```

```python
import functools
import math

import jax
import jax.numpy as jnp
from jax import lax
from jax.experimental import pallas as pl
from jax.experimental.pallas import tpu as pltpu
from jax.sharding import PartitionSpec as P

ITERS = 3

sharpness = 2.0
prior_weight = 1.0
epsilon = 1e-06

MESH = pl.DeviceIdType.MESH
LANES = 256
AHEAD = 2
BLOCK = 512
TILES = BLOCK // 128
ROWS = 128
LOG2E = math.log2(math.e)
QUADS = ((1, 0), (1, 1), (0, 1), (0, 0))
F32 = jnp.float32
BF16 = jnp.bfloat16

RATE = 48e3
HOP = 2.7
FAR = 0.0
BACKLOG = 0.9
EAGER = 1
DIRECT = 1
RANK = {"S1": 2, "S2": 1, "P": 4, "F": 4, "Q": 4}
COST = {"W": 1.1, "S2": 0.04, "Z": 0.06, "A": 0.11, "N": 0.2, "G": 1.1}
PAIR = 2


def low(k):
    return k & -k


def plan(groups, nz, block, pieces, pair):
    unit = block / RATE
    zs = range(1, nz)
    bits = [1 << j for j in range(nz.bit_length() - 1)]
    todo = {("W", s): ((-1, s, 0), [("W", s - 1)] if s else [], []) for s in range(4)}
    for g in range(groups):
        for s in (0, 1):
            for j in (0, 1):
                todo["S1", g, s, j] = (
                    (-2 if g < EAGER else RANK["S1"], g, j), [("W", s)],
                    [(("s1", g, s, j), "xy"[s], unit * nz)],
                )
            todo["S2", g, s] = (
                (RANK["S2"], g, 0), [("s1", g, s, 0), ("W", 3)], [(("s2", g, s), "yx"[s], unit * nz)]
            )
        met = [("s1", g, s, 1) for s in (0, 1)] + [("s2", g, s) for s in (0, 1)]
        met_z = [("z", g, k) for k in zs]
        if g < DIRECT:
            weight = {k: 2 * unit * (1.0 if k == 1 else 1.5) for k in zs}
            todo["Z", g, 0] = (0, g, 0), met, [(("z", g, k), "z", weight[k]) for k in zs]
            az = zs
        else:
            weight = dict.fromkeys(zs, 2 * unit)
            for bit in bits:
                inner = [("z", g, k) for k in zs if low(k) < bit and k > low(k)]
                todo["Z", g, bit] = (
                    (0, g, bit), met + inner,
                    [(("z", g, k), "z", weight[k]) for k in zs if low(k) == bit][::-1],
                )
            az = bits[::-1]
            for k in zs:
                if low(k) > 1:
                    todo["T", g, k] = (
                        (0, g, 0), [("az", g, k)],
                        [(("az", g, k + b), "z", weight[k]) for b in az if b < low(k)],
                    )
        todo["A", g] = (0, g, 0), met + met_z, [(("az", g, k), "z", weight[k]) for k in az]
        every = []
        for k in range(nz):
            base = [("az", g, k)] if k else [("A", g)]
            outs = [[(("y", g, k, 0), "y", unit), (("x", g, k, 1), "x", unit)]]
            outs.append([(("y", g, k, 1), "y", unit), (("x", g, k, 0), "x", unit)])
            outs.append([(("fx", g, k), "x", unit), (("fy", g, k), "y", unit)])
            todo["P", g, k] = (RANK["P"], g, 0), base, outs[0]
            todo["F", g, k] = (RANK["F"], g, 1), [("y", g, k, 0), ("x", g, k, 1)], outs[1 + 1]
            todo["Q", g, k] = (RANK["Q"], g, 2), base, outs[1]
            every += [name for out in outs for name, _, _ in out]
        todo["N", g] = (5, g, 0), every, []
        if g % pair == pair - 1:
            for p in range(pieces):
                todo["G", g // pair, p] = (6, g, p), [("N", i) for i in range(g + 1)], []
    clock, order, arrived = 0.0, [], {}
    free = dict.fromkeys("xyz", 0.0)
    while todo:
        best = None
        for name, (rank, waits, out) in todo.items():
            if all(wait in arrived for wait in waits):
                start = max([arrived[wait] for wait in waits], default=0.0)
                start = max(start, clock)
                if rank[0] > -2:
                    start = max([start] + [free[link] - BACKLOG for _, link, _ in out])
                if best is None or (start, rank, name) < best:
                    best = (start, rank, name)
        start, _, name = best
        out = todo.pop(name)[2]
        clock = start + COST.get(name[0], 0.02)
        arrived[name] = clock
        for message, link, length in out:
            free[link] = max(free[link], clock) + length
            arrived[message] = free[link] + HOP
            if link == "z":
                far = message[2] if message[1] < DIRECT else low(message[2])
                arrived[message] += FAR if far > 1 else 0.0
        order.append(name)
    return order


def kernel(
    nz, n_ref, im_hbm, ref_hbm, prior_hbm, newref, contrast_ref, loglik_ref,
    im, refs, norms, cross, w, snd1, rcv1, acc, snd2, rcv2, snd3, rcv3, own,
    stat_snd, stat_rcv, vecs, keep, prior_sem,
    stat_ssem, stat_rsem, im_sem, ref_sem, ssem, rsem,
):
    n, width = im.shape
    rows = refs.shape[0]
    groups = own.shape[0]
    rg = own.shape[2]
    gr = nz * rg
    qr = groups * gr
    half = width // 2
    me = lax.axis_index("img")
    rme = lax.axis_index("ref")
    x, y, z = lax.rem(me, 2), lax.rem(me // 2, 2), me // 4
    def chip(dx, dy, dz):
        zz, bit = z, 1
        while bit < nz:
            if dz & bit:
                zz = zz + bit - 2 * bit * lax.rem(z // bit, 2)
            bit *= 2
        return zz * 4 + lax.rem(y + dy, 2) * 2 + lax.rem(x + dx, 2)

    def send(src, dst, dev, kind, slot):
        pltpu.make_async_remote_copy(
            src_ref=src, dst_ref=dst, send_sem=ssem.at[kind], recv_sem=rsem.at[slot],
            device_id=dev, device_id_type=MESH,
        ).start()

    x_dev = {"img": chip(1, 0, 0)}
    y_dev = {"img": chip(0, 1, 0)}
    z_dev = [{"img": chip(0, 0, k)} for k in range(nz)]
    r_dev = [{"ref": lax.rem(rme + k, n_ref)} for k in range(n_ref)]

    barrier = pltpu.get_barrier_semaphore()
    peers = r_dev[1:] + [x_dev, y_dev] + z_dev[1:]
    for dev in peers:
        pl.semaphore_signal(barrier, inc=1, device_id=dev, device_id_type=MESH)

    ref_copies = []
    per_ref = rows // ref_sem.shape[0]
    for s in range(ref_sem.shape[0]):
        part = pl.ds(s * per_ref, per_ref)
        copy = pltpu.make_async_copy(ref_hbm.at[part], refs.at[part], ref_sem.at[s])
        copy.start()
        ref_copies.append(copy)
    def load_images(b):
        part = pl.ds(pl.multiple_of(b * LANES, LANES), LANES)
        return pltpu.make_async_copy(im_hbm.at[part], im.at[part], im_sem.at[b])

    ahead = min(AHEAD, n // LANES)
    for b in range(ahead):
        load_images(b).start()
    prior_copy = pltpu.make_async_copy(prior_hbm, vecs.at[3:4, :], prior_sem)
    prior_copy.start()

    stat_snd[...] = jnp.zeros_like(stat_snd)

    def square_sums(source, r0, count, scale):
        block = source[pl.ds(r0, count), :].astype(F32)
        total = jnp.sum(block * block, axis=1, keepdims=True) * scale
        norms[pl.ds(r0, count), :] = jnp.broadcast_to(total, (count, 128))

    for copy in ref_copies:
        copy.wait()
    for b in range(ahead, n // LANES):
        load_images(b).start()
    per_block = rows // (n // LANES)

    nt = (((1,), (1,)), ((), ()))
    nn = (((1,), (0,)), ((), ()))

    def fold(x):
        return x.reshape(x.shape[0] // 8, 8, 128)

    def spread8(x):
        return jnp.broadcast_to(x, (8, 128))

    at_chip = {
        (dx, dy, dz): chip(dx, dy, dz) * rg for dx, dy in QUADS for dz in range(nz)
    }

    def row0(g, where):
        return pl.multiple_of(g * (4 * gr) + at_chip[where], 8)

    def lanes(c0, width_=128):
        return pl.ds(pl.multiple_of(c0, 128), width_)

    def coefficients(c0, width_):
        a = vecs[0:1, lanes(c0, width_)]
        slope = (sharpness * LOG2E) * a
        bend = (0.5 * sharpness * LOG2E) * (a * a)
        tiles = range(0, width_, 128)
        return (
            [spread8(slope[:, t : t + 128]) for t in tiles],
            [spread8(bend[:, t : t + 128]) for t in tiles],
        )

    def over_rows(count, body, init):
        return lax.fori_loop(
            0, count // ROWS, lambda i, c: body(pl.multiple_of(i * ROWS, ROWS), c), init
        )

    def scores(c0):
        slope, bend = coefficients(c0, BLOCK)

        def body(r, high):
            part = pl.ds(r, ROWS)
            nrm = fold(norms[part, :])
            out = []
            for t in range(TILES):
                c = fold(cross[part, lanes(c0 + t * 128)])
                sc = slope[t][None] * c - bend[t][None] * nrm
                keep[part, t * 128 : (t + 1) * 128] = sc.reshape(ROWS, 128)
                out.append(jnp.maximum(high[t], jnp.max(sc, axis=0)))
            return tuple(out)

        high = over_rows(rows, body, (jnp.full((8, 128), -jnp.inf, F32),) * TILES)
        return [jnp.max(x, axis=0, keepdims=True) for x in high]

    def sums_of(c0, high, full):
        top = [spread8(x) for x in high]

        def body(r, carry):
            part = pl.ds(r, ROWS)
            nrm = fold(norms[part, :]) if full else None
            out = list(carry)
            for t in range(TILES):
                sc = fold(keep[part, t * 128 : (t + 1) * 128])
                e = jnp.exp2(sc - top[t][None])
                out[t] = out[t] + jnp.sum(e, axis=0)
                if full:
                    c = fold(cross[part, lanes(c0 + t * 128)])
                    out[TILES + t] = out[TILES + t] + jnp.sum(e * c, axis=0)
                    out[2 * TILES + t] = out[2 * TILES + t] + jnp.sum(e * nrm, axis=0)
            return tuple(out)

        zero = jnp.zeros((8, 128), F32)
        carry = over_rows(rows, body, (zero,) * (TILES * (3 if full else 1)))
        return [jnp.sum(x, axis=0, keepdims=True) for x in carry]

    def weigh(c0):
        slope, bend = coefficients(c0, BLOCK)
        top = [spread8(vecs[1:2, lanes(c0 + t * 128)]) for t in range(TILES)]
        gain = [spread8(vecs[2:3, lanes(c0 + t * 128)]) for t in range(TILES)]

        def body(g, carry):
            for q in range(4):
                parts = [pl.ds(row0(g, QUADS[q] + (dz,)), rg) for dz in range(nz)]
                nrm = [norms[part, :].reshape(rg // 8, 8, 128) for part in parts]
                to = pl.ds(pl.multiple_of(q * qr + g * gr, 8), gr)
                for t in range(TILES):
                    at = lanes(c0 + t * 128)
                    e = []
                    for part, norm in zip(parts, nrm):
                        c = cross[part, at].reshape(rg // 8, 8, 128)
                        sc = slope[t][None] * c - bend[t][None] * norm
                        e.append((jnp.exp2(sc - top[t][None]) * gain[t][None]).reshape(rg, 128))
                    w[to, at] = jnp.concatenate(e, axis=0).astype(BF16)
            return carry

        for g in range(groups):
            body(g, 0)

    blocks = n // BLOCK

    def stat_copy(it, h, k):
        slot = (it * blocks + h) * (n_ref - 1) + k - 1
        return pltpu.make_async_remote_copy(
            src_ref=stat_snd.at[it, h], dst_ref=stat_rcv.at[slot],
            send_sem=stat_ssem.at[k - 1],
            recv_sem=stat_rsem.at[(lax.rem(it, 2) * blocks + h) * (n_ref - 1) + k - 1],
            device_id=r_dev[k], device_id_type=MESH,
        )

    def local_stats(it, h, full, first=False):
        c0 = h * BLOCK
        high = scores(c0)
        sums = sums_of(c0, high, full)
        for t in range(TILES):
            at = slice(t * 128, (t + 1) * 128)
            stat_snd[it, h, 0:1, at] = high[t]
            for j in range(len(sums) // TILES):
                stat_snd[it, h, j + 1 : j + 2, at] = sums[j * TILES + t]
        if first:

            @pl.when(h == 0)
            def _():
                pl.semaphore_wait(barrier, len(peers))

        for k in range(1, n_ref):
            stat_copy(it, h, k).start()

    def joint_stats(it, h, full):
        shares = [stat_snd[it, h]]
        for k in range(1, n_ref):
            stat_copy(it, h, k).wait_recv()
            shares.append(stat_rcv[(it * blocks + h) * (n_ref - 1) + k - 1])
        high = functools.reduce(jnp.maximum, [share[0:1] for share in shares])
        scales = [jnp.exp2(share[0:1] - high) for share in shares]
        sums = [
            functools.reduce(
                jnp.add, [share[j : j + 1] * sc for share, sc in zip(shares, scales)]
            )
            for j in ((1, 2, 3) if full else (1,))
        ]
        return high, sums

    def each(count, body):
        def step(i, carry):
            body(i)
            return carry

        lax.fori_loop(0, count, step, 0)


    prior_copy.wait()
    vecs[0:1, :] = vecs[3:4, :]

    def first_cross(b):
        part = pl.ds(pl.multiple_of(b * LANES, LANES), LANES)
        load_images(b).wait()
        for r in range(0, per_block, 32):
            square_sums(refs, pl.multiple_of(b * per_block + r, 32), 32, 1.0)
        cross[:, part] = lax.dot_general(
            refs[...], im[part, :], nt, preferred_element_type=F32
        )

    def refit(i):
        it, h = i // blocks, lax.rem(i, blocks)
        at = lanes(h * BLOCK, BLOCK)
        _, (total, along, weight) = joint_stats(it, h, True)
        vecs[0:1, at] = (along / total + prior_weight * vecs[3:4, at]) / (
            weight / total + prior_weight
        )
        local_stats(it + 1, h, True)

    def settle(h):
        at = lanes(h * BLOCK, BLOCK)
        high, (total,) = joint_stats(ITERS, h, False)
        vecs[1:2, at] = high
        vecs[2:3, at] = vecs[0:1, at] / total
        weigh(h * BLOCK)

    each(n // LANES, first_cross)
    each(blocks, lambda h: local_stats(0, h, True, True))
    each(ITERS * blocks, refit)
    for h in range(blocks):
        settle(h)
    contrast_ref[...] = vecs[0:1, :]

    def weighted(r0s, c0, store):
        def body(b, carry):
            col = pl.multiple_of(b * LANES, LANES)
            lhs = [w[r0 : r0 + cnt, :] for r0, cnt in r0s]
            lhs = lhs[0] if len(lhs) == 1 else jnp.concatenate(lhs, axis=0)
            rhs = im[:, pl.ds(pl.multiple_of(c0 + col, LANES), LANES)]
            out = lax.dot_general(lhs, rhs, nn, preferred_element_type=F32)
            store(pl.ds(col, LANES), out[:qr], out[qr:])
            return carry

        for b in range(half // LANES):
            body(b, 0)

    def to_send(stream, first_is_far):
        def store(cols, lo, hi):
            far, near = (lo, hi) if first_is_far else (hi, lo)
            snd1[stream * 2, :, cols] = far.astype(BF16)
            snd1[stream * 2 + 1, :, cols] = near.astype(BF16)

        return store

    def to_keep(stream):
        def store(cols, lo, hi):
            acc[stream * 2, :, cols] = lo
            acc[stream * 2 + 1, :, cols] = hi

        return store

    hop_dev = (x_dev, y_dev)
    landed = set()
    kinds = {"s1": 0, "s2": 1, "z": 2, "az": 3, "y": 4, "x": 4, "fx": 5, "fy": 5}
    per_group = 3 * nz + 2
    bits = [1 << j for j in range(nz.bit_length() - 1)]

    def slot_of(name):
        kind, g = name[:2]
        if kind == "s1" and name[3] == 0:
            at = name[2]
        elif kind in ("s1", "s2"):
            at = 2
        elif kind == "z":
            at = 2 + name[2]
        elif kind == "az":
            at = 1 + nz + name[2]
        elif kind in ("x", "y") and name[3] == (kind == "x"):
            at = 1 + 2 * nz + name[2]
        else:
            at = 1 + 3 * nz
        return g * per_group + at

    def put(name, src, dst, dev):
        send(src, dst, dev, kinds[name[0]], slot_of(name))

    def arrive(name, like):
        slot = slot_of(name)
        if slot not in landed:
            landed.add(slot)
            pltpu.make_async_copy(like, like, rsem.at[slot]).wait()

    def send1(g, s, j):
        part = pl.ds(g * gr, gr)
        put(("s1", g, s, j), snd1.at[s * 2 + j, part], rcv1.at[s * 2 + j, part], hop_dev[s])

    def send2(g, s):
        part = pl.ds(g * gr, gr)
        arrive(("s1", g, s, 0), rcv1.at[s * 2, part])
        snd2[s, part, :] = (acc[s * 2, part, :] + rcv1[s * 2, part, :].astype(F32)).astype(BF16)
        put(("s2", g, s), snd2.at[s, part], rcv2.at[s, part], hop_dev[1 - s])

    def send3(g, bit):
        part = pl.ds(g * gr, gr)
        if bit < 2:
            arrive(("s2", g, 0), rcv1.at[:, part])
            for s in (0, 1):
                total = (
                    acc[s * 2 + 1, part, :]
                    + rcv1[s * 2 + 1, part, :].astype(F32)
                    + rcv2[s, part, :].astype(F32)
                )
                cols = slice(s * half, (s + 1) * half)
                for k in range(nz):
                    block = total[k * rg : (k + 1) * rg]
                    if k and (bit == 0 or low(k) == 1):
                        snd3[g, k - 1, :, cols] = block.astype(BF16)
                    else:
                        own[g, k, :, cols] = block
        for k in range(nz - 1, 0, -1):
            if bit and low(k) != bit:
                continue
            if bit > 1:
                total = own[g, k]
                for c in bits:
                    if c < bit:
                        arrive(("z", g, k + c), rcv3.at[g, 0])
                        total = total + rcv3[g, k + c - 1].astype(F32)
                snd3[g, k - 1] = total.astype(BF16)
            put(("z", g, k), snd3.at[g, k - 1], rcv3.at[g, k - 1], z_dev[bit or k])

    def finish(g):
        total = own[g, 0]
        for k in range(1, nz) if g < DIRECT else bits:
            arrive(("z", g, k), rcv3.at[g, 0])
            total = total + rcv3[g, k - 1].astype(F32)
        square = jnp.sum(total * total, axis=1, keepdims=True)
        mine = pl.ds(row0(g, (0, 0, 0)), rg)
        newref[mine, :] = (total * lax.rsqrt(square / width + epsilon)).astype(BF16)
        for k in range(1, nz) if g < DIRECT else bits[::-1]:
            put(("az", g, k), newref.at[mine], newref.at[mine], z_dev[k])

    def relay(g, k):
        part = newref.at[pl.ds(row0(g, (0, 0, k)), rg)]
        arrive(("az", g, k), part)
        for bit in bits[::-1]:
            if bit < low(k):
                put(("az", g, k + bit), part, part, z_dev[bit])

    def piece(g, where, side):
        return newref.at[pl.ds(row0(g, where), rg), pl.ds(side * half, half)]

    def pass_on(name, g, where, side, dev):
        part = piece(g, where, side)
        put(name, part, part, dev)

    def spread_first(g, k):
        if k:
            arrive(("az", g, k), newref.at[pl.ds(row0(g, (0, 0, k)), rg)])
        pass_on(("y", g, k, 0), g, (0, 0, k), 0, y_dev)
        pass_on(("x", g, k, 1), g, (0, 0, k), 1, x_dev)

    def spread_second(g, k):
        if k:
            arrive(("az", g, k), newref.at[pl.ds(row0(g, (0, 0, k)), rg)])
        pass_on(("y", g, k, 1), g, (0, 0, k), 1, y_dev)
        pass_on(("x", g, k, 0), g, (0, 0, k), 0, x_dev)

    def forward(g, k):
        arrive(("y", g, k, 0), newref.at[pl.ds(row0(g, (0, 1, k)), rg)])
        pass_on(("fx", g, k), g, (0, 1, k), 0, x_dev)
        pass_on(("fy", g, k), g, (1, 0, k), 1, y_dev)

    def new_norms(g):
        arrive(("fx", g, 0), newref.at[pl.ds(g * 4 * gr, 2 * gr)])

        step = math.gcd(4 * gr, 128)

        def squares(i):
            square_sums(newref, pl.multiple_of(g * 4 * gr + i * step, 8), step, 1.0 / width)

        each(4 * gr // step, squares)

    pair = PAIR if groups % PAIR == 0 else 1
    per_slot = BLOCK // LANES

    def likelihoods(c, h):
        r0, count = c * pair * 4 * gr, pair * 4 * gr
        chunks = [slice(r, min(r + ROWS, count)) for r in range(0, count, ROWS)]

        def body(i):
            c0 = h * BLOCK + i * LANES
            part = pl.ds(pl.multiple_of(c0, LANES), LANES)
            out = lax.dot_general(
                newref[r0 : r0 + count, :], im[part, :], nt, preferred_element_type=F32
            )
            slope, bend = coefficients(c0, LANES)
            slope = [x * width ** (-0.5) for x in slope]
            to = pl.ds(pl.multiple_of(i * LANES, 128), LANES)
            highs, totals = [], []
            for t in range(LANES // 128):
                sc = []
                for rr in chunks:
                    nrm = fold(norms[r0 + rr.start : r0 + rr.stop, :])
                    sc.append(
                        slope[t][None] * fold(out[rr, t * 128 : (t + 1) * 128])
                        - bend[t][None] * nrm
                    )
                high = functools.reduce(jnp.maximum, [jnp.max(x, axis=0) for x in sc])
                high = jnp.max(high, axis=0, keepdims=True)
                total = functools.reduce(
                    jnp.add, [jnp.sum(jnp.exp2(x - spread8(high)[None]), axis=0) for x in sc]
                )
                highs.append(high)
                totals.append(jnp.sum(total, axis=0, keepdims=True))
            high = jnp.concatenate(highs, axis=1)
            total = jnp.concatenate(totals, axis=1)
            if c > 0:
                before, sum_before = stat_snd[ITERS + 1, h, 0:1, to], stat_snd[ITERS + 1, h, 1:2, to]
                top = jnp.maximum(before, high)
                total = sum_before * jnp.exp2(before - top) + total * jnp.exp2(high - top)
                high = top
            stat_snd[ITERS + 1, h, 0:1, to] = high
            stat_snd[ITERS + 1, h, 1:2, to] = total

        for i in range(per_slot):
            body(i)
        if c == groups // pair - 1:
            for k in range(1, n_ref):
                stat_copy(ITERS + 1, h, k).start()

    steps = {
        "S1": send1, "S2": send2, "Z": send3, "A": finish, "T": relay, "P": spread_first,
        "Q": spread_second, "F": forward, "N": new_norms, "G": likelihoods,
    }
    order = plan(groups, nz, rg * width, blocks, pair)
    sums = (
        functools.partial(weighted, [(0, 2 * qr)], 0, to_send(0, False)),
        functools.partial(weighted, [(qr, 2 * qr)], half, to_send(1, True)),
        functools.partial(weighted, [(2 * qr, 2 * qr)], 0, to_keep(0)),
        functools.partial(weighted, [(0, qr), (3 * qr, qr)], half, to_keep(1)),
    )
    steps["W"] = lambda part: sums[part]()
    rest = order
    for name in rest:
        steps[name[0]](*name[1:])

    def final_likelihood(h):
        high, (total,) = joint_stats(ITERS + 1, h, False)
        loglik_ref[:, lanes(h * BLOCK, BLOCK)] = (
            high * math.log(2.0) + jnp.log(total) - math.log(rows * n_ref)
        )

    each(blocks, final_likelihood)
    def all_sent(like, sem):
        pltpu.make_async_copy(like, like, sem).wait()

    for k in range(1, n_ref):
        all_sent(stat_snd, stat_ssem.at[k - 1])
    for kind, like in enumerate((snd1, snd2, snd3, snd3)):
        all_sent(like, ssem.at[kind])
    all_sent(newref.at[pl.ds(0, 2 * qr)], ssem.at[4])
    all_sent(newref.at[pl.ds(0, qr)], ssem.at[5])


def put_out(new_vmem, contrast_vmem, loglik_vmem, new_hbm, contrast_hbm, loglik_hbm, sem):
    pairs = ((new_vmem, new_hbm), (contrast_vmem, contrast_hbm), (loglik_vmem, loglik_hbm))
    copies = [pltpu.make_async_copy(a, b, sem.at[i]) for i, (a, b) in enumerate(pairs)]
    for copy in copies:
        copy.start()
    for copy in copies:
        copy.wait()


def per_device(nz, n_ref, images, references, initial_contrast):
    n, width = images.shape
    rows = references.shape[0]
    groups = max(1, min(4, rows // (32 * nz)))
    rg = rows // (4 * nz * groups)
    qr, half = nz * rg * groups, width // 2
    steps = ITERS + 2
    peers = max(n_ref - 1, 1)
    stat_copies = steps * (n // BLOCK) * peers
    arrivals = groups * (3 * nz + 2)
    flops = 6 * n * width * rows
    new_references, contrast, loglik = pl.pallas_call(
        functools.partial(kernel, nz, n_ref),
        out_shape=(
            pltpu.VMEM((rows, width), BF16),
            pltpu.VMEM((1, n), F32),
            pltpu.VMEM((1, n), F32),
        ),
        in_specs=[
            pl.BlockSpec(memory_space=pl.ANY),
            pl.BlockSpec(memory_space=pl.ANY),
            pl.BlockSpec(memory_space=pl.ANY),
        ],
        out_specs=(
            pl.BlockSpec(memory_space=pltpu.VMEM),
            pl.BlockSpec(memory_space=pltpu.VMEM),
            pl.BlockSpec(memory_space=pltpu.VMEM),
        ),
        scratch_shapes=[
            pltpu.VMEM((n, width), BF16),
            pltpu.VMEM((rows, width), BF16),
            pltpu.VMEM((rows, 128), F32),
            pltpu.VMEM((rows, n), F32),
            pltpu.VMEM((rows, n), BF16),
            pltpu.VMEM((4, qr, half), BF16),
            pltpu.VMEM((4, qr, half), BF16),
            pltpu.VMEM((4, qr, half), F32),
            pltpu.VMEM((2, qr, half), BF16),
            pltpu.VMEM((2, qr, half), BF16),
            pltpu.VMEM((groups, max(nz - 1, 1), rg, width), BF16),
            pltpu.VMEM((groups, max(nz - 1, 1), rg, width), BF16),
            pltpu.VMEM((groups, nz, rg, width), F32),
            pltpu.VMEM((steps, n // BLOCK, 4, BLOCK), F32),
            pltpu.VMEM((stat_copies, 4, BLOCK), F32),
            pltpu.VMEM((8, n), F32),
            pltpu.VMEM((rows, BLOCK), F32),
            pltpu.SemaphoreType.DMA(()),
            pltpu.SemaphoreType.DMA((peers,)),
            pltpu.SemaphoreType.DMA((2 * (n // BLOCK) * peers,)),
            pltpu.SemaphoreType.DMA((n // LANES,)),
            pltpu.SemaphoreType.DMA((4,)),
            pltpu.SemaphoreType.DMA((6,)),
            pltpu.SemaphoreType.DMA((arrivals,)),
        ],
        compiler_params=pltpu.CompilerParams(
            collective_id=0, has_side_effects=True, vmem_limit_bytes=56 * 1024 * 1024
        ),
        cost_estimate=pl.CostEstimate(
            flops=flops, bytes_accessed=2 * n * width, transcendentals=0
        ),
    )(images, references, initial_contrast[None, :])
    anywhere = pl.BlockSpec(memory_space=pl.ANY)
    new_references, contrast, loglik = pl.pallas_call(
        put_out,
        out_shape=(
            jax.ShapeDtypeStruct((rows, width), BF16),
            jax.ShapeDtypeStruct((1, n), F32),
            jax.ShapeDtypeStruct((1, n), F32),
        ),
        in_specs=[pl.BlockSpec(memory_space=pltpu.VMEM)] * 3,
        out_specs=(anywhere,) * 3,
        scratch_shapes=[pltpu.SemaphoreType.DMA((3,))],
    )(*(pltpu.with_memory_space_constraint(v, pltpu.VMEM) for v in (new_references, contrast, loglik)))
    return (new_references, contrast[0], loglik[0])


def solution(mesh):
    n_img, n_ref = mesh.shape["img"], mesh.shape["ref"]
    placed = (P("img", None), P("ref", None), P("img"))
    return jax.shard_map(
        functools.partial(per_device, n_img // 4, n_ref),
        mesh=mesh,
        in_specs=placed,
        out_specs=(P("ref", None), P("img"), P("img")),
        check_vma=False,
    )
```
